1024 devices in a mesh: ctx: 64 (over x, z_lo), dp: 16 (over y, z_hi, core).
Axes of the slice: x: 4, y: 4, z: 32 (z_hi: 2, z_lo: 16; z = z_hi * 16 + z_lo), core: 2. Of those that a mesh axis runs over, the one named last changes fastest.
Arguments:
- xbc_raw: bfloat16 [16, 16384, 512], P('dp', 'ctx'), may hold values from -6 to 6
- conv_weight: float32 [4, 512], replicated, may hold values from -3 to 3
- conv_bias: float32 [512], replicated, may hold values from -3 to 3
- dt_raw: float32 [16, 16384, 4], P('dp', 'ctx'), may hold values from -1 to 10
- dt_bias: float32 [4], replicated, may hold values from -7.3 to -0.15
- a_log: float32 [4], replicated, may hold values from -3.5 to -2.5
- d_skip: float32 [4], replicated, may hold values from 0.5 to 1.5
- grad_out: bfloat16 [16, 16384, 256], P('dp', 'ctx'), may hold values from -6 to 6
Outputs:
- grad_xbc: bfloat16 [16, 16384, 512], P('dp', 'ctx')
- grad_dt: float32 [16, 16384, 4], P('dp', 'ctx')
- grad_conv_weight: float32 [4, 512], replicated
- grad_conv_bias: float32 [512], replicated
- grad_dt_bias: float32 [4], replicated
- grad_a_log: float32 [4], replicated
- grad_d_skip: float32 [4], replicated
The draws below stay inside these ranges and needn't reach their ends.
All inputs are finite; a program needn't handle non-finite values.
Results may differ from the reference program's by a relative error of at most 0.0025.
The reference program's roundings to bfloat16 on the way count: a program that leaves them out, or rounds other values in their place, can miss the bound.
Values may be sent and summed in bfloat16 or wider, within the bound.
A program may use at most 32 MiB of HBM per device.

```python
import jax
import jax.numpy as jnp
from jax import lax

H = 4
P_SIZE = 64
N = 128
K = 4
L = 256
CH = 512
CONTEXT_TOKENS = 16384
CONTEXT_COUNT = 16
N_CTX = 64


def draw_dt_raw(key, part):
    key_noise, key_position = jax.random.split(key)
    random_noise = jax.random.uniform(key_noise, (CONTEXT_COUNT, CONTEXT_TOKENS, H), jnp.float32, -0.7, 0.7)
    spike_position = jax.random.randint(key_position, (CONTEXT_COUNT, 3), 0, CONTEXT_TOKENS)
    token_positions = jnp.arange(CONTEXT_TOKENS)[None, :, None]
    spike_mask = jnp.any(token_positions == spike_position[:, None, :], axis=2).astype(jnp.float32)
    return random_noise + spike_mask[:, :, None] * 8.8


def draw_dt_bias(key, part):
    key_kind, key_level = jax.random.split(key)
    head_draw = jax.random.randint(key_kind, (H,), 0, 10)
    slow_heads = head_draw < 5
    level = jax.random.uniform(key_level, (H,), jnp.float32, -0.3, 0.3)
    return jnp.where(slow_heads, -7.0 + level, -0.45 + level)


def block_scale(stream_key, shape, cuts, low, top_value):
    level, own = 1.0, jax.random.fold_in(stream_key, 6)
    for axis_at, shards_of in cuts:
        draws = jnp.exp(jax.random.uniform(jax.random.fold_in(own, axis_at), (shards_of,), jnp.float32, low / len(cuts), top_value / len(cuts)))
        level = level * jnp.repeat(draws, shape[axis_at] // shards_of).reshape([-1 if axis == axis_at else 1 for axis in range(len(shape))])
    return level


def normal_values(own_key, shape, scale, reach, cuts=(), held_as=jnp.bfloat16):
    loudness = block_scale(own_key, shape, cuts, -0.22, 0.18) if cuts else 1.0
    entries = jax.random.normal(own_key, shape, jnp.float32) * scale * loudness
    return jnp.minimum(jnp.maximum(entries, -reach), reach).astype(held_as)


def setup_inputs(seed: int = 0) -> dict:
    streams_of = jax.random.split(jax.random.key(seed), 9)
    xbc_raw = normal_values(streams_of[0], (CONTEXT_COUNT, CONTEXT_TOKENS, CH), 1.0, 6.0, ((0, 16), (1, 64)))
    conv_weight = normal_values(streams_of[1], (K, CH), K ** -0.5, 3.0, (), jnp.float32)
    conv_bias = normal_values(streams_of[2], (CH,), 0.5, 3.0, (), jnp.float32)
    dt_raw = draw_dt_raw(jax.random.fold_in(streams_of[8], 71), 0)
    dt_bias = draw_dt_bias(jax.random.fold_in(streams_of[8], 71), 0)
    a_log = jnp.clip(jax.random.uniform(streams_of[5], (H,), jnp.float32, -3.5, -2.5), -3.5, -2.5)
    d_skip = jnp.clip(jax.random.uniform(streams_of[6], (H,), jnp.float32, 0.5, 1.5), 0.5, 1.5)
    grad_out = normal_values(streams_of[7], (CONTEXT_COUNT, CONTEXT_TOKENS, H * P_SIZE), 1.0, 6.0, ((0, 16), (1, 64)))
    return dict(xbc_raw=xbc_raw, conv_weight=conv_weight, conv_bias=conv_bias, dt_raw=dt_raw, dt_bias=dt_bias, a_log=a_log, d_skip=d_skip, grad_out=grad_out)


highest = lax.Precision.HIGHEST

def seq_forward(raw_rows, conv_weight, conv_bias, dt_seq, dt_bias, a_log, d_skip):
    length = raw_rows.shape[0]
    padded = jnp.pad(raw_rows.astype(jnp.float32), ((K - 1, 0), (0, 0)))
    pre_conv = conv_bias + sum((conv_weight[tap_idx] * padded[tap_idx:tap_idx + length] for tap_idx in range(K)))
    xbc_low = lax.optimization_barrier(jax.nn.silu(pre_conv).astype(jnp.bfloat16))
    xbc = xbc_low.astype(jnp.float32)
    inner_width = H * P_SIZE
    values = xbc[:, :inner_width].reshape(N_CTX, L, H, P_SIZE)
    b_proj = xbc[:, inner_width:inner_width + N].reshape(N_CTX, L, N)
    c_proj = xbc[:, inner_width + N:].reshape(N_CTX, L, N)
    step_size = jax.nn.softplus(dt_seq + dt_bias).reshape(N_CTX, L, H)
    decay_rate = -jnp.exp(a_log)
    causal = jnp.tril(jnp.ones((L, L), dtype=jnp.bool_))

    def block_step(carried, pieces):
        block_vals, block_b, block_c, block_size = pieces
        cum_log = jnp.cumsum(block_size * decay_rate, axis=0)
        cum_log_t = cum_log.T
        log_gaps = cum_log_t[:, :, None] - cum_log_t[:, None, :]
        within = jnp.where(causal, jnp.exp(jnp.where(causal, log_gaps, 0.0)), 0.0)
        gram_mat = jnp.dot(block_c, block_b.T, precision=highest)
        mixing = gram_mat[None] * within * block_size.T[:, None, :]
        local_out = jnp.einsum('hts,shp->thp', mixing, block_vals, precision=highest)
        state_out = jnp.einsum('tn,hpn->thp', block_c, carried, precision=highest)
        output = local_out + jnp.exp(cum_log)[:, :, None] * state_out + d_skip[:, None] * block_vals
        tail_w = jnp.exp(cum_log[-1:] - cum_log) * block_size
        new_state = jnp.exp(cum_log[-1])[:, None, None] * carried + jnp.einsum('shp,sn->hpn', block_vals * tail_w[:, :, None], block_b, precision=highest)
        return (new_state, output.reshape(L, H * P_SIZE))
    start_state = jnp.zeros((H, P_SIZE, N), jnp.float32)
    _, outputs = lax.scan(jax.checkpoint(block_step), start_state, (values, b_proj, c_proj, step_size))
    return outputs.reshape(length, H * P_SIZE)

def reference(xbc_raw, conv_weight, conv_bias, dt_raw, dt_bias, a_log, d_skip, grad_out):
    zeros_init = (jnp.zeros_like(conv_weight), jnp.zeros_like(conv_bias), jnp.zeros_like(dt_bias), jnp.zeros_like(a_log), jnp.zeros_like(d_skip))

    def per_context(totals, inputs):
        raw_rows, dt_seq, cotangent = inputs
        _, pullback = jax.vjp(seq_forward, raw_rows, conv_weight, conv_bias, dt_seq, dt_bias, a_log, d_skip)
        gradients = pullback(cotangent.astype(jnp.float32))
        totals = (totals[0] + gradients[1], totals[1] + gradients[2], totals[2] + gradients[4], totals[3] + gradients[5], totals[4] + gradients[6])
        return (totals, (gradients[0], gradients[3]))
    totals, outs_pair = lax.scan(per_context, zeros_init, (xbc_raw, dt_raw, grad_out))
    return (outs_pair[0], outs_pair[1], totals[0], totals[1], totals[2], totals[3], totals[4])
```

```python
import functools

import jax
import jax.numpy as jnp
from jax import lax
from jax.experimental import pallas as pl
from jax.experimental.pallas import tpu as pltpu
from jax.sharding import PartitionSpec as P

H = 4
P_SIZE = 64
N = 128
K = 4
L = 256
CH = 512
INNER = H * P_SIZE
NZ = 16
NX = 4
NC = 4
RC = N // NC
F32 = jnp.float32
BF16 = jnp.bfloat16
MESH = pl.DeviceIdType.MESH


def dot(a, b):
    return lax.dot_general(a, b, (((1,), (0,)), ((), ())), preferred_element_type=F32)


def dot_nt(a, b):
    return lax.dot_general(a, b, (((1,), (1,)), ((), ())), preferred_element_type=F32)


def dot_tn(a, b):
    return lax.dot_general(a, b, (((0,), (0,)), ((), ())), preferred_element_type=F32)


def split(a):
    hi = a.astype(BF16)
    return hi, (a - hi.astype(F32)).astype(BF16)


def split3(a):
    hi = a.astype(BF16)
    rest = a - hi.astype(F32)
    mid = rest.astype(BF16)
    return hi, mid, (rest - mid.astype(F32)).astype(BF16)


def iota(shape, dim):
    return lax.broadcasted_iota(jnp.int32, shape, dim)


def head_column(ref):
    rows = iota((8, 1), 0)
    col = jnp.zeros((8, 1), F32)
    for h in range(H):
        col = jnp.where(rows == h, ref[h], col)
    return col


def spread(cols, first):
    rows = cols.shape[0]
    low = iota((rows, 128), 1) < P_SIZE
    tiles = []
    for j in range(2):
        a = jnp.broadcast_to(cols[:, first + 2 * j : first + 2 * j + 1], (rows, 128))
        b = jnp.broadcast_to(cols[:, first + 2 * j + 1 : first + 2 * j + 2], (rows, 128))
        tiles.append(jnp.where(low, a, b))
    return jnp.concatenate(tiles, axis=1)


def head_rows(dtype):
    return (iota((8, INNER), 1) // P_SIZE == iota((8, INNER), 0)).astype(dtype)


def head_sums(x):
    sel = head_rows(F32).astype(BF16)
    hi, lo = split(x)
    return dot_nt(sel, hi) + dot_nt(sel, lo)


def main_kernel(
    dt_bias_ref, a_log_ref, skip_ref, raw_ref, halo_ref, w_ref, bias_ref, dt_ref, cot_ref,
    gx_ref, tail_ref, spill_ref, gpre_ref, sums_ref,
    xp, pre_s, sig_s, xb, rows_s, cols_s, loc, dec, tw_e, up_e, st_e, ac, gbl, gcl, pair_s,
    gc_pad, rbuf, sbuf, xsend, xrecv, s_in, g_after,
    send_sem, recv_sem, xsend_sem, xrecv_sem,
):
    place = lax.axis_index("ctx")
    dp = lax.axis_index("dp")
    z = lax.rem(place, NZ)
    x = place // NZ
    barrier = pltpu.get_barrier_semaphore()

    @pl.when(z > 0)
    def _():
        pl.semaphore_signal(barrier, inc=1, device_id=(place - 1, dp), device_id_type=MESH)

    @pl.when(z < NZ - 1)
    def _():
        pl.semaphore_signal(barrier, inc=1, device_id=(place + 1, dp), device_id_type=MESH)

    for k in range(1, NX):
        pl.semaphore_signal(
            barrier, inc=1, device_id=(lax.rem(place + k * NZ, NX * NZ), dp), device_id_type=MESH
        )

    xp[0:8, :] = halo_ref[...].astype(F32)
    xp[8 : 8 + L, :] = raw_ref[...].astype(F32)
    for r in range(0, L, 64):
        pre = bias_ref[...] + sum(
            w_ref[k : k + 1, :] * xp[5 + k + r : 5 + k + r + 64, :] for k in range(K)
        )
        sig = 1.0 / (1.0 + jnp.exp(-pre))
        pre_s[r : r + 64, :] = pre
        sig_s[r : r + 64, :] = sig
        xb[r : r + 64, :] = (pre * sig).astype(BF16)

    rate = -jnp.exp(head_column(a_log_ref))
    live = iota((8, 1), 0) < H
    rate = jnp.where(live, rate, 0.0)
    rows_s[...] = jnp.zeros_like(rows_s)
    rows_s[0:H, :] = dt_ref[...]
    dt_pre = rows_s[0:8, :] + head_column(dt_bias_ref)
    step = jnp.where(
        live, jnp.maximum(dt_pre, 0.0) + jnp.log1p(jnp.exp(-jnp.abs(dt_pre))), 0.0
    )
    upto = (iota((L, L), 0) <= iota((L, L), 1)).astype(F32).astype(BF16)
    cum = sum(dot(part, upto) for part in split3(step * rate))
    cum_last = cum[:, L - 1 : L]
    to_end = jnp.exp(cum_last - cum)
    tw = to_end * step
    up = jnp.exp(cum)
    rows_s[0:8, :] = cum
    rows_s[8:16, :] = step
    rows_s[16:24, :] = tw
    rows_s[24:32, :] = up
    cols = jnp.transpose(rows_s[...])
    cols_s[...] = cols
    tw_e[...] = spread(cols, 16)
    up_e[...] = spread(cols, 24)
    st_e[...] = spread(cols, 8)
    decay_lanes = up_e[L - 1 : L, :]
    dec[...] = jnp.broadcast_to(decay_lanes, (8, INNER))

    b_val = xb[:, INNER : INNER + N]
    c_val = xb[:, INNER + N :]
    hi, lo = split(xb[:, :INNER].astype(F32) * tw_e[...])
    loc[0] = dot_tn(b_val, hi) + dot_tn(b_val, lo)
    hi, lo = split(cot_ref[...].astype(F32) * up_e[...])
    loc[1] = dot_tn(c_val, hi) + dot_tn(c_val, lo)

    @pl.when(z == 0)
    def _():
        rbuf[0, :, 0 : 2 * RC, :] = jnp.zeros((NC, 2 * RC, INNER), F32)
        rbuf[0, :, 2 * RC :, :] = jnp.ones((NC, 8, INNER), F32)

    @pl.when(z == NZ - 1)
    def _():
        rbuf[1, :, 0 : 2 * RC, :] = jnp.zeros((NC, 2 * RC, INNER), F32)
        rbuf[1, :, 2 * RC :, :] = jnp.ones((NC, 8, INNER), F32)

    pl.semaphore_wait(
        barrier, NX - 1 + (z > 0).astype(jnp.int32) + (z < NZ - 1).astype(jnp.int32)
    )

    first = (z >= NZ // 2).astype(jnp.int32)

    def hop(way, c):
        nearer = place + 1 - 2 * way
        return pltpu.make_async_remote_copy(
            src_ref=sbuf.at[way, c],
            dst_ref=rbuf.at[way, c],
            send_sem=send_sem.at[way, c],
            recv_sem=recv_sem.at[way, c],
            device_id=(nearer, dp),
            device_id_type=MESH,
        )

    def has_in(way):
        return jnp.where(way == 0, z, NZ - 1 - z) > 0

    def has_out(way):
        return jnp.where(way == 0, NZ - 1 - z, z) > 0

    def relay(way, c):
        @pl.when(has_in(way))
        def _():
            hop(way, c).wait_recv()

        @pl.when(has_out(way))
        def _():
            rows = pl.ds(pl.multiple_of(c * RC, RC), RC)
            d = dec[0:1, :]
            main = rbuf[way, c, 0:RC, :]
            aux = rbuf[way, c, RC : 2 * RC, :]
            factor = rbuf[way, c, 2 * RC :, :]
            sbuf[way, c, 0:RC, :] = d * main + loc[way, rows, :]
            sbuf[way, c, RC : 2 * RC, :] = aux + factor[0:1, :] * loc[1 - way, rows, :]
            sbuf[way, c, 2 * RC :, :] = factor * dec[...]
            hop(way, c).start()

    def cross(k, c, kind):
        other = lax.rem(x + k, NX)
        return pltpu.make_async_remote_copy(
            src_ref=xsend.at[kind, c],
            dst_ref=xrecv.at[x, c],
            send_sem=xsend_sem.at[k - 1, c],
            recv_sem=xrecv_sem.at[x, c],
            device_id=(other * NZ + z, dp),
            device_id_type=MESH,
        )

    def arrival(k, c):
        source = lax.rem(x + k, NX)
        return pltpu.make_async_remote_copy(
            src_ref=xsend.at[0, c],
            dst_ref=xrecv.at[source, c],
            send_sem=xsend_sem.at[k - 1, c],
            recv_sem=xrecv_sem.at[source, c],
            device_id=(source * NZ + z, dp),
            device_id_type=MESH,
        )

    def exchange(c):
        rows = pl.ds(pl.multiple_of(c * RC, RC), RC)
        d = dec[0:1, :]
        f = rbuf[0, c, 2 * RC :, :]
        e = rbuf[1, c, 2 * RC :, :]
        xsend[0, c, 0:RC, :] = (
            e[0:1, :] * (d * rbuf[0, c, 0:RC, :] + loc[0, rows, :]) + rbuf[1, c, RC : 2 * RC, :]
        )
        xsend[1, c, 0:RC, :] = (
            f[0:1, :] * (d * rbuf[1, c, 0:RC, :] + loc[1, rows, :]) + rbuf[0, c, RC : 2 * RC, :]
        )
        whole = f * e * dec[...]
        xsend[0, c, RC:, :] = whole
        xsend[1, c, RC:, :] = whole
        for k in range(1, NX):
            other = lax.rem(x + k, NX)
            cross(k, c, (other < x).astype(jnp.int32)).start()

    def relay_first(c, _):
        relay(first, c)
        return 0

    def relay_second(c, _):
        relay(1 - first, c)
        exchange(c)
        return 0

    early = jnp.logical_or(z < 4, z >= NZ - 4)

    @pl.when(early)
    def _():
        lax.fori_loop(0, NC, relay_first, 0)

    pair_s[...] = jnp.zeros_like(pair_s)
    low = iota((128, 128), 1) < P_SIZE
    for sb in range(2):
        t0 = 128 * sb
        wide = L - t0
        rs = slice(t0, t0 + 128)
        gram = dot_nt(xb[rs, INNER : INNER + N], xb[t0:, INNER + N :])
        mask = iota((128, wide), 1) >= iota((128, wide), 0)
        dgram = jnp.zeros((128, wide), F32)
        for j in range(2):
            cot_t = cot_ref[t0:, 128 * j : 128 * j + 128]
            v_t = xb[rs, 128 * j : 128 * j + 128]
            parts = []
            for i in range(2):
                h = 2 * j + i
                keep = low if i == 0 else jnp.logical_not(low)
                v_h = jnp.where(keep, v_t.astype(F32), 0.0).astype(BF16)
                gap = rows_s[h : h + 1, t0:] - cols_s[rs, h : h + 1]
                within = jnp.exp(jnp.where(mask, gap, -1e30))
                dmix = dot_nt(v_h, cot_t)
                hi, lo = split(gram * within)
                parts.append(dot(hi, cot_t) + dot(lo, cot_t))
                dw = dmix * within * cols_s[rs, 8 + h : 9 + h]
                dgram = dgram + dw
                pair_s[h : h + 1, t0:] += jnp.sum(dw * gram, axis=0, keepdims=True)
            ac[rs, 128 * j : 128 * j + 128] = jnp.where(low, parts[0], parts[1])
        hi, lo = split(dgram)
        c_t = xb[t0:, INNER + N :]
        b_s = xb[rs, INNER : INNER + N]
        gbl[rs, :] = dot(hi, c_t) + dot(lo, c_t)
        from_here = dot_tn(hi, b_s) + dot_tn(lo, b_s)
        if sb == 0:
            gcl[...] = from_here
        else:
            gcl[t0:, :] += from_here

    @pl.when(jnp.logical_not(early))
    def _():
        lax.fori_loop(0, NC, relay_first, 0)

    lax.fori_loop(0, NC, relay_second, 0)

    def gather(c, _):
        for k in range(1, NX):
            arrival(k, c).wait_recv()
        s_in[pl.ds(pl.multiple_of(c * RC, RC), RC), :] = jnp.zeros((RC, INNER), F32)
        g_after[pl.ds(pl.multiple_of(c * RC, RC), RC), :] = jnp.zeros((RC, INNER), F32)
        rows = pl.ds(pl.multiple_of(c * RC, RC), RC)
        for k in range(NX - 1):

            @pl.when(k < x)
            def _():
                s_in[rows, :] = xrecv[k, c, RC : RC + 1, :] * s_in[rows, :] + xrecv[k, c, 0:RC, :]

        for k in range(NX - 1, 0, -1):

            @pl.when(k > x)
            def _():
                g_after[rows, :] = (
                    xrecv[k, c, RC : RC + 1, :] * g_after[rows, :] + xrecv[k, c, 0:RC, :]
                )

        s_in[rows, :] = rbuf[0, c, 0:RC, :] + rbuf[0, c, 2 * RC : 2 * RC + 1, :] * s_in[rows, :]
        g_after[rows, :] = (
            rbuf[1, c, 0:RC, :] + rbuf[1, c, 2 * RC : 2 * RC + 1, :] * g_after[rows, :]
        )
        return 0

    lax.fori_loop(0, NC, gather, 0)

    b_val = xb[:, INNER : INNER + N]
    c_val = xb[:, INNER + N :]
    s_hi, s_lo = split(s_in[...])
    g_hi, g_lo = split(g_after[...])
    state_back = dot(b_val, g_hi) + dot(b_val, g_lo)
    state_proj = dot(c_val, s_hi) + dot(c_val, s_lo)
    cot = cot_ref[...].astype(F32)
    vals = xb[:, :INNER].astype(F32)
    scaled = cot * up_e[...]
    hi, lo = split(scaled)
    grad_c = gcl[...] + dot_nt(hi, s_hi) + dot_nt(hi, s_lo) + dot_nt(lo, s_hi)
    hi, lo = split(vals * tw_e[...])
    grad_b = gbl[...] + dot_nt(hi, g_hi) + dot_nt(hi, g_lo) + dot_nt(lo, g_hi)
    local_step = head_sums(vals * ac[...])
    tail_grad = head_sums(vals * state_back)
    proj_term = head_sums(scaled * state_proj)
    skip_lanes = spread(jnp.broadcast_to(0.0, (8, 128)) + sum(
        jnp.where(iota((8, 128), 1) == h, skip_ref[h], 0.0) for h in range(H)
    ), 0)[0:1, :]
    grad_vals = st_e[...] * ac[...] + skip_lanes * cot + tw_e[...] * state_back

    step = rows_s[8:16, :]
    tw = rows_s[16:24, :]
    cum = rows_s[0:8, :]
    cum_last = cum[:, L - 1 : L]
    sel = head_rows(F32)
    skip_sum = jnp.sum(sel * jnp.sum(cot * vals, axis=0, keepdims=True), axis=1, keepdims=True)
    both = jnp.sum(
        sel * jnp.sum(s_in[...] * g_after[...], axis=0, keepdims=True), axis=1, keepdims=True
    )
    tail_term = tail_grad * tw
    extra = jnp.sum(tail_term, axis=1, keepdims=True) + jnp.exp(cum_last) * both
    grad_cum = pair_s[...] - step * local_step + proj_term - tail_term
    since = (iota((L, L), 0) >= iota((L, L), 1)).astype(F32).astype(BF16)
    grad_log = sum(dot(part, since) for part in split3(grad_cum)) + extra
    rows_s[32 : 32 + H, :] = dt_ref[...]
    dt_pre = rows_s[32:40, :] + head_column(dt_bias_ref)
    rate = -jnp.exp(head_column(a_log_ref))
    grad_step = local_step + tail_grad * jnp.exp(cum_last - cum) + rate * grad_log
    grad_pre = grad_step / (1.0 + jnp.exp(-dt_pre))
    gpre_ref[...] = grad_pre[0:H, :]
    alog_sum = rate * jnp.sum(grad_log * step, axis=1, keepdims=True)
    bias_sum = jnp.sum(grad_pre, axis=1, keepdims=True)

    gc_pad[0:8, :] = jnp.zeros((8, CH), F32)
    gc_pad[8 + L : 16 + L, :] = jnp.zeros((8, CH), F32)
    for lanes, value in (
        (slice(0, INNER), grad_vals),
        (slice(INNER, INNER + N), grad_b),
        (slice(INNER + N, CH), grad_c),
    ):
        low_value = value.astype(BF16).astype(F32)
        sig = sig_s[:, lanes]
        gc_pad[8 : 8 + L, lanes] = low_value * sig * (1.0 + pre_s[:, lanes] * (1.0 - sig))

    spill_ref[...] = sum(w_ref[k : k + 1, :] * gc_pad[3 - k : 11 - k, :] for k in range(K))
    sums_ref[...] = jnp.zeros_like(sums_ref)
    for r in range(0, L, 64):
        rows = sum(
            w_ref[k : k + 1, :] * gc_pad[11 - k + r : 11 - k + r + 64, :] for k in range(K)
        )
        gx_ref[r : r + 64, :] = rows.astype(BF16)
        if r + 64 == L:
            tail_ref[...] = rows[56:64, :]
    for k in range(K + 1):
        term = gc_pad[8 : 8 + L, :]
        if k < K:
            term = term * xp[5 + k : 5 + k + L, :]
        total = jnp.sum(term, axis=0, keepdims=True)
        for j in range(4):
            sums_ref[4 * k + j] = total[:, 128 * j : 128 * j + 128]
    lane = iota((8, 128), 1)
    row = iota((8, 128), 0)
    small = (
        jnp.where(lane == row, bias_sum, 0.0)
        + jnp.where(lane == row + 8, alog_sum, 0.0)
        + jnp.where(lane == row + 16, skip_sum, 0.0)
    )
    small = jnp.where(row < H, small, 0.0)
    sums_ref[20] = jnp.sum(small, axis=0, keepdims=True)

    def drain(c, _):
        for way in range(2):

            @pl.when(has_out(way))
            def _():
                hop(way, c).wait_send()

        for k in range(1, NX):
            arrival(k, c).wait_send()
        return 0

    lax.fori_loop(0, NC, drain, 0)


def run_main(raw, halo, weight, bias, dt_t, dt_bias, a_log, d_skip, cot):
    vmem = pl.BlockSpec(memory_space=pltpu.VMEM)
    smem = pl.BlockSpec(memory_space=pltpu.SMEM)
    return pl.pallas_call(
        main_kernel,
        out_shape=(
            jax.ShapeDtypeStruct((L, CH), BF16),
            jax.ShapeDtypeStruct((8, CH), F32),
            jax.ShapeDtypeStruct((8, CH), F32),
            jax.ShapeDtypeStruct((H, L), F32),
            jax.ShapeDtypeStruct((32, 1, 128), F32),
        ),
        in_specs=[smem] * 3 + [vmem] * 6,
        out_specs=(vmem,) * 5,
        scratch_shapes=[
            pltpu.VMEM((8 + L, CH), F32),
            pltpu.VMEM((L, CH), F32),
            pltpu.VMEM((L, CH), F32),
            pltpu.VMEM((L, CH), BF16),
            pltpu.VMEM((128, L), F32),
            pltpu.VMEM((L, 128), F32),
            pltpu.VMEM((2, N, INNER), F32),
            pltpu.VMEM((8, INNER), F32),
            pltpu.VMEM((L, INNER), F32),
            pltpu.VMEM((L, INNER), F32),
            pltpu.VMEM((L, INNER), F32),
            pltpu.VMEM((L, INNER), F32),
            pltpu.VMEM((L, N), F32),
            pltpu.VMEM((L, N), F32),
            pltpu.VMEM((8, L), F32),
            pltpu.VMEM((16 + L, CH), F32),
            pltpu.VMEM((2, NC, 2 * RC + 8, INNER), F32),
            pltpu.VMEM((2, NC, 2 * RC + 8, INNER), F32),
            pltpu.VMEM((2, NC, RC + 8, INNER), F32),
            pltpu.VMEM((NX, NC, RC + 8, INNER), F32),
            pltpu.VMEM((N, INNER), F32),
            pltpu.VMEM((N, INNER), F32),
            pltpu.SemaphoreType.DMA((2, NC)),
            pltpu.SemaphoreType.DMA((2, NC)),
            pltpu.SemaphoreType.DMA((NX - 1, NC)),
            pltpu.SemaphoreType.DMA((NX, NC)),
        ],
        compiler_params=pltpu.CompilerParams(
            collective_id=0, has_side_effects=True, vmem_limit_bytes=48 << 20
        ),
        name="slab",
    )(dt_bias, a_log, d_skip, raw, halo, weight, bias, dt_t, cot)


NY = 4
NR = 32
ZR = 32


def reduce_kernel(in_ref, out_ref, plane, line, own, send_sem, recv_sem):
    place = lax.axis_index("ctx")
    dp = lax.axis_index("dp")
    z_lo = lax.rem(place, NZ)
    x = place // NZ
    y = dp // 4
    z_hi = lax.rem(dp // 2, 2)
    core = lax.rem(dp, 2)
    me = (x * NY + y) * 2 + core
    z = z_hi * NZ + z_lo

    def in_plane(r):
        rx = r // 8
        ry = lax.rem(r // 2, NY)
        rc = lax.rem(r, 2)
        return (rx * NZ + z_lo, ry * 4 + z_hi * 2 + rc)

    def in_line(q):
        return (x * NZ + lax.rem(q, NZ), y * 4 + (q // NZ) * 2 + core)

    barrier = pltpu.get_barrier_semaphore()

    def greet(k, _):
        pl.semaphore_signal(
            barrier, inc=1, device_id=in_plane(lax.rem(me + k, NR)), device_id_type=MESH
        )
        pl.semaphore_signal(
            barrier, inc=1, device_id=in_line(lax.rem(z + k, ZR)), device_id_type=MESH
        )
        return 0

    lax.fori_loop(1, NR, greet, 0)
    plane[pl.ds(me, 1)] = in_ref[pl.ds(me, 1)]
    pl.semaphore_wait(barrier, NR - 1 + ZR - 1)

    def send(src, dst, stage, target):
        return pltpu.make_async_remote_copy(
            src_ref=src,
            dst_ref=dst,
            send_sem=send_sem.at[stage],
            recv_sem=recv_sem.at[stage],
            device_id=target,
            device_id_type=MESH,
        )

    def all_of(buf, stage):
        return pltpu.make_async_remote_copy(
            src_ref=buf.at[pl.ds(0, NR - 1)],
            dst_ref=buf.at[pl.ds(0, NR - 1)],
            send_sem=send_sem.at[stage],
            recv_sem=recv_sem.at[stage],
            device_id=in_plane(lax.rem(me + 1, NR)),
            device_id_type=MESH,
        )

    def scatter(k, _):
        r = lax.rem(me + k, NR)
        send(in_ref.at[r], plane.at[me], 0, in_plane(r)).start()
        return 0

    lax.fori_loop(1, NR, scatter, 0)
    all_of(plane, 0).wait_recv()
    mine = jnp.sum(plane[...], axis=0, keepdims=True)
    own[0:1] = mine
    line[pl.ds(z, 1)] = mine

    def along(k, _):
        q = lax.rem(z + k, ZR)
        send(own.at[0], line.at[z], 1, in_line(q)).start()
        return 0

    lax.fori_loop(1, ZR, along, 0)
    all_of(line, 1).wait_recv()
    total = jnp.sum(line[...], axis=0, keepdims=True)
    own[1:2] = total
    out_ref[pl.ds(me, 1)] = total

    def spread_out(k, _):
        send(own.at[1], out_ref.at[me], 2, in_plane(lax.rem(me + k, NR))).start()
        return 0

    lax.fori_loop(1, NR, spread_out, 0)
    all_of(out_ref, 2).wait_recv()
    for stage, buf in enumerate((plane, line, out_ref)):
        all_of(buf, stage).wait_send()


def run_reduce(sums):
    vmem = pl.BlockSpec(memory_space=pltpu.VMEM)
    return pl.pallas_call(
        reduce_kernel,
        out_shape=jax.ShapeDtypeStruct((32, 1, 128), F32),
        in_specs=[vmem],
        out_specs=vmem,
        scratch_shapes=[
            pltpu.VMEM((NR, 1, 128), F32),
            pltpu.VMEM((ZR, 1, 128), F32),
            pltpu.VMEM((2, 1, 128), F32),
            pltpu.SemaphoreType.DMA((3,)),
            pltpu.SemaphoreType.DMA((3,)),
        ],
        compiler_params=pltpu.CompilerParams(collective_id=1, has_side_effects=True),
        name="totals",
    )(sums)


def shift(block, axis, distance):
    devices = range(lax.axis_size(axis))
    route = [(i - distance, i) for i in devices if i - distance in devices]
    return lax.ppermute(block, axis, route)


def on_device(xbc_raw, conv_weight, conv_bias, dt_raw, dt_bias, a_log, d_skip, grad_out):
    raw = xbc_raw[0]
    halo = shift(raw[L - 8 :], "ctx", 1)
    gx, tail, spill, gpre, sums = run_main(
        raw, halo, conv_weight, conv_bias[None], dt_raw[0].T, dt_bias, a_log, d_skip, grad_out[0]
    )
    back = shift(spill[5:], "ctx", -1)
    totals = run_reduce(sums)
    last = jnp.concatenate([tail[:5], tail[5:] + back], 0).astype(BF16)
    grad_input = lax.dynamic_update_slice(gx, last, (L - 8, 0))[None]
    weight_grad = totals[:16].reshape(K, CH)
    bias_grad = totals[16:20].reshape(CH)
    small = totals[20, 0]
    return (
        grad_input, gpre.T[None], weight_grad, bias_grad, small[0:4], small[8:12], small[16:20],
    )


def solution(mesh):
    rows = P("dp", "ctx", None)
    return jax.shard_map(
        on_device,
        mesh=mesh,
        in_specs=(rows, P(), P(), rows, P(), P(), P(), rows),
        out_specs=(rows, rows, P(), P(), P(), P(), P()),
        check_vma=False,
    )
```

```python
import functools

import jax
import jax.numpy as jnp
from jax import lax
from jax.experimental import pallas as pl
from jax.experimental.pallas import tpu as pltpu
from jax.sharding import PartitionSpec as P

H = 4
P_SIZE = 64
N = 128
K = 4
L = 256
CH = 512
INNER = H * P_SIZE
NZ = 16
NX = 4
NY = 4
NR = 32
ZR = 32
NC = 16
RC = N // NC
F32 = jnp.float32
BF16 = jnp.bfloat16
MESH = pl.DeviceIdType.MESH


def dot(a, b):
    return lax.dot_general(a, b, (((1,), (0,)), ((), ())), preferred_element_type=F32)


def dot_nt(a, b):
    return lax.dot_general(a, b, (((1,), (1,)), ((), ())), preferred_element_type=F32)


def dot_tn(a, b):
    return lax.dot_general(a, b, (((0,), (0,)), ((), ())), preferred_element_type=F32)


def split(a):
    hi = a.astype(BF16)
    return hi, (a - hi.astype(F32)).astype(BF16)


def split3(a):
    hi = a.astype(BF16)
    rest = a - hi.astype(F32)
    mid = rest.astype(BF16)
    return hi, mid, (rest - mid.astype(F32)).astype(BF16)


def iota(shape, dim):
    return lax.broadcasted_iota(jnp.int32, shape, dim)


def head_column(ref):
    rows = iota((8, 1), 0)
    col = jnp.zeros((8, 1), F32)
    for h in range(H):
        col = jnp.where(rows == h, ref[h], col)
    return col


def spread(cols, first):
    rows = cols.shape[0]
    low = iota((rows, 128), 1) < P_SIZE
    tiles = []
    for j in range(2):
        a = jnp.broadcast_to(cols[:, first + 2 * j : first + 2 * j + 1], (rows, 128))
        b = jnp.broadcast_to(cols[:, first + 2 * j + 1 : first + 2 * j + 2], (rows, 128))
        tiles.append(jnp.where(low, a, b))
    return jnp.concatenate(tiles, axis=1)


def head_rows(dtype):
    return (iota((8, INNER), 1) // P_SIZE == iota((8, INNER), 0)).astype(dtype)


def head_sums(x):
    sel = head_rows(F32).astype(BF16)
    hi, lo = split(x)
    return dot_nt(sel, hi) + dot_nt(sel, lo)


def main_kernel(
    dt_bias_ref, a_log_ref, skip_ref, halo_ref, raw_hbm, w_hbm, bias_hbm, dt_hbm, cot_hbm,
    gx_ref, gpre_ref, wg_ref, bg_ref, small_ref,
    raw_ref, w_ref, bias_ref, dt_ref, cot_ref, in_sem,
    xp, pre_s, sig_s, xb, rows_s, cols_s, loc, dec, tw_e, up_e, st_e, ac, gbl, gcl, pair_s,
    gc_pad, rbuf, sbuf, rfac, sfac, xsend, xrecv, xfac, xdec, s_in, g_after,
    spill_out, spill_in, sums_ref, plane, line, own, totals,
    send_sem, recv_sem, fsend_sem, frecv_sem, xsend_sem, xrecv_sem, ssend_sem, srecv_sem,
    rsend_sem, rrecv_sem, edge_sem, known_sem,
):
    place = lax.axis_index("ctx")
    dp = lax.axis_index("dp")
    z = lax.rem(place, NZ)
    x = place // NZ
    y = dp // 4
    z_hi = lax.rem(dp // 2, 2)
    core = lax.rem(dp, 2)

    def device(x_, y_, ring, core_):
        return (x_ * NZ + lax.rem(ring, NZ), y_ * 4 + (ring // NZ) * 2 + core_)

    ring = z_hi * NZ + z
    barrier = pltpu.get_barrier_semaphore()
    inputs = [
        pltpu.make_async_copy(src, dst, in_sem.at[i])
        for i, (src, dst) in enumerate(
            ((raw_hbm, raw_ref), (w_hbm, w_ref), (bias_hbm, bias_ref), (dt_hbm, dt_ref),
             (cot_hbm, cot_ref))
        )
    ]
    for copy in inputs:
        copy.start()
    for step in (1, ZR - 1):
        pl.semaphore_signal(
            barrier, inc=1, device_id=device(x, y, lax.rem(ring + step, ZR), core),
            device_id_type=MESH,
        )
    for k in range(1, NX):
        pl.semaphore_signal(
            barrier, inc=1, device_id=device(lax.rem(x + k, NX), y, ring, core),
            device_id_type=MESH,
        )
    for k in range(1, 2 * NY):
        q = lax.rem(y * 2 + core + k, 2 * NY)
        pl.semaphore_signal(
            barrier, inc=1, device_id=device(x, q // 2, ring, lax.rem(q, 2)), device_id_type=MESH
        )
    for copy in inputs:
        copy.wait()

    xp[0:8, :] = halo_ref[...].astype(F32)
    xp[8 : 8 + L, :] = raw_ref[...].astype(F32)
    for r in range(0, L, 64):
        pre = bias_ref[...] + sum(
            w_ref[k : k + 1, :] * xp[5 + k + r : 5 + k + r + 64, :] for k in range(K)
        )
        sig = 1.0 / (1.0 + jnp.exp(-pre))
        pre_s[r : r + 64, :] = pre
        sig_s[r : r + 64, :] = sig
        xb[r : r + 64, :] = (pre * sig).astype(BF16)

    rate = -jnp.exp(head_column(a_log_ref))
    live = iota((8, 1), 0) < H
    rate = jnp.where(live, rate, 0.0)
    rows_s[...] = jnp.zeros_like(rows_s)
    rows_s[0:H, :] = dt_ref[...]
    dt_pre = rows_s[0:8, :] + head_column(dt_bias_ref)
    step = jnp.where(
        live, jnp.maximum(dt_pre, 0.0) + jnp.log1p(jnp.exp(-jnp.abs(dt_pre))), 0.0
    )
    upto = (iota((L, L), 0) <= iota((L, L), 1)).astype(F32).astype(BF16)
    cum = sum(dot(part, upto) for part in split3(step * rate))
    cum_last = cum[:, L - 1 : L]
    to_end = jnp.exp(cum_last - cum)
    tw = to_end * step
    up = jnp.exp(cum)
    rows_s[0:8, :] = cum
    rows_s[8:16, :] = step
    rows_s[16:24, :] = tw
    rows_s[24:32, :] = up
    cols = jnp.transpose(rows_s[...])
    cols_s[...] = cols
    tw_e[...] = spread(cols, 16)
    up_e[...] = spread(cols, 24)
    st_e[...] = spread(cols, 8)
    decay_lanes = up_e[L - 1 : L, :]
    dec[...] = jnp.broadcast_to(decay_lanes, (8, INNER))

    b_val = xb[:, INNER : INNER + N]
    c_val = xb[:, INNER + N :]
    hi, lo = split(xb[:, :INNER].astype(F32) * tw_e[...])
    loc[0] = dot_tn(b_val, hi) + dot_tn(b_val, lo)
    hi, lo = split(cot_ref[...].astype(F32) * up_e[...])
    loc[1] = dot_tn(c_val, hi) + dot_tn(c_val, lo)

    @pl.when(z == 0)
    def _():
        rbuf[0] = jnp.zeros((NC, 2 * RC, INNER), F32)
        rfac[0] = jnp.ones((8, INNER), F32)

    @pl.when(z == NZ - 1)
    def _():
        rbuf[1] = jnp.zeros((NC, 2 * RC, INNER), F32)
        rfac[1] = jnp.ones((8, INNER), F32)

    pl.semaphore_wait(barrier, 2 + NX - 1 + 2 * NY - 1)

    first = (z >= NZ // 2).astype(jnp.int32)

    def nearer(way):
        return (place + 1 - 2 * way, dp)

    def hop(way, c):
        return pltpu.make_async_remote_copy(
            src_ref=sbuf.at[way, c],
            dst_ref=rbuf.at[way, c],
            send_sem=send_sem.at[way, c],
            recv_sem=recv_sem.at[way, c],
            device_id=nearer(way),
            device_id_type=MESH,
        )

    def factor_hop(way):
        return pltpu.make_async_remote_copy(
            src_ref=sfac.at[way],
            dst_ref=rfac.at[way],
            send_sem=fsend_sem.at[way],
            recv_sem=frecv_sem.at[way],
            device_id=nearer(way),
            device_id_type=MESH,
        )

    def has_in(way):
        return jnp.where(way == 0, z, NZ - 1 - z) > 0

    def has_out(way):
        return jnp.where(way == 0, NZ - 1 - z, z) > 0

    def relay_factor(way):
        @pl.when(has_in(way))
        def _():
            factor_hop(way).wait_recv()

        @pl.when(has_out(way))
        def _():
            sfac[way] = rfac[way] * dec[...]
            factor_hop(way).start()

    def relay(way, c):
        @pl.when(has_in(way))
        def _():
            hop(way, c).wait_recv()

        @pl.when(has_out(way))
        def _():
            rows = pl.ds(pl.multiple_of(c * RC, RC), RC)
            main = rbuf[way, c, 0:RC, :]
            aux = rbuf[way, c, RC : 2 * RC, :]
            sbuf[way, c, 0:RC, :] = dec[...] * main + loc[way, rows, :]
            sbuf[way, c, RC : 2 * RC, :] = aux + rfac[way] * loc[1 - way, rows, :]
            hop(way, c).start()

    def remote(src, dst, send, recv, target):
        return pltpu.make_async_remote_copy(
            src_ref=src, dst_ref=dst, send_sem=send, recv_sem=recv, device_id=target,
            device_id_type=MESH,
        )

    def across(k):
        return device(lax.rem(x + k, NX), y, ring, core)

    def exchange_factor():
        xfac[...] = rfac[0] * rfac[1] * dec[...]
        for k in range(1, NX):
            remote(xfac, xdec.at[x], xsend_sem.at[0, k], xrecv_sem.at[0, x], across(k)).start()

    def exchange(c):
        rows = pl.ds(pl.multiple_of(c * RC, RC), RC)
        xsend[0, c] = (
            rfac[1] * (dec[...] * rbuf[0, c, 0:RC, :] + loc[0, rows, :])
            + rbuf[1, c, RC : 2 * RC, :]
        )
        xsend[1, c] = (
            rfac[0] * (dec[...] * rbuf[1, c, 0:RC, :] + loc[1, rows, :])
            + rbuf[0, c, RC : 2 * RC, :]
        )
        for k in range(1, NX):
            kind = (lax.rem(x + k, NX) < x).astype(jnp.int32)
            remote(
                xsend.at[kind, c], xrecv.at[x, c], xsend_sem.at[1, k], xrecv_sem.at[1, x],
                across(k),
            ).start()

    def all_pieces(k, source):
        return remote(
            xrecv.at[source], xrecv.at[source], xsend_sem.at[1, k], xrecv_sem.at[1, source],
            across(k),
        )

    def the_factor(k, source):
        return remote(
            xfac, xdec.at[source], xsend_sem.at[0, k], xrecv_sem.at[0, source], across(k)
        )

    def relay_first(c, _):
        relay(first, c)
        return 0

    def relay_second(c, _):
        relay(1 - first, c)
        exchange(c)
        return 0

    early = jnp.logical_or(z < 4, z >= NZ - 4)

    @pl.when(early)
    def _():
        relay_factor(first)
        lax.fori_loop(0, NC, relay_first, 0)

    pair_s[...] = jnp.zeros_like(pair_s)
    low = iota((128, 128), 1) < P_SIZE
    for sb in range(2):
        t0 = 128 * sb
        wide = L - t0
        rs = slice(t0, t0 + 128)
        gram = dot_nt(xb[rs, INNER : INNER + N], xb[t0:, INNER + N :])
        mask = iota((128, wide), 1) >= iota((128, wide), 0)
        dgram = jnp.zeros((128, wide), F32)
        for j in range(2):
            cot_t = cot_ref[t0:, 128 * j : 128 * j + 128]
            v_t = xb[rs, 128 * j : 128 * j + 128]
            parts = []
            for i in range(2):
                h = 2 * j + i
                keep = low if i == 0 else jnp.logical_not(low)
                v_h = jnp.where(keep, v_t.astype(F32), 0.0).astype(BF16)
                gap = rows_s[h : h + 1, t0:] - cols_s[rs, h : h + 1]
                within = jnp.exp(jnp.where(mask, gap, -1e30))
                dmix = dot_nt(v_h, cot_t)
                hi, lo = split(gram * within)
                parts.append(dot(hi, cot_t) + dot(lo, cot_t))
                dw = dmix * within * cols_s[rs, 8 + h : 9 + h]
                dgram = dgram + dw
                pair_s[h : h + 1, t0:] += jnp.sum(dw * gram, axis=0, keepdims=True)
            ac[rs, 128 * j : 128 * j + 128] = jnp.where(low, parts[0], parts[1])
        hi, lo = split(dgram)
        c_t = xb[t0:, INNER + N :]
        b_s = xb[rs, INNER : INNER + N]
        gbl[rs, :] = dot(hi, c_t) + dot(lo, c_t)
        from_here = dot_tn(hi, b_s) + dot_tn(lo, b_s)
        if sb == 0:
            gcl[...] = from_here
        else:
            gcl[t0:, :] += from_here

    @pl.when(jnp.logical_not(early))
    def _():
        relay_factor(first)
        lax.fori_loop(0, NC, relay_first, 0)

    relay_factor(1 - first)
    exchange_factor()
    lax.fori_loop(0, NC, relay_second, 0)

    for k in range(1, NX):
        source = lax.rem(x + k, NX)
        the_factor(k, source).wait_recv()
        all_pieces(k, source).wait_recv()

    def gather(c, _):
        rows = pl.ds(pl.multiple_of(c * RC, RC), RC)
        s_in[rows, :] = jnp.zeros((RC, INNER), F32)
        g_after[rows, :] = jnp.zeros((RC, INNER), F32)
        for k in range(NX - 1):

            @pl.when(k < x)
            def _():
                s_in[rows, :] = xdec[k] * s_in[rows, :] + xrecv[k, c]

        for k in range(NX - 1, 0, -1):

            @pl.when(k > x)
            def _():
                g_after[rows, :] = xdec[k] * g_after[rows, :] + xrecv[k, c]

        s_in[rows, :] = rbuf[0, c, 0:RC, :] + rfac[0] * s_in[rows, :]
        g_after[rows, :] = rbuf[1, c, 0:RC, :] + rfac[1] * g_after[rows, :]
        return 0

    lax.fori_loop(0, NC, gather, 0)

    @pl.when(z == 0)
    def _():
        pl.semaphore_signal(
            edge_sem, inc=1, device_id=device(x, y, lax.rem(ring + ZR - 1, ZR), core),
            device_id_type=MESH,
        )
        pl.semaphore_wait(edge_sem, 1)
        for k in range(1, NZ // 2):
            pl.semaphore_signal(
                known_sem, inc=1, device_id=device(x, y, ring + k, core), device_id_type=MESH
            )

    @pl.when(z == NZ - 1)
    def _():
        pl.semaphore_signal(
            edge_sem, inc=1, device_id=device(x, y, lax.rem(ring + 1, ZR), core),
            device_id_type=MESH,
        )
        pl.semaphore_wait(edge_sem, 1)
        for k in range(1, NZ // 2):
            pl.semaphore_signal(
                known_sem, inc=1, device_id=device(x, y, ring - k, core), device_id_type=MESH
            )

    b_val = xb[:, INNER : INNER + N]
    c_val = xb[:, INNER + N :]
    s_hi, s_lo = split(s_in[...])
    g_hi, g_lo = split(g_after[...])
    state_back = dot(b_val, g_hi) + dot(b_val, g_lo)
    state_proj = dot(c_val, s_hi) + dot(c_val, s_lo)
    cot = cot_ref[...].astype(F32)
    vals = xb[:, :INNER].astype(F32)
    scaled = cot * up_e[...]
    hi, lo = split(scaled)
    grad_c = gcl[...] + dot_nt(hi, s_hi) + dot_nt(hi, s_lo) + dot_nt(lo, s_hi)
    hi, lo = split(vals * tw_e[...])
    grad_b = gbl[...] + dot_nt(hi, g_hi) + dot_nt(hi, g_lo) + dot_nt(lo, g_hi)
    local_step = head_sums(vals * ac[...])
    tail_grad = head_sums(vals * state_back)
    proj_term = head_sums(scaled * state_proj)
    skip_lanes = spread(jnp.broadcast_to(0.0, (8, 128)) + sum(
        jnp.where(iota((8, 128), 1) == h, skip_ref[h], 0.0) for h in range(H)
    ), 0)[0:1, :]
    grad_vals = st_e[...] * ac[...] + skip_lanes * cot + tw_e[...] * state_back

    step = rows_s[8:16, :]
    tw = rows_s[16:24, :]
    cum = rows_s[0:8, :]
    cum_last = cum[:, L - 1 : L]
    sel = head_rows(F32)
    skip_sum = jnp.sum(sel * jnp.sum(cot * vals, axis=0, keepdims=True), axis=1, keepdims=True)
    both = jnp.sum(
        sel * jnp.sum(s_in[...] * g_after[...], axis=0, keepdims=True), axis=1, keepdims=True
    )
    tail_term = tail_grad * tw
    extra = jnp.sum(tail_term, axis=1, keepdims=True) + jnp.exp(cum_last) * both
    grad_cum = pair_s[...] - step * local_step + proj_term - tail_term
    since = (iota((L, L), 0) >= iota((L, L), 1)).astype(F32).astype(BF16)
    grad_log = sum(dot(part, since) for part in split3(grad_cum)) + extra
    rows_s[32 : 32 + H, :] = dt_ref[...]
    dt_pre = rows_s[32:40, :] + head_column(dt_bias_ref)
    rate = -jnp.exp(head_column(a_log_ref))
    grad_step = local_step + tail_grad * jnp.exp(cum_last - cum) + rate * grad_log
    grad_pre = grad_step / (1.0 + jnp.exp(-dt_pre))
    gpre_ref[...] = grad_pre[0:H, :]
    alog_sum = rate * jnp.sum(grad_log * step, axis=1, keepdims=True)
    bias_sum = jnp.sum(grad_pre, axis=1, keepdims=True)

    gc_pad[0:8, :] = jnp.zeros((8, CH), F32)
    gc_pad[8 + L : 16 + L, :] = jnp.zeros((8, CH), F32)
    for lanes, value in (
        (slice(0, INNER), grad_vals),
        (slice(INNER, INNER + N), grad_b),
        (slice(INNER + N, CH), grad_c),
    ):
        low_value = value.astype(BF16).astype(F32)
        sig = sig_s[:, lanes]
        gc_pad[8 : 8 + L, lanes] = low_value * sig * (1.0 + pre_s[:, lanes] * (1.0 - sig))

    spill_out[...] = sum(w_ref[k : k + 1, :] * gc_pad[3 - k : 11 - k, :] for k in range(K))

    def spill(target):
        return remote(spill_out, spill_in, ssend_sem.at[0], srecv_sem.at[0], (target, dp))

    @pl.when(place > 0)
    def _():
        spill(place - 1).start()

    sums_ref[...] = jnp.zeros_like(sums_ref)
    for k in range(K + 1):
        term = gc_pad[8 : 8 + L, :]
        if k < K:
            term = term * xp[5 + k : 5 + k + L, :]
        total = jnp.sum(term, axis=0, keepdims=True)
        for j in range(4):
            sums_ref[4 * k + j] = total[:, 128 * j : 128 * j + 128]
    lane = iota((8, 128), 1)
    row = iota((8, 128), 0)
    small = (
        jnp.where(lane == row, bias_sum, 0.0)
        + jnp.where(lane == row + 8, alog_sum, 0.0)
        + jnp.where(lane == row + 16, skip_sum, 0.0)
    )
    small = jnp.where(row < H, small, 0.0)
    sums_ref[20] = jnp.sum(small, axis=0, keepdims=True)

    me = (x * NY + y) * 2 + core

    def in_plane(k):
        r = lax.rem(me + k, NR)
        return r, device(r // 8, lax.rem(r // 2, NY), ring, lax.rem(r, 2))

    def all_of(buf, stage):
        part = buf.at[pl.ds(0, NR - 1)]
        return remote(part, part, rsend_sem.at[stage], rrecv_sem.at[stage], in_plane(1)[1])

    def scatter(k, _):
        r, target = in_plane(k)
        remote(sums_ref.at[r], plane.at[me], rsend_sem.at[0], rrecv_sem.at[0], target).start()
        return 0

    lax.fori_loop(1, NR, scatter, 0)
    plane[pl.ds(me, 1)] = sums_ref[pl.ds(me, 1)]
    for r in range(0, L, 64):
        rows = sum(
            w_ref[k : k + 1, :] * gc_pad[11 - k + r : 11 - k + r + 64, :] for k in range(K)
        )
        gx_ref[r : r + 64, :] = rows.astype(BF16)
        if r + 64 == L:
            tail = rows[48:64, :]

    @pl.when(jnp.logical_and(z > 0, z < NZ - 1))
    def _():
        pl.semaphore_wait(known_sem, 1)

    all_of(plane, 0).wait_recv()
    mine = jnp.sum(plane[...], axis=0, keepdims=True)
    own[0:1] = mine

    def along(k, _):
        q = lax.rem(ring + k, ZR)
        remote(
            own.at[0], line.at[ring], rsend_sem.at[1], rrecv_sem.at[1], device(x, y, q, core)
        ).start()
        return 0

    lax.fori_loop(1, ZR, along, 0)
    line[pl.ds(ring, 1)] = mine

    @pl.when(place < NX * NZ - 1)
    def _():
        spill(place + 1).wait_recv()

    @pl.when(place == NX * NZ - 1)
    def _():
        spill_in[...] = jnp.zeros_like(spill_in)

    gx_ref[L - 16 : L, :] = jnp.concatenate(
        [tail[0:8, :], tail[8:16, :] + spill_in[...]], axis=0
    ).astype(BF16)

    all_of(line, 1).wait_recv()
    total = jnp.sum(line[...], axis=0, keepdims=True)
    own[1:2] = total
    totals[pl.ds(me, 1)] = total

    def spread_out(k, _):
        remote(
            own.at[1], totals.at[me], rsend_sem.at[2], rrecv_sem.at[2], in_plane(k)[1]
        ).start()
        return 0

    lax.fori_loop(1, NR, spread_out, 0)
    def drain(c, _):
        for way in range(2):

            @pl.when(has_out(way))
            def _():
                hop(way, c).wait_send()

        return 0

    lax.fori_loop(0, NC, drain, 0)
    for way in range(2):

        @pl.when(has_out(way))
        def _():
            factor_hop(way).wait_send()

    for k in range(1, NX):
        source = lax.rem(x + k, NX)
        the_factor(k, source).wait_send()
        all_pieces(k, source).wait_send()

    @pl.when(place > 0)
    def _():
        spill(place - 1).wait_send()

    for stage, buf in enumerate((plane, line)):
        all_of(buf, stage).wait_send()
    all_of(totals, 2).wait_recv()
    for k in range(K):
        for j in range(4):
            wg_ref[k : k + 1, 128 * j : 128 * j + 128] = totals[4 * k + j]
    for j in range(4):
        bg_ref[0:1, 128 * j : 128 * j + 128] = totals[16 + j]
    small_ref[...] = totals[20]
    all_of(totals, 2).wait_send()


def run_main(halo, raw, weight, bias, dt_t, dt_bias, a_log, d_skip, cot):
    vmem = pl.BlockSpec(memory_space=pltpu.VMEM)
    smem = pl.BlockSpec(memory_space=pltpu.SMEM)
    hbm = pl.BlockSpec(memory_space=pl.ANY)
    return pl.pallas_call(
        main_kernel,
        out_shape=(
            jax.ShapeDtypeStruct((L, CH), BF16),
            jax.ShapeDtypeStruct((H, L), F32),
            jax.ShapeDtypeStruct((K, CH), F32),
            jax.ShapeDtypeStruct((1, CH), F32),
            jax.ShapeDtypeStruct((1, 128), F32),
        ),
        in_specs=[smem] * 3 + [vmem] + [hbm] * 5,
        out_specs=(vmem,) * 5,
        scratch_shapes=[
            pltpu.VMEM((L, CH), BF16),
            pltpu.VMEM((K, CH), F32),
            pltpu.VMEM((1, CH), F32),
            pltpu.VMEM((H, L), F32),
            pltpu.VMEM((L, INNER), BF16),
            pltpu.SemaphoreType.DMA((5,)),
            pltpu.VMEM((8 + L, CH), F32),
            pltpu.VMEM((L, CH), F32),
            pltpu.VMEM((L, CH), F32),
            pltpu.VMEM((L, CH), BF16),
            pltpu.VMEM((128, L), F32),
            pltpu.VMEM((L, 128), F32),
            pltpu.VMEM((2, N, INNER), F32),
            pltpu.VMEM((8, INNER), F32),
            pltpu.VMEM((L, INNER), F32),
            pltpu.VMEM((L, INNER), F32),
            pltpu.VMEM((L, INNER), F32),
            pltpu.VMEM((L, INNER), F32),
            pltpu.VMEM((L, N), F32),
            pltpu.VMEM((L, N), F32),
            pltpu.VMEM((8, L), F32),
            pltpu.VMEM((16 + L, CH), F32),
            pltpu.VMEM((2, NC, 2 * RC, INNER), F32),
            pltpu.VMEM((2, NC, 2 * RC, INNER), F32),
            pltpu.VMEM((2, 8, INNER), F32),
            pltpu.VMEM((2, 8, INNER), F32),
            pltpu.VMEM((2, NC, RC, INNER), F32),
            pltpu.VMEM((NX, NC, RC, INNER), F32),
            pltpu.VMEM((8, INNER), F32),
            pltpu.VMEM((NX, 8, INNER), F32),
            pltpu.VMEM((N, INNER), F32),
            pltpu.VMEM((N, INNER), F32),
            pltpu.VMEM((8, CH), F32),
            pltpu.VMEM((8, CH), F32),
            pltpu.VMEM((NR, 1, 128), F32),
            pltpu.VMEM((NR, 1, 128), F32),
            pltpu.VMEM((ZR, 1, 128), F32),
            pltpu.VMEM((2, 1, 128), F32),
            pltpu.VMEM((NR, 1, 128), F32),
            pltpu.SemaphoreType.DMA((2, NC)),
            pltpu.SemaphoreType.DMA((2, NC)),
            pltpu.SemaphoreType.DMA((2,)),
            pltpu.SemaphoreType.DMA((2,)),
            pltpu.SemaphoreType.DMA((2, NX)),
            pltpu.SemaphoreType.DMA((2, NX)),
            pltpu.SemaphoreType.DMA((1,)),
            pltpu.SemaphoreType.DMA((1,)),
            pltpu.SemaphoreType.DMA((3,)),
            pltpu.SemaphoreType.DMA((3,)),
            pltpu.SemaphoreType.REGULAR,
            pltpu.SemaphoreType.REGULAR,
        ],
        compiler_params=pltpu.CompilerParams(
            collective_id=0, has_side_effects=True, vmem_limit_bytes=48 << 20
        ),
        name="slab",
    )(dt_bias, a_log, d_skip, halo, raw, weight, bias, dt_t, cot)


def shift(block, axis, distance):
    devices = range(lax.axis_size(axis))
    route = [(i - distance, i) for i in devices if i - distance in devices]
    return lax.ppermute(block, axis, route)


def on_device(xbc_raw, conv_weight, conv_bias, dt_raw, dt_bias, a_log, d_skip, grad_out):
    raw = xbc_raw[0]
    halo = shift(raw[L - 8 :], "ctx", 1)
    gx, gpre, weight_grad, bias_grad, small = run_main(
        halo, raw, conv_weight, conv_bias[None], dt_raw[0].T, dt_bias, a_log, d_skip, grad_out[0]
    )
    return (
        gx[None], gpre.T[None], weight_grad, bias_grad[0], small[0, 0:4], small[0, 8:12],
        small[0, 16:20],
    )


def solution(mesh):
    rows = P("dp", "ctx", None)
    return jax.shard_map(
        on_device,
        mesh=mesh,
        in_specs=(rows, P(), P(), rows, P(), P(), P(), rows),
        out_specs=(rows, rows, P(), P(), P(), P(), P()),
        check_vma=False,
    )
```

```python
import functools

import jax
import jax.numpy as jnp
from jax import lax
from jax.experimental import pallas as pl
from jax.experimental.pallas import tpu as pltpu
from jax.sharding import PartitionSpec as P

H = 4
P_SIZE = 64
N = 128
K = 4
L = 256
CH = 512
INNER = H * P_SIZE
NZ = 16
NX = 4
NY = 4
NR = 32
ZR = 32
NB = 4
NO = 16
RC = N // NO
F32 = jnp.float32
BF16 = jnp.bfloat16
MESH = pl.DeviceIdType.MESH


def dot(a, b):
    return lax.dot_general(a, b, (((1,), (0,)), ((), ())), preferred_element_type=F32)


def dot_nt(a, b):
    return lax.dot_general(a, b, (((1,), (1,)), ((), ())), preferred_element_type=F32)


def dot_tn(a, b):
    return lax.dot_general(a, b, (((0,), (0,)), ((), ())), preferred_element_type=F32)


def split(a):
    hi = a.astype(BF16)
    return hi, (a - hi.astype(F32)).astype(BF16)


def split3(a):
    hi = a.astype(BF16)
    rest = a - hi.astype(F32)
    mid = rest.astype(BF16)
    return hi, mid, (rest - mid.astype(F32)).astype(BF16)


def iota(shape, dim):
    return lax.broadcasted_iota(jnp.int32, shape, dim)


def head_column(ref):
    rows = iota((8, 1), 0)
    col = jnp.zeros((8, 1), F32)
    for h in range(H):
        col = jnp.where(rows == h, ref[h], col)
    return col


def spread(cols, first):
    rows = cols.shape[0]
    low = iota((rows, 128), 1) < P_SIZE
    tiles = []
    for j in range(2):
        a = jnp.broadcast_to(cols[:, first + 2 * j : first + 2 * j + 1], (rows, 128))
        b = jnp.broadcast_to(cols[:, first + 2 * j + 1 : first + 2 * j + 2], (rows, 128))
        tiles.append(jnp.where(low, a, b))
    return jnp.concatenate(tiles, axis=1)


def head_rows(dtype):
    return (iota((8, INNER), 1) // P_SIZE == iota((8, INNER), 0)).astype(dtype)


def head_sums(x):
    sel = head_rows(F32).astype(BF16)
    hi, lo = split(x)
    return dot_nt(sel, hi) + dot_nt(sel, lo)


def main_kernel(
    dt_bias_ref, a_log_ref, skip_ref, raw_hbm, w_hbm, bias_hbm, dt_hbm, cot_hbm,
    gx_ref, gpre_ref, wg_ref, bg_ref, small_ref,
    raw_ref, w_ref, bias_ref, dt_ref, cot_ref, in_sem,
    xp, pre_s, sig_s, xb, rows_s, cols_s, loc, dec, tw_e, up_e, st_e, ac, gbl, gcl, pair_s,
    gc_pad, abuf, dbuf, pre_p, pre_q, tot, blk, rbuf, sbuf, rfac, sfac, heads, tails, cfull, corr,
    rsend, ret, near_out, near_in, spill_out, spill_in, sums_ref, plane, line, own, totals,
    send_sem, recv_sem, fsend_sem, frecv_sem, asend_sem, arecv_sem, hsend_sem, hrecv_sem,
    hcast_sem, nsend_sem, nrecv_sem, ssend_sem, srecv_sem, rsend_sem, rrecv_sem, edge_sem,
    known_sem,
):
    place = lax.axis_index("ctx")
    dp = lax.axis_index("dp")
    z = lax.rem(place, NZ)
    x = place // NZ
    y = dp // 4
    z_hi = lax.rem(dp // 2, 2)
    core = lax.rem(dp, 2)

    def device(x_, y_, ring, core_):
        return (x_ * NZ + lax.rem(ring, NZ), y_ * 4 + (ring // NZ) * 2 + core_)

    ring = z_hi * NZ + z
    zq = z // NB
    zi = lax.rem(z, NB)
    me_o = x * NB + zi

    def remote(src, dst, send, recv, target):
        return pltpu.make_async_remote_copy(
            src_ref=src, dst_ref=dst, send_sem=send, recv_sem=recv, device_id=target,
            device_id_type=MESH,
        )

    def mate(k):
        o = lax.rem(me_o + k, NO)
        return o, ((o // NB) * NZ + zq * NB + lax.rem(o, NB), dp)

    heads[...] = jnp.zeros_like(heads)
    tails[...] = jnp.zeros_like(tails)
    barrier = pltpu.get_barrier_semaphore()
    inputs = [
        pltpu.make_async_copy(src, dst, in_sem.at[i])
        for i, (src, dst) in enumerate(
            ((raw_hbm, raw_ref), (w_hbm, w_ref), (bias_hbm, bias_ref), (dt_hbm, dt_ref),
             (cot_hbm, cot_ref))
        )
    ]
    for copy in inputs:
        copy.start()
    for step in (1, ZR - 1, NB, ZR - NB):
        pl.semaphore_signal(
            barrier, inc=1, device_id=device(x, y, lax.rem(ring + step, ZR), core),
            device_id_type=MESH,
        )

    def greet(k, _):
        pl.semaphore_signal(barrier, inc=1, device_id=mate(k)[1], device_id_type=MESH)
        return 0

    lax.fori_loop(1, NO, greet, 0)
    for k in range(1, 2 * NY):
        q = lax.rem(y * 2 + core + k, 2 * NY)
        pl.semaphore_signal(
            barrier, inc=1, device_id=device(x, q // 2, ring, lax.rem(q, 2)), device_id_type=MESH
        )
    for copy in inputs:
        copy.wait()

    xp[0:8, :] = jnp.zeros((8, CH), F32)
    xp[8 : 8 + L, :] = raw_ref[...].astype(F32)

    def activate(r, size):
        pre = bias_ref[...] + sum(
            w_ref[k : k + 1, :] * xp[5 + k + r : 5 + k + r + size, :] for k in range(K)
        )
        sig = 1.0 / (1.0 + jnp.exp(-pre))
        pre_s[r : r + size, :] = pre
        sig_s[r : r + size, :] = sig
        xb[r : r + size, :] = (pre * sig).astype(BF16)

    for r in range(0, L, 64):
        activate(r, 64)

    rate = -jnp.exp(head_column(a_log_ref))
    live = iota((8, 1), 0) < H
    rate = jnp.where(live, rate, 0.0)
    rows_s[...] = jnp.zeros_like(rows_s)
    rows_s[0:H, :] = dt_ref[...]
    dt_pre = rows_s[0:8, :] + head_column(dt_bias_ref)
    step = jnp.where(
        live, jnp.maximum(dt_pre, 0.0) + jnp.log1p(jnp.exp(-jnp.abs(dt_pre))), 0.0
    )
    upto = (iota((L, L), 0) <= iota((L, L), 1)).astype(F32).astype(BF16)
    cum = sum(dot(part, upto) for part in split3(step * rate))
    cum_last = cum[:, L - 1 : L]
    to_end = jnp.exp(cum_last - cum)
    tw = to_end * step
    up = jnp.exp(cum)
    rows_s[0:8, :] = cum
    rows_s[8:16, :] = step
    rows_s[16:24, :] = tw
    rows_s[24:32, :] = up
    cols = jnp.transpose(rows_s[...])
    cols_s[...] = cols
    tw_e[...] = spread(cols, 16)
    up_e[...] = spread(cols, 24)
    st_e[...] = spread(cols, 8)
    dec[0] = up_e[L - 1 : L, :]
    near_out[0:3, :] = xp[5 + L : 8 + L, :]

    pl.semaphore_wait(barrier, 4 + NO - 1 + 2 * NY - 1)

    def near(target):
        return remote(
            near_out.at[0:3], near_in.at[0:3], nsend_sem.at[0], nrecv_sem.at[0], (target, dp)
        )

    @pl.when(z < NZ - 1)
    def _():
        near(place + 1).start()

    def head(l, send, target):
        return remote(heads.at[l, 0:3], heads.at[l, 0:3], send, hrecv_sem.at[0, l], target)

    def last(l, send, target):
        return remote(tails.at[l, 0:3], tails.at[l, 0:3], send, hrecv_sem.at[1, l], target)

    @pl.when(z == 0)
    def _():
        heads[x, 0:3, 0:CH] = pre_s[0:3, :]
        heads[x, 0:3, CH : CH + INNER] = tw_e[0:3, :]
        heads[x, 0:3, CH + INNER :] = (cot_ref[...].astype(F32) * up_e[...])[0:3, :]

        def cast(k, _):
            o, target = mate(k)
            head(x, hcast_sem.at[k], target).start()
            return 0

        lax.fori_loop(1, NO, cast, 0)

    has_tail = jnp.logical_and(z == NZ - 1, x < NX - 1)

    @pl.when(has_tail)
    def _():
        tails[x + 1, 0:3, :] = near_out[0:3, :]

        def cast(k, _):
            o, target = mate(k)
            last(x + 1, hcast_sem.at[k], target).start()
            return 0

        lax.fori_loop(1, NO, cast, 0)

    @pl.when(z > 0)
    def _():
        near(place - 1).wait_recv()
        xp[5:8, :] = near_in[0:3, :]
        activate(0, 16)

    ready = jnp.logical_or(iota((L, INNER), 0) >= 3, z > 0)
    b_val = xb[:, INNER : INNER + N]
    c_val = xb[:, INNER + N :]
    hi, lo = split(jnp.where(ready, xb[:, :INNER].astype(F32) * tw_e[...], 0.0))
    loc[:, 0:RC, :] = (dot_tn(b_val, hi) + dot_tn(b_val, lo)).reshape(NO, RC, INNER)
    hi, lo = split(jnp.where(ready, cot_ref[...].astype(F32) * up_e[...], 0.0))
    loc[:, RC:, :] = (dot_tn(c_val, hi) + dot_tn(c_val, lo)).reshape(NO, RC, INNER)

    def to_owners(k, _):
        o, target = mate(k)
        remote(dec.at[0], dbuf.at[me_o], asend_sem.at[0], arecv_sem.at[0], target).start()
        remote(loc.at[o], abuf.at[me_o], asend_sem.at[1], arecv_sem.at[1], target).start()
        return 0

    lax.fori_loop(1, NO, to_owners, 0)
    abuf[pl.ds(me_o, 1)] = loc[pl.ds(me_o, 1)]
    dbuf[pl.ds(me_o, 1)] = dec[...]

    def from_block(buf, i):
        part = buf.at[pl.ds(0, NO - 1)]
        return remote(part, part, asend_sem.at[i], arecv_sem.at[i], mate(1)[1])

    def along_line(step):
        return (place + NB * step, dp)

    def relay_heads():
        for l in range(NX):

            @pl.when(jnp.logical_not(jnp.logical_and(z == 0, x == l)))
            def _():
                head(l, hsend_sem.at[0, l], along_line(1)).wait_recv()

            @pl.when(zq < NB - 1)
            def _():
                head(l, hsend_sem.at[0, l], along_line(1)).start()

    def relay_tails():
        for l in range(1, NX):

            @pl.when(jnp.logical_not(jnp.logical_and(z == NZ - 1, x == l - 1)))
            def _():
                last(l, hsend_sem.at[1, l], along_line(-1)).wait_recv()

            @pl.when(zq > 0)
            def _():
                last(l, hsend_sem.at[1, l], along_line(-1)).start()

    def local_terms():
        pair_s[...] = jnp.zeros_like(pair_s)
        low = iota((128, 128), 1) < P_SIZE
        for sb in range(2):
            t0 = 128 * sb
            wide = L - t0
            rs = slice(t0, t0 + 128)
            gram = dot_nt(xb[rs, INNER : INNER + N], xb[t0:, INNER + N :])
            mask = iota((128, wide), 1) >= iota((128, wide), 0)
            dgram = jnp.zeros((128, wide), F32)
            for j in range(2):
                cot_t = cot_ref[t0:, 128 * j : 128 * j + 128]
                v_t = xb[rs, 128 * j : 128 * j + 128]
                parts = []
                for i in range(2):
                    h = 2 * j + i
                    keep = low if i == 0 else jnp.logical_not(low)
                    v_h = jnp.where(keep, v_t.astype(F32), 0.0).astype(BF16)
                    gap = rows_s[h : h + 1, t0:] - cols_s[rs, h : h + 1]
                    within = jnp.exp(jnp.where(mask, gap, -1e30))
                    dmix = dot_nt(v_h, cot_t)
                    hi, lo = split(gram * within)
                    parts.append(dot(hi, cot_t) + dot(lo, cot_t))
                    dw = dmix * within * cols_s[rs, 8 + h : 9 + h]
                    dgram = dgram + dw
                    pair_s[h : h + 1, t0:] += jnp.sum(dw * gram, axis=0, keepdims=True)
                ac[rs, 128 * j : 128 * j + 128] = jnp.where(low, parts[0], parts[1])
            hi, lo = split(dgram)
            c_t = xb[t0:, INNER + N :]
            b_s = xb[rs, INNER : INNER + N]
            gbl[rs, :] = dot(hi, c_t) + dot(lo, c_t)
            from_here = dot_tn(hi, b_s) + dot_tn(lo, b_s)
            if sb == 0:
                gcl[...] = from_here
            else:
                gcl[t0:, :] += from_here

    @pl.when(z > 0)
    def _():
        local_terms()

    left = zq < NB // 2

    @pl.when(left)
    def _():
        relay_heads()

    @pl.when(jnp.logical_not(left))
    def _():
        relay_tails()

    from_block(dbuf, 0).wait_recv()
    from_block(abuf, 1).wait_recv()
    for l in range(NX):
        p = abuf[NB * l, 0:RC, :]
        q = abuf[NB * l + NB - 1, RC:, :]
        for i in range(1, NB):
            pre_p[NB * l + i] = p
            p = dbuf[NB * l + i] * p + abuf[NB * l + i, 0:RC, :]
            j = NB - 1 - i
            pre_q[NB * l + j] = q
            q = dbuf[NB * l + j] * q + abuf[NB * l + j, RC:, :]
        tot[0, l] = p
        tot[1, l] = q
        blk[l] = dbuf[NB * l] * dbuf[NB * l + 1] * dbuf[NB * l + 2] * dbuf[NB * l + 3]

    @pl.when(zq == 0)
    def _():
        rbuf[0] = jnp.zeros((NX, 2 * RC, INNER), F32)
        rfac[0] = jnp.ones((8, INNER), F32)

    @pl.when(zq == NB - 1)
    def _():
        rbuf[1] = jnp.zeros((NX, 2 * RC, INNER), F32)
        rfac[1] = jnp.ones((8, INNER), F32)

    first = jnp.where(left, 0, 1)

    def hop(way, l):
        return remote(
            sbuf.at[way, l], rbuf.at[way, l], send_sem.at[way, l], recv_sem.at[way, l],
            along_line(1 - 2 * way),
        )

    def factor_hop(way):
        return remote(
            sfac.at[way], rfac.at[way], fsend_sem.at[way], frecv_sem.at[way],
            along_line(1 - 2 * way),
        )

    def has_in(way):
        return jnp.where(way == 0, zq, NB - 1 - zq) > 0

    def has_out(way):
        return jnp.where(way == 0, NB - 1 - zq, zq) > 0

    def head_weights(l):
        v0 = jnp.where(zq == 0, 0.0, rfac[0, 4 + l : 5 + l, :])
        v1 = jnp.where(zq == 0, 1.0, v0 * dbuf[NB * l])
        v2 = v1 * dbuf[NB * l + 1]
        v3 = v2 * dbuf[NB * l + 2]
        return v0, v1, v2, v3, v3 * dbuf[NB * l + 3]

    def relay(way):
        @pl.when(has_in(way))
        def _():
            factor_hop(way).wait_recv()

        @pl.when(has_out(way))
        def _():
            for l in range(NX):
                sfac[way, l : l + 1, :] = rfac[way, l : l + 1, :] * blk[l]
                sfac[way, 4 + l : 5 + l, :] = (
                    head_weights(l)[4] if way == 0 else jnp.zeros((1, INNER), F32)
                )
            factor_hop(way).start()

        for l in range(NX):

            @pl.when(has_in(way))
            def _():
                hop(way, l).wait_recv()

            @pl.when(has_out(way))
            def _():
                sbuf[way, l, 0:RC, :] = blk[l] * rbuf[way, l, 0:RC, :] + tot[way, l]
                sbuf[way, l, RC:, :] = (
                    rbuf[way, l, RC:, :] + rfac[way, l : l + 1, :] * tot[1 - way, l]
                )
                hop(way, l).start()

    @pl.when(left)
    def _():
        relay(0)
        relay_tails()

    @pl.when(jnp.logical_not(left))
    def _():
        relay(1)
        relay_heads()

    @pl.when(z == 0)
    def _():
        xp[5:8, :] = tails[x, 0:3, :]
        activate(0, 16)
        local_terms()

    mine_rows = pl.ds(pl.multiple_of(me_o * RC, RC), RC)
    for l in range(NX):
        pre = heads[l, :, 0:CH] + sum(w_ref[k : k + 1, :] * tails[l, k : k + 8, :] for k in range(3))
        act = jnp.where(iota((8, CH), 0) < 3, pre / (1.0 + jnp.exp(-pre)), 0.0).astype(BF16)
        hi, lo = split(act[:, :INNER].astype(F32) * heads[l, :, CH : CH + INNER])
        b_row = act[:, INNER : INNER + N]
        c_row = act[:, INNER + N :]
        cfull[...] = dot_tn(b_row, hi) + dot_tn(b_row, lo)
        corr[0, l] = cfull[mine_rows, :]
        hi, lo = split(heads[l, :, CH + INNER :])
        cfull[...] = dot_tn(c_row, hi) + dot_tn(c_row, lo)
        corr[1, l] = cfull[mine_rows, :]

    @pl.when(left)
    def _():
        relay(1)

    @pl.when(jnp.logical_not(left))
    def _():
        relay(0)

    def line_terms(l):
        f = rfac[0, l : l + 1, :]
        e = rfac[1, l : l + 1, :]
        return f, e, f * e * blk[l]

    def give_back(l, i, entering, way):
        rsend[NB * l + i, RC * way : RC * way + RC, :] = entering

    carry = jnp.zeros((RC, INNER), F32)
    for l in range(NX):
        f, e, whole = line_terms(l)
        weights = head_weights(l)
        at = rbuf[0, l, 0:RC, :] + f * carry
        for i in range(NB):
            here = at + weights[i] * corr[0, l]
            if i:
                here = here + pre_p[NB * l + i]
            give_back(l, i, here, 0)
            at = at * dbuf[NB * l + i]
        total = (
            e * (blk[l] * rbuf[0, l, 0:RC, :] + tot[0, l] + weights[4] * corr[0, l])
            + rbuf[1, l, RC:, :]
        )
        carry = whole * carry + total
    carry = jnp.zeros((RC, INNER), F32)
    for l in range(NX - 1, -1, -1):
        f, e, whole = line_terms(l)
        at = rbuf[1, l, 0:RC, :] + e * carry
        for i in range(NB - 1, -1, -1):
            here = at
            if i < NB - 1:
                here = here + pre_q[NB * l + i]
            give_back(l, i, here, 1)
            at = at * dbuf[NB * l + i]
        total = (
            f * (blk[l] * rbuf[1, l, 0:RC, :] + tot[1, l]) + rbuf[0, l, RC:, :] + corr[1, l]
        )
        carry = whole * carry + total

    def back(k, _):
        o, target = mate(k)
        remote(rsend.at[o], ret.at[me_o], asend_sem.at[2], arecv_sem.at[2], target).start()
        return 0

    lax.fori_loop(1, NO, back, 0)
    ret[pl.ds(me_o, 1)] = rsend[pl.ds(me_o, 1)]

    @pl.when(zq == 0)
    def _():
        pl.semaphore_signal(
            edge_sem, inc=1, device_id=device(x, y, lax.rem(ring + ZR - NB, ZR), core),
            device_id_type=MESH,
        )
        pl.semaphore_wait(edge_sem, 1)
        pl.semaphore_signal(known_sem, inc=1, device_id=along_line(1), device_id_type=MESH)

    @pl.when(zq == NB - 1)
    def _():
        pl.semaphore_signal(
            edge_sem, inc=1, device_id=device(x, y, lax.rem(ring + NB, ZR), core),
            device_id_type=MESH,
        )
        pl.semaphore_wait(edge_sem, 1)
        pl.semaphore_signal(known_sem, inc=1, device_id=along_line(-1), device_id_type=MESH)

    from_block(ret, 2).wait_recv()
    s_in = ret[:, 0:RC, :].reshape(N, INNER)
    g_after = ret[:, RC:, :].reshape(N, INNER)

    b_val = xb[:, INNER : INNER + N]
    c_val = xb[:, INNER + N :]
    s_hi, s_lo = split(s_in)
    g_hi, g_lo = split(g_after)
    state_back = dot(b_val, g_hi) + dot(b_val, g_lo)
    state_proj = dot(c_val, s_hi) + dot(c_val, s_lo)
    cot = cot_ref[...].astype(F32)
    vals = xb[:, :INNER].astype(F32)
    scaled = cot * up_e[...]
    hi, lo = split(scaled)
    grad_c = gcl[...] + dot_nt(hi, s_hi) + dot_nt(hi, s_lo) + dot_nt(lo, s_hi)
    hi, lo = split(vals * tw_e[...])
    grad_b = gbl[...] + dot_nt(hi, g_hi) + dot_nt(hi, g_lo) + dot_nt(lo, g_hi)
    local_step = head_sums(vals * ac[...])
    tail_grad = head_sums(vals * state_back)
    proj_term = head_sums(scaled * state_proj)
    skip_lanes = spread(jnp.broadcast_to(0.0, (8, 128)) + sum(
        jnp.where(iota((8, 128), 1) == h, skip_ref[h], 0.0) for h in range(H)
    ), 0)[0:1, :]
    grad_vals = st_e[...] * ac[...] + skip_lanes * cot + tw_e[...] * state_back

    step = rows_s[8:16, :]
    tw = rows_s[16:24, :]
    cum = rows_s[0:8, :]
    cum_last = cum[:, L - 1 : L]
    sel = head_rows(F32)
    skip_sum = jnp.sum(sel * jnp.sum(cot * vals, axis=0, keepdims=True), axis=1, keepdims=True)
    both = jnp.sum(
        sel * jnp.sum(s_in * g_after, axis=0, keepdims=True), axis=1, keepdims=True
    )
    tail_term = tail_grad * tw
    extra = jnp.sum(tail_term, axis=1, keepdims=True) + jnp.exp(cum_last) * both
    grad_cum = pair_s[...] - step * local_step + proj_term - tail_term
    since = (iota((L, L), 0) >= iota((L, L), 1)).astype(F32).astype(BF16)
    grad_log = sum(dot(part, since) for part in split3(grad_cum)) + extra
    rows_s[32 : 32 + H, :] = dt_ref[...]
    dt_pre = rows_s[32:40, :] + head_column(dt_bias_ref)
    rate = -jnp.exp(head_column(a_log_ref))
    grad_step = local_step + tail_grad * jnp.exp(cum_last - cum) + rate * grad_log
    grad_pre = grad_step / (1.0 + jnp.exp(-dt_pre))
    gpre_ref[...] = grad_pre[0:H, :]
    alog_sum = rate * jnp.sum(grad_log * step, axis=1, keepdims=True)
    bias_sum = jnp.sum(grad_pre, axis=1, keepdims=True)

    gc_pad[0:8, :] = jnp.zeros((8, CH), F32)
    gc_pad[8 + L : 16 + L, :] = jnp.zeros((8, CH), F32)
    for lanes, value in (
        (slice(0, INNER), grad_vals),
        (slice(INNER, INNER + N), grad_b),
        (slice(INNER + N, CH), grad_c),
    ):
        low_value = value.astype(BF16).astype(F32)
        sig = sig_s[:, lanes]
        gc_pad[8 : 8 + L, lanes] = low_value * sig * (1.0 + pre_s[:, lanes] * (1.0 - sig))

    spill_out[...] = sum(w_ref[k : k + 1, :] * gc_pad[3 - k : 11 - k, :] for k in range(K))

    def spill(target):
        return remote(spill_out, spill_in, ssend_sem.at[0], srecv_sem.at[0], (target, dp))

    @pl.when(place > 0)
    def _():
        spill(place - 1).start()

    sums_ref[...] = jnp.zeros_like(sums_ref)
    for k in range(K + 1):
        term = gc_pad[8 : 8 + L, :]
        if k < K:
            term = term * xp[5 + k : 5 + k + L, :]
        total = jnp.sum(term, axis=0, keepdims=True)
        for j in range(4):
            sums_ref[4 * k + j] = total[:, 128 * j : 128 * j + 128]
    lane = iota((8, 128), 1)
    row = iota((8, 128), 0)
    small = (
        jnp.where(lane == row, bias_sum, 0.0)
        + jnp.where(lane == row + 8, alog_sum, 0.0)
        + jnp.where(lane == row + 16, skip_sum, 0.0)
    )
    small = jnp.where(row < H, small, 0.0)
    sums_ref[20] = jnp.sum(small, axis=0, keepdims=True)

    me = (x * NY + y) * 2 + core

    def in_plane(k):
        r = lax.rem(me + k, NR)
        return r, device(r // 8, lax.rem(r // 2, NY), ring, lax.rem(r, 2))

    def all_of(buf, stage):
        part = buf.at[pl.ds(0, NR - 1)]
        return remote(part, part, rsend_sem.at[stage], rrecv_sem.at[stage], in_plane(1)[1])

    def scatter(k, _):
        r, target = in_plane(k)
        remote(sums_ref.at[r], plane.at[me], rsend_sem.at[0], rrecv_sem.at[0], target).start()
        return 0

    lax.fori_loop(1, NR, scatter, 0)
    plane[pl.ds(me, 1)] = sums_ref[pl.ds(me, 1)]
    for r in range(0, L, 64):
        rows = sum(
            w_ref[k : k + 1, :] * gc_pad[11 - k + r : 11 - k + r + 64, :] for k in range(K)
        )
        gx_ref[r : r + 64, :] = rows.astype(BF16)
        if r + 64 == L:
            tail = rows[48:64, :]

    @pl.when(jnp.logical_and(zq > 0, zq < NB - 1))
    def _():
        pl.semaphore_wait(known_sem, 1)

    all_of(plane, 0).wait_recv()
    mine = jnp.sum(plane[...], axis=0, keepdims=True)
    own[0:1] = mine

    def along(k, _):
        q = lax.rem(ring + k, ZR)
        remote(
            own.at[0], line.at[ring], rsend_sem.at[1], rrecv_sem.at[1], device(x, y, q, core)
        ).start()
        return 0

    lax.fori_loop(1, ZR, along, 0)
    line[pl.ds(ring, 1)] = mine

    @pl.when(place < NX * NZ - 1)
    def _():
        spill(place + 1).wait_recv()

    @pl.when(place == NX * NZ - 1)
    def _():
        spill_in[...] = jnp.zeros_like(spill_in)

    gx_ref[L - 16 : L, :] = jnp.concatenate(
        [tail[0:8, :], tail[8:16, :] + spill_in[...]], axis=0
    ).astype(BF16)

    all_of(line, 1).wait_recv()
    total = jnp.sum(line[...], axis=0, keepdims=True)
    own[1:2] = total
    totals[pl.ds(me, 1)] = total

    def spread_out(k, _):
        remote(
            own.at[1], totals.at[me], rsend_sem.at[2], rrecv_sem.at[2], in_plane(k)[1]
        ).start()
        return 0

    lax.fori_loop(1, NR, spread_out, 0)
    for way in range(2):

        @pl.when(has_out(way))
        def _():
            factor_hop(way).wait_send()
            for l in range(NX):
                hop(way, l).wait_send()

    @pl.when(zq < NB - 1)
    def _():
        for l in range(NX):
            head(l, hsend_sem.at[0, l], along_line(1)).wait_send()

    @pl.when(zq > 0)
    def _():
        for l in range(1, NX):
            last(l, hsend_sem.at[1, l], along_line(-1)).wait_send()

    @pl.when(z == 0)
    def _():
        for k in range(1, NO):
            head(0, hcast_sem.at[k], along_line(1)).wait_send()

    @pl.when(has_tail)
    def _():
        for k in range(1, NO):
            last(0, hcast_sem.at[k], along_line(-1)).wait_send()

    @pl.when(z < NZ - 1)
    def _():
        near(place + 1).wait_send()

    for i, buf in enumerate((dbuf, abuf, ret)):
        from_block(buf, i).wait_send()

    @pl.when(place > 0)
    def _():
        spill(place - 1).wait_send()

    for stage, buf in enumerate((plane, line)):
        all_of(buf, stage).wait_send()
    all_of(totals, 2).wait_recv()
    for k in range(K):
        for j in range(4):
            wg_ref[k : k + 1, 128 * j : 128 * j + 128] = totals[4 * k + j]
    for j in range(4):
        bg_ref[0:1, 128 * j : 128 * j + 128] = totals[16 + j]
    small_ref[...] = totals[20]
    all_of(totals, 2).wait_send()


def run_main(raw, weight, bias, dt_t, dt_bias, a_log, d_skip, cot):
    vmem = pl.BlockSpec(memory_space=pltpu.VMEM)
    smem = pl.BlockSpec(memory_space=pltpu.SMEM)
    hbm = pl.BlockSpec(memory_space=pl.ANY)
    return pl.pallas_call(
        main_kernel,
        out_shape=(
            jax.ShapeDtypeStruct((L, CH), BF16),
            jax.ShapeDtypeStruct((H, L), F32),
            jax.ShapeDtypeStruct((K, CH), F32),
            jax.ShapeDtypeStruct((1, CH), F32),
            jax.ShapeDtypeStruct((1, 128), F32),
        ),
        in_specs=[smem] * 3 + [hbm] * 5,
        out_specs=(vmem,) * 5,
        scratch_shapes=[
            pltpu.VMEM((L, CH), BF16),
            pltpu.VMEM((K, CH), F32),
            pltpu.VMEM((1, CH), F32),
            pltpu.VMEM((H, L), F32),
            pltpu.VMEM((L, INNER), BF16),
            pltpu.SemaphoreType.DMA((5,)),
            pltpu.VMEM((8 + L, CH), F32),
            pltpu.VMEM((L, CH), F32),
            pltpu.VMEM((L, CH), F32),
            pltpu.VMEM((L, CH), BF16),
            pltpu.VMEM((128, L), F32),
            pltpu.VMEM((L, 128), F32),
            pltpu.VMEM((NO, 2 * RC, INNER), F32),
            pltpu.VMEM((1, 1, INNER), F32),
            pltpu.VMEM((L, INNER), F32),
            pltpu.VMEM((L, INNER), F32),
            pltpu.VMEM((L, INNER), F32),
            pltpu.VMEM((L, INNER), F32),
            pltpu.VMEM((L, N), F32),
            pltpu.VMEM((L, N), F32),
            pltpu.VMEM((8, L), F32),
            pltpu.VMEM((16 + L, CH), F32),
            pltpu.VMEM((NO, 2 * RC, INNER), F32),
            pltpu.VMEM((NO, 1, INNER), F32),
            pltpu.VMEM((NO, RC, INNER), F32),
            pltpu.VMEM((NO, RC, INNER), F32),
            pltpu.VMEM((2, NX, RC, INNER), F32),
            pltpu.VMEM((NX, 1, INNER), F32),
            pltpu.VMEM((2, NX, 2 * RC, INNER), F32),
            pltpu.VMEM((2, NX, 2 * RC, INNER), F32),
            pltpu.VMEM((2, 8, INNER), F32),
            pltpu.VMEM((2, 8, INNER), F32),
            pltpu.VMEM((NX, 8, CH + 2 * INNER), F32),
            pltpu.VMEM((NX, 16, CH), F32),
            pltpu.VMEM((N, INNER), F32),
            pltpu.VMEM((2, NX, RC, INNER), F32),
            pltpu.VMEM((NO, 2 * RC, INNER), F32),
            pltpu.VMEM((NO, 2 * RC, INNER), F32),
            pltpu.VMEM((8, CH), F32),
            pltpu.VMEM((8, CH), F32),
            pltpu.VMEM((8, CH), F32),
            pltpu.VMEM((8, CH), F32),
            pltpu.VMEM((NR, 1, 128), F32),
            pltpu.VMEM((NR, 1, 128), F32),
            pltpu.VMEM((ZR, 1, 128), F32),
            pltpu.VMEM((2, 1, 128), F32),
            pltpu.VMEM((NR, 1, 128), F32),
            pltpu.SemaphoreType.DMA((2, NX)),
            pltpu.SemaphoreType.DMA((2, NX)),
            pltpu.SemaphoreType.DMA((2,)),
            pltpu.SemaphoreType.DMA((2,)),
            pltpu.SemaphoreType.DMA((3,)),
            pltpu.SemaphoreType.DMA((3,)),
            pltpu.SemaphoreType.DMA((2, NX)),
            pltpu.SemaphoreType.DMA((2, NX)),
            pltpu.SemaphoreType.DMA((NO,)),
            pltpu.SemaphoreType.DMA((1,)),
            pltpu.SemaphoreType.DMA((1,)),
            pltpu.SemaphoreType.DMA((1,)),
            pltpu.SemaphoreType.DMA((1,)),
            pltpu.SemaphoreType.DMA((3,)),
            pltpu.SemaphoreType.DMA((3,)),
            pltpu.SemaphoreType.REGULAR,
            pltpu.SemaphoreType.REGULAR,
        ],
        compiler_params=pltpu.CompilerParams(
            collective_id=0, has_side_effects=True, vmem_limit_bytes=48 << 20
        ),
        name="slab",
    )(dt_bias, a_log, d_skip, raw, weight, bias, dt_t, cot)


def on_device(xbc_raw, conv_weight, conv_bias, dt_raw, dt_bias, a_log, d_skip, grad_out):
    raw = xbc_raw[0]
    gx, gpre, weight_grad, bias_grad, small = run_main(
        raw, conv_weight, conv_bias[None], dt_raw[0].T, dt_bias, a_log, d_skip, grad_out[0]
    )
    return (
        gx[None], gpre.T[None], weight_grad, bias_grad[0], small[0, 0:4], small[0, 8:12],
        small[0, 16:20],
    )


def solution(mesh):
    rows = P("dp", "ctx", None)
    return jax.shard_map(
        on_device,
        mesh=mesh,
        in_specs=(rows, P(), P(), rows, P(), P(), P(), rows),
        out_specs=(rows, rows, P(), P(), P(), P(), P()),
        check_vma=False,
    )
```

```python
import functools

import jax
import jax.numpy as jnp
from jax import lax
from jax.experimental import pallas as pl
from jax.experimental.pallas import tpu as pltpu
from jax.sharding import PartitionSpec as P

H = 4
P_SIZE = 64
N = 128
K = 4
L = 256
CH = 512
INNER = H * P_SIZE
NZ = 16
NX = 4
NY = 4
NR = 32
ZR = 32
NB = 4
NO = 16
RC = N // NO
F32 = jnp.float32
BF16 = jnp.bfloat16
MESH = pl.DeviceIdType.MESH


def dot(a, b):
    return lax.dot_general(a, b, (((1,), (0,)), ((), ())), preferred_element_type=F32)


def dot_nt(a, b):
    return lax.dot_general(a, b, (((1,), (1,)), ((), ())), preferred_element_type=F32)


def dot_tn(a, b):
    return lax.dot_general(a, b, (((0,), (0,)), ((), ())), preferred_element_type=F32)


def split(a):
    hi = a.astype(BF16)
    return hi, (a - hi.astype(F32)).astype(BF16)


def split3(a):
    hi = a.astype(BF16)
    rest = a - hi.astype(F32)
    mid = rest.astype(BF16)
    return hi, mid, (rest - mid.astype(F32)).astype(BF16)


def iota(shape, dim):
    return lax.broadcasted_iota(jnp.int32, shape, dim)


def head_column(ref):
    rows = iota((8, 1), 0)
    col = jnp.zeros((8, 1), F32)
    for h in range(H):
        col = jnp.where(rows == h, ref[h], col)
    return col


def spread(cols, first):
    rows = cols.shape[0]
    low = iota((rows, 128), 1) < P_SIZE
    tiles = []
    for j in range(2):
        a = jnp.broadcast_to(cols[:, first + 2 * j : first + 2 * j + 1], (rows, 128))
        b = jnp.broadcast_to(cols[:, first + 2 * j + 1 : first + 2 * j + 2], (rows, 128))
        tiles.append(jnp.where(low, a, b))
    return jnp.concatenate(tiles, axis=1)


def head_rows(dtype):
    return (iota((8, INNER), 1) // P_SIZE == iota((8, INNER), 0)).astype(dtype)


def head_sums(x):
    sel = head_rows(F32).astype(BF16)
    hi, lo = split(x)
    return dot_nt(sel, hi) + dot_nt(sel, lo)


def main_kernel(
    dt_bias_hbm, a_log_hbm, skip_hbm, raw_hbm, w_hbm, bias_hbm, dt_hbm, cot_hbm,
    gx_ref, gpre_ref, wg_ref, bg_ref, small_ref,
    dt_bias_ref, a_log_ref, skip_ref, raw_ref, w_ref, bias_ref, dt_ref, cot_ref, in_sem,
    xp, pre_s, sig_s, xb, rows_s, cols_s, loc, dec, tw_e, up_e, st_e, ac, gbl, gcl, pair_s,
    gc_pad, abuf, dbuf, pre_p, pre_q, tot, blk, rbuf, sbuf, rfac, sfac, heads, tails, cfull, corr,
    rsend, ret, near_out, near_in, spill_out, spill_in, sums_ref, plane, line, own, totals,
    send_sem, recv_sem, fsend_sem, frecv_sem, asend_sem, arecv_sem, hsend_sem, hrecv_sem,
    hcast_sem, nsend_sem, nrecv_sem, ssend_sem, srecv_sem, rsend_sem, rrecv_sem, edge_sem,
    known_sem,
):
    place = lax.axis_index("ctx")
    dp = lax.axis_index("dp")
    z = lax.rem(place, NZ)
    x = place // NZ
    y = dp // 4
    z_hi = lax.rem(dp // 2, 2)
    core = lax.rem(dp, 2)

    def device(x_, y_, ring, core_):
        return (x_ * NZ + lax.rem(ring, NZ), y_ * 4 + (ring // NZ) * 2 + core_)

    ring = z_hi * NZ + z
    zq = z // NB
    zi = lax.rem(z, NB)
    me_o = x * NB + zi

    def remote(src, dst, send, recv, target):
        return pltpu.make_async_remote_copy(
            src_ref=src, dst_ref=dst, send_sem=send, recv_sem=recv, device_id=target,
            device_id_type=MESH,
        )

    def mate(k):
        o = lax.rem(me_o + k, NO)
        return o, ((o // NB) * NZ + zq * NB + lax.rem(o, NB), dp)

    heads[...] = jnp.zeros_like(heads)
    tails[...] = jnp.zeros_like(tails)
    barrier = pltpu.get_barrier_semaphore()
    inputs = [
        pltpu.make_async_copy(src, dst, in_sem.at[i])
        for i, (src, dst) in enumerate(
            ((raw_hbm, raw_ref), (w_hbm, w_ref), (bias_hbm, bias_ref), (dt_hbm, dt_ref),
             (cot_hbm, cot_ref), (dt_bias_hbm, dt_bias_ref), (a_log_hbm, a_log_ref),
             (skip_hbm, skip_ref))
        )
    ]
    for copy in inputs:
        copy.start()
    for step in (1, ZR - 1, NB, ZR - NB):
        pl.semaphore_signal(
            barrier, inc=1, device_id=device(x, y, lax.rem(ring + step, ZR), core),
            device_id_type=MESH,
        )

    def greet(k, _):
        pl.semaphore_signal(barrier, inc=1, device_id=mate(k)[1], device_id_type=MESH)
        return 0

    lax.fori_loop(1, NO, greet, 0)
    for k in range(1, 2 * NY):
        q = lax.rem(y * 2 + core + k, 2 * NY)
        pl.semaphore_signal(
            barrier, inc=1, device_id=device(x, q // 2, ring, lax.rem(q, 2)), device_id_type=MESH
        )
    for copy in inputs:
        copy.wait()

    xp[0:8, :] = jnp.zeros((8, CH), F32)
    xp[8 : 8 + L, :] = raw_ref[...].astype(F32)

    def activate(r, size):
        pre = bias_ref[...] + sum(
            w_ref[k : k + 1, :] * xp[5 + k + r : 5 + k + r + size, :] for k in range(K)
        )
        sig = 1.0 / (1.0 + jnp.exp(-pre))
        pre_s[r : r + size, :] = pre
        sig_s[r : r + size, :] = sig
        xb[r : r + size, :] = (pre * sig).astype(BF16)

    for r in range(0, L, 64):
        activate(r, 64)

    rate = -jnp.exp(head_column(a_log_ref))
    live = iota((8, 1), 0) < H
    rate = jnp.where(live, rate, 0.0)
    rows_s[...] = jnp.zeros_like(rows_s)
    rows_s[0:H, :] = dt_ref[...]
    dt_pre = rows_s[0:8, :] + head_column(dt_bias_ref)
    step = jnp.where(
        live, jnp.maximum(dt_pre, 0.0) + jnp.log1p(jnp.exp(-jnp.abs(dt_pre))), 0.0
    )
    upto = (iota((L, L), 0) <= iota((L, L), 1)).astype(F32).astype(BF16)
    cum = sum(dot(part, upto) for part in split3(step * rate))
    cum_last = cum[:, L - 1 : L]
    to_end = jnp.exp(cum_last - cum)
    tw = to_end * step
    up = jnp.exp(cum)
    rows_s[0:8, :] = cum
    rows_s[8:16, :] = step
    rows_s[16:24, :] = tw
    rows_s[24:32, :] = up
    cols = jnp.transpose(rows_s[...])
    cols_s[...] = cols
    tw_e[...] = spread(cols, 16)
    up_e[...] = spread(cols, 24)
    st_e[...] = spread(cols, 8)
    dec[0] = up_e[L - 1 : L, :]
    near_out[0:3, :] = xp[5 + L : 8 + L, :]

    pl.semaphore_wait(barrier, 4 + NO - 1 + 2 * NY - 1)

    def near(target):
        return remote(
            near_out.at[0:3], near_in.at[0:3], nsend_sem.at[0], nrecv_sem.at[0], (target, dp)
        )

    @pl.when(z < NZ - 1)
    def _():
        near(place + 1).start()

    def head(l, send, target):
        return remote(heads.at[l, 0:3], heads.at[l, 0:3], send, hrecv_sem.at[0, l], target)

    def last(l, send, target):
        return remote(tails.at[l, 0:3], tails.at[l, 0:3], send, hrecv_sem.at[1, l], target)

    @pl.when(z == 0)
    def _():
        heads[x, 0:3, 0:CH] = pre_s[0:3, :]
        heads[x, 0:3, CH : CH + INNER] = tw_e[0:3, :]
        heads[x, 0:3, CH + INNER :] = (cot_ref[...].astype(F32) * up_e[...])[0:3, :]

        def cast(k, _):
            o, target = mate(k)
            head(x, hcast_sem.at[k], target).start()
            return 0

        lax.fori_loop(1, NO, cast, 0)

    has_tail = jnp.logical_and(z == NZ - 1, x < NX - 1)

    @pl.when(has_tail)
    def _():
        tails[x + 1, 0:3, :] = near_out[0:3, :]

        def cast(k, _):
            o, target = mate(k)
            last(x + 1, hcast_sem.at[k], target).start()
            return 0

        lax.fori_loop(1, NO, cast, 0)

    @pl.when(z > 0)
    def _():
        near(place - 1).wait_recv()
        xp[5:8, :] = near_in[0:3, :]
        activate(0, 16)

    ready = jnp.logical_or(iota((L, INNER), 0) >= 3, z > 0)
    b_val = xb[:, INNER : INNER + N]
    c_val = xb[:, INNER + N :]
    hi, lo = split(jnp.where(ready, xb[:, :INNER].astype(F32) * tw_e[...], 0.0))
    loc[:, 0:RC, :] = (dot_tn(b_val, hi) + dot_tn(b_val, lo)).reshape(NO, RC, INNER)
    hi, lo = split(jnp.where(ready, cot_ref[...].astype(F32) * up_e[...], 0.0))
    loc[:, RC:, :] = (dot_tn(c_val, hi) + dot_tn(c_val, lo)).reshape(NO, RC, INNER)

    def to_owners(k, _):
        o, target = mate(k)
        remote(dec.at[0], dbuf.at[me_o], asend_sem.at[0], arecv_sem.at[0], target).start()
        remote(loc.at[o], abuf.at[me_o], asend_sem.at[1], arecv_sem.at[1], target).start()
        return 0

    lax.fori_loop(1, NO, to_owners, 0)
    abuf[pl.ds(me_o, 1)] = loc[pl.ds(me_o, 1)]
    dbuf[pl.ds(me_o, 1)] = dec[...]

    def from_block(buf, i):
        part = buf.at[pl.ds(0, NO - 1)]
        return remote(part, part, asend_sem.at[i], arecv_sem.at[i], mate(1)[1])

    def along_line(step):
        return (place + NB * step, dp)

    def relay_heads():
        for l in range(NX):

            @pl.when(jnp.logical_not(jnp.logical_and(z == 0, x == l)))
            def _():
                head(l, hsend_sem.at[0, l], along_line(1)).wait_recv()

            @pl.when(zq < NB - 1)
            def _():
                head(l, hsend_sem.at[0, l], along_line(1)).start()

    def relay_tails():
        for l in range(1, NX):

            @pl.when(jnp.logical_not(jnp.logical_and(z == NZ - 1, x == l - 1)))
            def _():
                last(l, hsend_sem.at[1, l], along_line(-1)).wait_recv()

            @pl.when(zq > 0)
            def _():
                last(l, hsend_sem.at[1, l], along_line(-1)).start()

    def local_terms():
        pair_s[...] = jnp.zeros_like(pair_s)
        low = iota((128, 128), 1) < P_SIZE
        for sb in range(2):
            t0 = 128 * sb
            wide = L - t0
            rs = slice(t0, t0 + 128)
            gram = dot_nt(xb[rs, INNER : INNER + N], xb[t0:, INNER + N :])
            mask = iota((128, wide), 1) >= iota((128, wide), 0)
            dgram = jnp.zeros((128, wide), F32)
            for j in range(2):
                cot_t = cot_ref[t0:, 128 * j : 128 * j + 128]
                v_t = xb[rs, 128 * j : 128 * j + 128]
                parts = []
                for i in range(2):
                    h = 2 * j + i
                    keep = low if i == 0 else jnp.logical_not(low)
                    v_h = jnp.where(keep, v_t.astype(F32), 0.0).astype(BF16)
                    gap = rows_s[h : h + 1, t0:] - cols_s[rs, h : h + 1]
                    within = jnp.exp(jnp.where(mask, gap, -1e30))
                    dmix = dot_nt(v_h, cot_t)
                    hi, lo = split(gram * within)
                    parts.append(dot(hi, cot_t) + dot(lo, cot_t))
                    dw = dmix * within * cols_s[rs, 8 + h : 9 + h]
                    dgram = dgram + dw
                    pair_s[h : h + 1, t0:] += jnp.sum(dw * gram, axis=0, keepdims=True)
                ac[rs, 128 * j : 128 * j + 128] = jnp.where(low, parts[0], parts[1])
            hi, lo = split(dgram)
            c_t = xb[t0:, INNER + N :]
            b_s = xb[rs, INNER : INNER + N]
            gbl[rs, :] = dot(hi, c_t) + dot(lo, c_t)
            from_here = dot_tn(hi, b_s) + dot_tn(lo, b_s)
            if sb == 0:
                gcl[...] = from_here
            else:
                gcl[t0:, :] += from_here

    left = zq < NB // 2

    @pl.when(left)
    def _():
        relay_heads()

    @pl.when(zq > 0)
    def _():
        relay_tails()

    @pl.when(zq == NB // 2)
    def _():
        relay_heads()

    from_block(dbuf, 0).wait_recv()
    from_block(abuf, 1).wait_recv()
    for l in range(NX):
        p = abuf[NB * l, 0:RC, :]
        q = abuf[NB * l + NB - 1, RC:, :]
        for i in range(1, NB):
            pre_p[NB * l + i] = p
            p = dbuf[NB * l + i] * p + abuf[NB * l + i, 0:RC, :]
            j = NB - 1 - i
            pre_q[NB * l + j] = q
            q = dbuf[NB * l + j] * q + abuf[NB * l + j, RC:, :]
        tot[0, l] = p
        tot[1, l] = q
        blk[l] = dbuf[NB * l] * dbuf[NB * l + 1] * dbuf[NB * l + 2] * dbuf[NB * l + 3]

    @pl.when(zq == 0)
    def _():
        rbuf[0] = jnp.zeros((NX, 2 * RC, INNER), F32)
        rfac[0] = jnp.ones((8, INNER), F32)

    @pl.when(zq == NB - 1)
    def _():
        rbuf[1] = jnp.zeros((NX, 2 * RC, INNER), F32)
        rfac[1] = jnp.ones((8, INNER), F32)

    first = jnp.where(left, 0, 1)

    def hop(way, l):
        return remote(
            sbuf.at[way, l], rbuf.at[way, l], send_sem.at[way, l], recv_sem.at[way, l],
            along_line(1 - 2 * way),
        )

    def factor_hop(way):
        return remote(
            sfac.at[way], rfac.at[way], fsend_sem.at[way], frecv_sem.at[way],
            along_line(1 - 2 * way),
        )

    def has_in(way):
        return jnp.where(way == 0, zq, NB - 1 - zq) > 0

    def has_out(way):
        return jnp.where(way == 0, NB - 1 - zq, zq) > 0

    def head_weights(l):
        v0 = jnp.where(zq == 0, 0.0, rfac[0, 4 + l : 5 + l, :])
        v1 = jnp.where(zq == 0, 1.0, v0 * dbuf[NB * l])
        v2 = v1 * dbuf[NB * l + 1]
        v3 = v2 * dbuf[NB * l + 2]
        return v0, v1, v2, v3, v3 * dbuf[NB * l + 3]

    def relay(way):
        @pl.when(has_in(way))
        def _():
            factor_hop(way).wait_recv()

        @pl.when(has_out(way))
        def _():
            for l in range(NX):
                sfac[way, l : l + 1, :] = rfac[way, l : l + 1, :] * blk[l]
                sfac[way, 4 + l : 5 + l, :] = (
                    head_weights(l)[4] if way == 0 else jnp.zeros((1, INNER), F32)
                )
            factor_hop(way).start()

        for l in range(NX):

            @pl.when(has_in(way))
            def _():
                hop(way, l).wait_recv()

            @pl.when(has_out(way))
            def _():
                sbuf[way, l, 0:RC, :] = blk[l] * rbuf[way, l, 0:RC, :] + tot[way, l]
                sbuf[way, l, RC:, :] = (
                    rbuf[way, l, RC:, :] + rfac[way, l : l + 1, :] * tot[1 - way, l]
                )
                hop(way, l).start()

    @pl.when(left)
    def _():
        relay(0)

    @pl.when(jnp.logical_not(left))
    def _():
        relay(1)

    @pl.when(zq == 0)
    def _():
        relay_tails()

    @pl.when(zq == NB - 1)
    def _():
        relay_heads()

    mine_rows = pl.ds(pl.multiple_of(me_o * RC, RC), RC)
    for l in range(NX):
        pre = heads[l, :, 0:CH] + sum(w_ref[k : k + 1, :] * tails[l, k : k + 8, :] for k in range(3))
        act = jnp.where(iota((8, CH), 0) < 3, pre / (1.0 + jnp.exp(-pre)), 0.0).astype(BF16)
        hi, lo = split(act[:, :INNER].astype(F32) * heads[l, :, CH : CH + INNER])
        b_row = act[:, INNER : INNER + N]
        c_row = act[:, INNER + N :]
        cfull[...] = dot_tn(b_row, hi) + dot_tn(b_row, lo)
        corr[0, l] = cfull[mine_rows, :]
        hi, lo = split(heads[l, :, CH + INNER :])
        cfull[...] = dot_tn(c_row, hi) + dot_tn(c_row, lo)
        corr[1, l] = cfull[mine_rows, :]

    @pl.when(left)
    def _():
        relay(1)

    @pl.when(jnp.logical_not(left))
    def _():
        relay(0)

    def line_terms(l):
        f = rfac[0, l : l + 1, :]
        e = rfac[1, l : l + 1, :]
        return f, e, f * e * blk[l]

    def give_back(l, i, entering, way):
        rsend[NB * l + i, RC * way : RC * way + RC, :] = entering

    carry = jnp.zeros((RC, INNER), F32)
    for l in range(NX):
        f, e, whole = line_terms(l)
        weights = head_weights(l)
        at = rbuf[0, l, 0:RC, :] + f * carry
        for i in range(NB):
            here = at + weights[i] * corr[0, l]
            if i:
                here = here + pre_p[NB * l + i]
            give_back(l, i, here, 0)
            at = at * dbuf[NB * l + i]
        total = (
            e * (blk[l] * rbuf[0, l, 0:RC, :] + tot[0, l] + weights[4] * corr[0, l])
            + rbuf[1, l, RC:, :]
        )
        carry = whole * carry + total
    carry = jnp.zeros((RC, INNER), F32)
    for l in range(NX - 1, -1, -1):
        f, e, whole = line_terms(l)
        at = rbuf[1, l, 0:RC, :] + e * carry
        for i in range(NB - 1, -1, -1):
            here = at
            if i < NB - 1:
                here = here + pre_q[NB * l + i]
            give_back(l, i, here, 1)
            at = at * dbuf[NB * l + i]
        total = (
            f * (blk[l] * rbuf[1, l, 0:RC, :] + tot[1, l]) + rbuf[0, l, RC:, :] + corr[1, l]
        )
        carry = whole * carry + total

    def back(k, _):
        o, target = mate(k)
        remote(rsend.at[o], ret.at[me_o], asend_sem.at[2], arecv_sem.at[2], target).start()
        return 0

    lax.fori_loop(1, NO, back, 0)
    ret[pl.ds(me_o, 1)] = rsend[pl.ds(me_o, 1)]

    @pl.when(z == 0)
    def _():
        xp[5:8, :] = tails[x, 0:3, :]
        activate(0, 16)

    local_terms()

    @pl.when(zq == 0)
    def _():
        pl.semaphore_signal(
            edge_sem, inc=1, device_id=device(x, y, lax.rem(ring + ZR - NB, ZR), core),
            device_id_type=MESH,
        )
        pl.semaphore_wait(edge_sem, 1)
        pl.semaphore_signal(known_sem, inc=1, device_id=along_line(1), device_id_type=MESH)

    @pl.when(zq == NB - 1)
    def _():
        pl.semaphore_signal(
            edge_sem, inc=1, device_id=device(x, y, lax.rem(ring + NB, ZR), core),
            device_id_type=MESH,
        )
        pl.semaphore_wait(edge_sem, 1)
        pl.semaphore_signal(known_sem, inc=1, device_id=along_line(-1), device_id_type=MESH)

    from_block(ret, 2).wait_recv()
    s_in = ret[:, 0:RC, :].reshape(N, INNER)
    g_after = ret[:, RC:, :].reshape(N, INNER)

    b_val = xb[:, INNER : INNER + N]
    c_val = xb[:, INNER + N :]
    s_hi, s_lo = split(s_in)
    g_hi, g_lo = split(g_after)
    state_back = dot(b_val, g_hi) + dot(b_val, g_lo)
    state_proj = dot(c_val, s_hi) + dot(c_val, s_lo)
    cot = cot_ref[...].astype(F32)
    vals = xb[:, :INNER].astype(F32)
    scaled = cot * up_e[...]
    hi, lo = split(scaled)
    grad_c = gcl[...] + dot_nt(hi, s_hi) + dot_nt(hi, s_lo) + dot_nt(lo, s_hi)
    hi, lo = split(vals * tw_e[...])
    grad_b = gbl[...] + dot_nt(hi, g_hi) + dot_nt(hi, g_lo) + dot_nt(lo, g_hi)
    local_step = head_sums(vals * ac[...])
    tail_grad = head_sums(vals * state_back)
    proj_term = head_sums(scaled * state_proj)
    skip_lanes = spread(jnp.broadcast_to(0.0, (8, 128)) + sum(
        jnp.where(iota((8, 128), 1) == h, skip_ref[h], 0.0) for h in range(H)
    ), 0)[0:1, :]
    grad_vals = st_e[...] * ac[...] + skip_lanes * cot + tw_e[...] * state_back

    step = rows_s[8:16, :]
    tw = rows_s[16:24, :]
    cum = rows_s[0:8, :]
    cum_last = cum[:, L - 1 : L]
    sel = head_rows(F32)
    skip_sum = jnp.sum(sel * jnp.sum(cot * vals, axis=0, keepdims=True), axis=1, keepdims=True)
    both = jnp.sum(
        sel * jnp.sum(s_in * g_after, axis=0, keepdims=True), axis=1, keepdims=True
    )
    tail_term = tail_grad * tw
    extra = jnp.sum(tail_term, axis=1, keepdims=True) + jnp.exp(cum_last) * both
    grad_cum = pair_s[...] - step * local_step + proj_term - tail_term
    since = (iota((L, L), 0) >= iota((L, L), 1)).astype(F32).astype(BF16)
    grad_log = sum(dot(part, since) for part in split3(grad_cum)) + extra
    rows_s[32 : 32 + H, :] = dt_ref[...]
    dt_pre = rows_s[32:40, :] + head_column(dt_bias_ref)
    rate = -jnp.exp(head_column(a_log_ref))
    grad_step = local_step + tail_grad * jnp.exp(cum_last - cum) + rate * grad_log
    grad_pre = grad_step / (1.0 + jnp.exp(-dt_pre))
    gpre_ref[...] = grad_pre[0:H, :]
    alog_sum = rate * jnp.sum(grad_log * step, axis=1, keepdims=True)
    bias_sum = jnp.sum(grad_pre, axis=1, keepdims=True)

    gc_pad[0:8, :] = jnp.zeros((8, CH), F32)
    gc_pad[8 + L : 16 + L, :] = jnp.zeros((8, CH), F32)
    for lanes, value in (
        (slice(0, INNER), grad_vals),
        (slice(INNER, INNER + N), grad_b),
        (slice(INNER + N, CH), grad_c),
    ):
        low_value = value.astype(BF16).astype(F32)
        sig = sig_s[:, lanes]
        gc_pad[8 : 8 + L, lanes] = low_value * sig * (1.0 + pre_s[:, lanes] * (1.0 - sig))

    spill_out[...] = sum(w_ref[k : k + 1, :] * gc_pad[3 - k : 11 - k, :] for k in range(K))

    def spill(target):
        return remote(spill_out, spill_in, ssend_sem.at[0], srecv_sem.at[0], (target, dp))

    @pl.when(place > 0)
    def _():
        spill(place - 1).start()

    sums_ref[...] = jnp.zeros_like(sums_ref)
    for k in range(K + 1):
        term = gc_pad[8 : 8 + L, :]
        if k < K:
            term = term * xp[5 + k : 5 + k + L, :]
        total = jnp.sum(term, axis=0, keepdims=True)
        for j in range(4):
            sums_ref[4 * k + j] = total[:, 128 * j : 128 * j + 128]
    lane = iota((8, 128), 1)
    row = iota((8, 128), 0)
    small = (
        jnp.where(lane == row, bias_sum, 0.0)
        + jnp.where(lane == row + 8, alog_sum, 0.0)
        + jnp.where(lane == row + 16, skip_sum, 0.0)
    )
    small = jnp.where(row < H, small, 0.0)
    sums_ref[20] = jnp.sum(small, axis=0, keepdims=True)

    me = (x * NY + y) * 2 + core

    def in_plane(k):
        r = lax.rem(me + k, NR)
        return r, device(r // 8, lax.rem(r // 2, NY), ring, lax.rem(r, 2))

    def all_of(buf, stage):
        part = buf.at[pl.ds(0, NR - 1)]
        return remote(part, part, rsend_sem.at[stage], rrecv_sem.at[stage], in_plane(1)[1])

    def scatter(k, _):
        r, target = in_plane(k)
        remote(sums_ref.at[r], plane.at[me], rsend_sem.at[0], rrecv_sem.at[0], target).start()
        return 0

    lax.fori_loop(1, NR, scatter, 0)
    plane[pl.ds(me, 1)] = sums_ref[pl.ds(me, 1)]
    for r in range(0, L, 64):
        rows = sum(
            w_ref[k : k + 1, :] * gc_pad[11 - k + r : 11 - k + r + 64, :] for k in range(K)
        )
        gx_ref[r : r + 64, :] = rows.astype(BF16)
        if r + 64 == L:
            tail = rows[48:64, :]

    @pl.when(jnp.logical_and(zq > 0, zq < NB - 1))
    def _():
        pl.semaphore_wait(known_sem, 1)

    all_of(plane, 0).wait_recv()
    mine = jnp.sum(plane[...], axis=0, keepdims=True)
    own[0:1] = mine

    def along(k, _):
        q = lax.rem(ring + k, ZR)
        remote(
            own.at[0], line.at[ring], rsend_sem.at[1], rrecv_sem.at[1], device(x, y, q, core)
        ).start()
        return 0

    lax.fori_loop(1, ZR, along, 0)
    line[pl.ds(ring, 1)] = mine

    @pl.when(place < NX * NZ - 1)
    def _():
        spill(place + 1).wait_recv()

    @pl.when(place == NX * NZ - 1)
    def _():
        spill_in[...] = jnp.zeros_like(spill_in)

    gx_ref[L - 16 : L, :] = jnp.concatenate(
        [tail[0:8, :], tail[8:16, :] + spill_in[...]], axis=0
    ).astype(BF16)

    all_of(line, 1).wait_recv()
    total = jnp.sum(line[...], axis=0, keepdims=True)
    own[1:2] = total
    totals[pl.ds(me, 1)] = total

    def spread_out(k, _):
        remote(
            own.at[1], totals.at[me], rsend_sem.at[2], rrecv_sem.at[2], in_plane(k)[1]
        ).start()
        return 0

    lax.fori_loop(1, NR, spread_out, 0)
    for way in range(2):

        @pl.when(has_out(way))
        def _():
            factor_hop(way).wait_send()
            for l in range(NX):
                hop(way, l).wait_send()

    @pl.when(zq < NB - 1)
    def _():
        for l in range(NX):
            head(l, hsend_sem.at[0, l], along_line(1)).wait_send()

    @pl.when(zq > 0)
    def _():
        for l in range(1, NX):
            last(l, hsend_sem.at[1, l], along_line(-1)).wait_send()

    @pl.when(z == 0)
    def _():
        for k in range(1, NO):
            head(0, hcast_sem.at[k], along_line(1)).wait_send()

    @pl.when(has_tail)
    def _():
        for k in range(1, NO):
            last(0, hcast_sem.at[k], along_line(-1)).wait_send()

    @pl.when(z < NZ - 1)
    def _():
        near(place + 1).wait_send()

    for i, buf in enumerate((dbuf, abuf, ret)):
        from_block(buf, i).wait_send()

    @pl.when(place > 0)
    def _():
        spill(place - 1).wait_send()

    for stage, buf in enumerate((plane, line)):
        all_of(buf, stage).wait_send()
    all_of(totals, 2).wait_recv()
    for k in range(K):
        for j in range(4):
            wg_ref[k : k + 1, 128 * j : 128 * j + 128] = totals[4 * k + j]
    for j in range(4):
        bg_ref[0:1, 128 * j : 128 * j + 128] = totals[16 + j]
    small_ref[...] = totals[20]
    all_of(totals, 2).wait_send()


def run_main(raw, weight, bias, dt_t, dt_bias, a_log, d_skip, cot):
    vmem = pl.BlockSpec(memory_space=pltpu.VMEM)
    hbm = pl.BlockSpec(memory_space=pltpu.HBM)
    return pl.pallas_call(
        main_kernel,
        out_shape=(
            jax.ShapeDtypeStruct((L, CH), BF16),
            jax.ShapeDtypeStruct((H, L), F32),
            jax.ShapeDtypeStruct((K, CH), F32),
            jax.ShapeDtypeStruct((1, CH), F32),
            jax.ShapeDtypeStruct((1, 128), F32),
        ),
        in_specs=[hbm] * 8,
        out_specs=(vmem,) * 5,
        scratch_shapes=[
            pltpu.SMEM((H,), F32),
            pltpu.SMEM((H,), F32),
            pltpu.SMEM((H,), F32),
            pltpu.VMEM((L, CH), BF16),
            pltpu.VMEM((K, CH), F32),
            pltpu.VMEM((1, CH), F32),
            pltpu.VMEM((H, L), F32),
            pltpu.VMEM((L, INNER), BF16),
            pltpu.SemaphoreType.DMA((8,)),
            pltpu.VMEM((8 + L, CH), F32),
            pltpu.VMEM((L, CH), F32),
            pltpu.VMEM((L, CH), F32),
            pltpu.VMEM((L, CH), BF16),
            pltpu.VMEM((128, L), F32),
            pltpu.VMEM((L, 128), F32),
            pltpu.VMEM((NO, 2 * RC, INNER), F32),
            pltpu.VMEM((1, 1, INNER), F32),
            pltpu.VMEM((L, INNER), F32),
            pltpu.VMEM((L, INNER), F32),
            pltpu.VMEM((L, INNER), F32),
            pltpu.VMEM((L, INNER), F32),
            pltpu.VMEM((L, N), F32),
            pltpu.VMEM((L, N), F32),
            pltpu.VMEM((8, L), F32),
            pltpu.VMEM((16 + L, CH), F32),
            pltpu.VMEM((NO, 2 * RC, INNER), F32),
            pltpu.VMEM((NO, 1, INNER), F32),
            pltpu.VMEM((NO, RC, INNER), F32),
            pltpu.VMEM((NO, RC, INNER), F32),
            pltpu.VMEM((2, NX, RC, INNER), F32),
            pltpu.VMEM((NX, 1, INNER), F32),
            pltpu.VMEM((2, NX, 2 * RC, INNER), F32),
            pltpu.VMEM((2, NX, 2 * RC, INNER), F32),
            pltpu.VMEM((2, 8, INNER), F32),
            pltpu.VMEM((2, 8, INNER), F32),
            pltpu.VMEM((NX, 8, CH + 2 * INNER), F32),
            pltpu.VMEM((NX, 16, CH), F32),
            pltpu.VMEM((N, INNER), F32),
            pltpu.VMEM((2, NX, RC, INNER), F32),
            pltpu.VMEM((NO, 2 * RC, INNER), F32),
            pltpu.VMEM((NO, 2 * RC, INNER), F32),
            pltpu.VMEM((8, CH), F32),
            pltpu.VMEM((8, CH), F32),
            pltpu.VMEM((8, CH), F32),
            pltpu.VMEM((8, CH), F32),
            pltpu.VMEM((NR, 1, 128), F32),
            pltpu.VMEM((NR, 1, 128), F32),
            pltpu.VMEM((ZR, 1, 128), F32),
            pltpu.VMEM((2, 1, 128), F32),
            pltpu.VMEM((NR, 1, 128), F32),
            pltpu.SemaphoreType.DMA((2, NX)),
            pltpu.SemaphoreType.DMA((2, NX)),
            pltpu.SemaphoreType.DMA((2,)),
            pltpu.SemaphoreType.DMA((2,)),
            pltpu.SemaphoreType.DMA((3,)),
            pltpu.SemaphoreType.DMA((3,)),
            pltpu.SemaphoreType.DMA((2, NX)),
            pltpu.SemaphoreType.DMA((2, NX)),
            pltpu.SemaphoreType.DMA((NO,)),
            pltpu.SemaphoreType.DMA((1,)),
            pltpu.SemaphoreType.DMA((1,)),
            pltpu.SemaphoreType.DMA((1,)),
            pltpu.SemaphoreType.DMA((1,)),
            pltpu.SemaphoreType.DMA((3,)),
            pltpu.SemaphoreType.DMA((3,)),
            pltpu.SemaphoreType.REGULAR,
            pltpu.SemaphoreType.REGULAR,
        ],
        compiler_params=pltpu.CompilerParams(
            collective_id=0, has_side_effects=True, vmem_limit_bytes=67043328
        ),
        name="slab",
    )(dt_bias, a_log, d_skip, raw, weight, bias, dt_t, cot)


def finish_kernel(gx, gpre, wg, bg, small, gx_o, gpre_o, wg_o, bg_o, db_o, da_o, ds_o):
    gx_o[...] = gx[...]
    gpre_o[...] = gpre[...]
    wg_o[...] = wg[...]
    bg_o[...] = bg[...]
    db_o[...] = small[0:1, 0:4]
    da_o[...] = small[0:1, 8:12]
    ds_o[...] = small[0:1, 16:20]


def finish(*parts):
    vmem = pl.BlockSpec(memory_space=pltpu.VMEM)
    head = jax.ShapeDtypeStruct((1, H), F32)
    return pl.pallas_call(
        finish_kernel,
        out_shape=tuple(jax.ShapeDtypeStruct(p.shape, p.dtype) for p in parts[:4]) + (head,) * 3,
        in_specs=[vmem] * 5,
        out_specs=(vmem,) * 7,
        compiler_params=pltpu.CompilerParams(vmem_limit_bytes=67043328),
        name="finish",
    )(*parts)


def on_device(xbc_raw, conv_weight, conv_bias, dt_raw, dt_bias, a_log, d_skip, grad_out):
    gx, gpre, weight_grad, bias_grad, bias, decay, skip = finish(*run_main(
        xbc_raw[0], conv_weight, conv_bias[None], dt_raw[0].T, dt_bias, a_log, d_skip, grad_out[0]
    ))
    return (
        gx[None], gpre.T[None], weight_grad, bias_grad[0], bias[0], decay[0], skip[0],
    )


def solution(mesh):
    rows = P("dp", "ctx", None)
    return jax.shard_map(
        on_device,
        mesh=mesh,
        in_specs=(rows, P(), P(), rows, P(), P(), P(), rows),
        out_specs=(rows, rows, P(), P(), P(), P(), P()),
        check_vma=False,
    )
```

```python
import functools

import jax
import jax.numpy as jnp
from jax import lax
from jax.experimental import pallas as pl
from jax.experimental.pallas import tpu as pltpu
from jax.sharding import PartitionSpec as P

H = 4
P_SIZE = 64
N = 128
K = 4
L = 256
CH = 512
INNER = H * P_SIZE
NZ = 16
NX = 4
NY = 4
NR = 32
ZR = 32
NB = 4
NO = 16
RC = N // NO
F32 = jnp.float32
BF16 = jnp.bfloat16
MESH = pl.DeviceIdType.MESH


def dot(a, b):
    return lax.dot_general(a, b, (((1,), (0,)), ((), ())), preferred_element_type=F32)


def dot_nt(a, b):
    return lax.dot_general(a, b, (((1,), (1,)), ((), ())), preferred_element_type=F32)


def dot_tn(a, b):
    return lax.dot_general(a, b, (((0,), (0,)), ((), ())), preferred_element_type=F32)


def split(a):
    hi = a.astype(BF16)
    return hi, (a - hi.astype(F32)).astype(BF16)


def split3(a):
    hi = a.astype(BF16)
    rest = a - hi.astype(F32)
    mid = rest.astype(BF16)
    return hi, mid, (rest - mid.astype(F32)).astype(BF16)


def iota(shape, dim):
    return lax.broadcasted_iota(jnp.int32, shape, dim)


def head_column(ref):
    rows = iota((8, 1), 0)
    col = jnp.zeros((8, 1), F32)
    for h in range(H):
        col = jnp.where(rows == h, ref[h], col)
    return col


def spread(cols, first):
    rows = cols.shape[0]
    low = iota((rows, 128), 1) < P_SIZE
    tiles = []
    for j in range(2):
        a = jnp.broadcast_to(cols[:, first + 2 * j : first + 2 * j + 1], (rows, 128))
        b = jnp.broadcast_to(cols[:, first + 2 * j + 1 : first + 2 * j + 2], (rows, 128))
        tiles.append(jnp.where(low, a, b))
    return jnp.concatenate(tiles, axis=1)


def head_rows(dtype):
    return (iota((8, INNER), 1) // P_SIZE == iota((8, INNER), 0)).astype(dtype)


def head_sums(x):
    sel = head_rows(F32).astype(BF16)
    hi, lo = split(x)
    return dot_nt(sel, hi) + dot_nt(sel, lo)


def main_kernel(
    dt_bias_hbm, a_log_hbm, skip_hbm, raw_hbm, w_hbm, bias_hbm, dt_hbm, cot_hbm,
    gx_ref, gpre_ref, wg_ref, bg_ref, small_ref,
    dt_bias_ref, a_log_ref, skip_ref, raw_ref, w_ref, bias_ref, dt_ref, cot_ref, in_sem,
    xp, pre_s, sig_s, xb, rows_s, cols_s, loc, dec, tw_e, up_e, st_e, ac, gbl, gcl, pair_s,
    gc_pad, abuf, dbuf, pre_p, pre_q, tot, blk, rbuf, sbuf, rfac, sfac, heads, tails, cfull, corr,
    rsend, ret, near_out, near_in, spill_out, spill_in, sums_ref, plane, line, own, totals,
    send_sem, recv_sem, fsend_sem, frecv_sem, asend_sem, arecv_sem, hsend_sem, hrecv_sem,
    hcast_sem, nsend_sem, nrecv_sem, ssend_sem, srecv_sem, rsend_sem, rrecv_sem, edge_sem,
    known_sem,
):
    place = lax.axis_index("ctx")
    dp = lax.axis_index("dp")
    z = lax.rem(place, NZ)
    x = place // NZ
    y = dp // 4
    z_hi = lax.rem(dp // 2, 2)
    core = lax.rem(dp, 2)

    def device(x_, y_, ring, core_):
        return (x_ * NZ + lax.rem(ring, NZ), y_ * 4 + (ring // NZ) * 2 + core_)

    ring = z_hi * NZ + z
    zq = z // NB
    zi = lax.rem(z, NB)
    me_o = x * NB + zi

    def remote(src, dst, send, recv, target):
        return pltpu.make_async_remote_copy(
            src_ref=src, dst_ref=dst, send_sem=send, recv_sem=recv, device_id=target,
            device_id_type=MESH,
        )

    def mate(k):
        o = lax.rem(me_o + k, NO)
        return o, ((o // NB) * NZ + zq * NB + lax.rem(o, NB), dp)

    heads[...] = jnp.zeros_like(heads)
    tails[...] = jnp.zeros_like(tails)
    barrier = pltpu.get_barrier_semaphore()
    inputs = [
        pltpu.make_async_copy(src, dst, in_sem.at[i])
        for i, (src, dst) in enumerate(
            ((raw_hbm, raw_ref), (w_hbm, w_ref), (bias_hbm, bias_ref), (dt_hbm, dt_ref),
             (cot_hbm, cot_ref), (dt_bias_hbm, dt_bias_ref), (a_log_hbm, a_log_ref),
             (skip_hbm, skip_ref))
        )
    ]
    for copy in inputs:
        copy.start()
    for step in (1, ZR - 1, NB, ZR - NB):
        pl.semaphore_signal(
            barrier, inc=1, device_id=device(x, y, lax.rem(ring + step, ZR), core),
            device_id_type=MESH,
        )

    def greet(k, _):
        pl.semaphore_signal(barrier, inc=1, device_id=mate(k)[1], device_id_type=MESH)
        return 0

    lax.fori_loop(1, NO, greet, 0)
    for k in range(1, 2 * NY):
        q = lax.rem(y * 2 + core + k, 2 * NY)
        pl.semaphore_signal(
            barrier, inc=1, device_id=device(x, q // 2, ring, lax.rem(q, 2)), device_id_type=MESH
        )
    for copy in inputs:
        copy.wait()

    xp[0:8, :] = jnp.zeros((8, CH), F32)
    xp[8 : 8 + L, :] = raw_ref[...].astype(F32)

    def activate(r, size):
        pre = bias_ref[...] + sum(
            w_ref[k : k + 1, :] * xp[5 + k + r : 5 + k + r + size, :] for k in range(K)
        )
        sig = 1.0 / (1.0 + jnp.exp(-pre))
        pre_s[r : r + size, :] = pre
        sig_s[r : r + size, :] = sig
        xb[r : r + size, :] = (pre * sig).astype(BF16)

    for r in range(0, L, 64):
        activate(r, 64)

    rate = -jnp.exp(head_column(a_log_ref))
    live = iota((8, 1), 0) < H
    rate = jnp.where(live, rate, 0.0)
    rows_s[...] = jnp.zeros_like(rows_s)
    rows_s[0:H, :] = dt_ref[...]
    dt_pre = rows_s[0:8, :] + head_column(dt_bias_ref)
    step = jnp.where(
        live, jnp.maximum(dt_pre, 0.0) + jnp.log1p(jnp.exp(-jnp.abs(dt_pre))), 0.0
    )
    upto = (iota((L, L), 0) <= iota((L, L), 1)).astype(F32).astype(BF16)
    cum = sum(dot(part, upto) for part in split3(step * rate))
    cum_last = cum[:, L - 1 : L]
    to_end = jnp.exp(cum_last - cum)
    tw = to_end * step
    up = jnp.exp(cum)
    rows_s[0:8, :] = cum
    rows_s[8:16, :] = step
    rows_s[16:24, :] = tw
    rows_s[24:32, :] = up
    cols = jnp.transpose(rows_s[...])
    cols_s[...] = cols
    tw_e[...] = spread(cols, 16)
    up_e[...] = spread(cols, 24)
    st_e[...] = spread(cols, 8)
    dec[0] = up_e[L - 1 : L, :]
    near_out[0:3, :] = xp[5 + L : 8 + L, :]

    pl.semaphore_wait(barrier, 4 + NO - 1 + 2 * NY - 1)

    def near(target):
        return remote(
            near_out.at[0:3], near_in.at[0:3], nsend_sem.at[0], nrecv_sem.at[0], (target, dp)
        )

    @pl.when(z < NZ - 1)
    def _():
        near(place + 1).start()

    def head(l, send, target):
        return remote(heads.at[l, 0:3], heads.at[l, 0:3], send, hrecv_sem.at[0, l], target)

    def last(l, send, target):
        return remote(tails.at[l, 0:3], tails.at[l, 0:3], send, hrecv_sem.at[1, l], target)

    @pl.when(z == 0)
    def _():
        heads[x, 0:3, 0:CH] = pre_s[0:3, :]
        heads[x, 0:3, CH : CH + INNER] = tw_e[0:3, :]
        heads[x, 0:3, CH + INNER :] = (cot_ref[...].astype(F32) * up_e[...])[0:3, :]

        def cast(k, _):
            o, target = mate(k)
            head(x, hcast_sem.at[k], target).start()
            return 0

        lax.fori_loop(1, NO, cast, 0)

    has_tail = jnp.logical_and(z == NZ - 1, x < NX - 1)

    @pl.when(has_tail)
    def _():
        tails[x + 1, 0:3, :] = near_out[0:3, :]

        def cast(k, _):
            o, target = mate(k)
            last(x + 1, hcast_sem.at[k], target).start()
            return 0

        lax.fori_loop(1, NO, cast, 0)

    @pl.when(z > 0)
    def _():
        near(place - 1).wait_recv()
        xp[5:8, :] = near_in[0:3, :]
        activate(0, 16)

    ready = jnp.logical_or(iota((L, INNER), 0) >= 3, z > 0)
    b_val = xb[:, INNER : INNER + N]
    c_val = xb[:, INNER + N :]
    hi, lo = split(jnp.where(ready, xb[:, :INNER].astype(F32) * tw_e[...], 0.0))
    loc[:, 0:RC, :] = (dot_tn(b_val, hi) + dot_tn(b_val, lo)).reshape(NO, RC, INNER)
    hi, lo = split(jnp.where(ready, cot_ref[...].astype(F32) * up_e[...], 0.0))
    loc[:, RC:, :] = (dot_tn(c_val, hi) + dot_tn(c_val, lo)).reshape(NO, RC, INNER)

    def to_owners(k, _):
        o, target = mate(k)
        remote(dec.at[0], dbuf.at[me_o], asend_sem.at[0], arecv_sem.at[0], target).start()
        remote(loc.at[o], abuf.at[me_o], asend_sem.at[1], arecv_sem.at[1], target).start()
        return 0

    lax.fori_loop(1, NO, to_owners, 0)
    abuf[pl.ds(me_o, 1)] = loc[pl.ds(me_o, 1)]
    dbuf[pl.ds(me_o, 1)] = dec[...]

    def from_block(buf, i):
        part = buf.at[pl.ds(0, NO - 1)]
        return remote(part, part, asend_sem.at[i], arecv_sem.at[i], mate(1)[1])

    def along_line(step):
        return (place + NB * step, dp)

    def relay_heads():
        for l in range(NX):

            @pl.when(jnp.logical_not(jnp.logical_and(z == 0, x == l)))
            def _():
                head(l, hsend_sem.at[0, l], along_line(1)).wait_recv()

            @pl.when(zq < NB - 1)
            def _():
                head(l, hsend_sem.at[0, l], along_line(1)).start()

    def relay_tails():
        for l in range(1, NX):

            @pl.when(jnp.logical_not(jnp.logical_and(z == NZ - 1, x == l - 1)))
            def _():
                last(l, hsend_sem.at[1, l], along_line(-1)).wait_recv()

            @pl.when(zq > 0)
            def _():
                last(l, hsend_sem.at[1, l], along_line(-1)).start()

    def local_terms():
        pair_s[...] = jnp.zeros_like(pair_s)
        low = iota((128, 128), 1) < P_SIZE
        for sb in range(2):
            t0 = 128 * sb
            wide = L - t0
            rs = slice(t0, t0 + 128)
            gram = dot_nt(xb[rs, INNER : INNER + N], xb[t0:, INNER + N :])
            mask = iota((128, wide), 1) >= iota((128, wide), 0)
            dgram = jnp.zeros((128, wide), F32)
            for j in range(2):
                cot_t = cot_ref[t0:, 128 * j : 128 * j + 128]
                v_t = xb[rs, 128 * j : 128 * j + 128]
                parts = []
                for i in range(2):
                    h = 2 * j + i
                    keep = low if i == 0 else jnp.logical_not(low)
                    v_h = jnp.where(keep, v_t.astype(F32), 0.0).astype(BF16)
                    gap = rows_s[h : h + 1, t0:] - cols_s[rs, h : h + 1]
                    within = jnp.exp(jnp.where(mask, gap, -1e30))
                    dmix = dot_nt(v_h, cot_t)
                    hi, lo = split(gram * within)
                    parts.append(dot(hi, cot_t) + dot(lo, cot_t))
                    dw = dmix * within * cols_s[rs, 8 + h : 9 + h]
                    dgram = dgram + dw
                    pair_s[h : h + 1, t0:] += jnp.sum(dw * gram, axis=0, keepdims=True)
                ac[rs, 128 * j : 128 * j + 128] = jnp.where(low, parts[0], parts[1])
            hi, lo = split(dgram)
            c_t = xb[t0:, INNER + N :]
            b_s = xb[rs, INNER : INNER + N]
            gbl[rs, :] = dot(hi, c_t) + dot(lo, c_t)
            from_here = dot_tn(hi, b_s) + dot_tn(lo, b_s)
            if sb == 0:
                gcl[...] = from_here
            else:
                gcl[t0:, :] += from_here

    left = zq < NB // 2

    @pl.when(left)
    def _():
        relay_heads()

    @pl.when(zq > 0)
    def _():
        relay_tails()

    @pl.when(zq == NB // 2)
    def _():
        relay_heads()

    from_block(dbuf, 0).wait_recv()
    from_block(abuf, 1).wait_recv()
    for l in range(NX):
        p = abuf[NB * l, 0:RC, :]
        q = abuf[NB * l + NB - 1, RC:, :]
        for i in range(1, NB):
            pre_p[NB * l + i] = p
            p = dbuf[NB * l + i] * p + abuf[NB * l + i, 0:RC, :]
            j = NB - 1 - i
            pre_q[NB * l + j] = q
            q = dbuf[NB * l + j] * q + abuf[NB * l + j, RC:, :]
        tot[0, l] = p
        tot[1, l] = q
        blk[l] = dbuf[NB * l] * dbuf[NB * l + 1] * dbuf[NB * l + 2] * dbuf[NB * l + 3]

    @pl.when(zq == 0)
    def _():
        rbuf[0] = jnp.zeros((NX, 2 * RC, INNER), F32)
        rfac[0] = jnp.ones((8, INNER), F32)

    @pl.when(zq == NB - 1)
    def _():
        rbuf[1] = jnp.zeros((NX, 2 * RC, INNER), F32)
        rfac[1] = jnp.ones((8, INNER), F32)

    first = jnp.where(left, 0, 1)

    def hop(way, l):
        rows = slice(0, RC if l == (0, NX - 1)[way] else 2 * RC)
        return remote(
            sbuf.at[way, l, rows], rbuf.at[way, l, rows], send_sem.at[way, l], recv_sem.at[way, l],
            along_line(1 - 2 * way),
        )

    def factor_hop(way):
        return remote(
            sfac.at[way], rfac.at[way], fsend_sem.at[way], frecv_sem.at[way],
            along_line(1 - 2 * way),
        )

    def has_in(way):
        return jnp.where(way == 0, zq, NB - 1 - zq) > 0

    def has_out(way):
        return jnp.where(way == 0, NB - 1 - zq, zq) > 0

    def head_weights(l):
        v0 = jnp.where(zq == 0, 0.0, rfac[0, 4 + l : 5 + l, :])
        v1 = jnp.where(zq == 0, 1.0, v0 * dbuf[NB * l])
        v2 = v1 * dbuf[NB * l + 1]
        v3 = v2 * dbuf[NB * l + 2]
        return v0, v1, v2, v3, v3 * dbuf[NB * l + 3]

    def relay(way):
        @pl.when(has_in(way))
        def _():
            factor_hop(way).wait_recv()

        @pl.when(has_out(way))
        def _():
            for l in range(NX):
                sfac[way, l : l + 1, :] = rfac[way, l : l + 1, :] * blk[l]
                sfac[way, 4 + l : 5 + l, :] = (
                    head_weights(l)[4] if way == 0 else jnp.zeros((1, INNER), F32)
                )
            factor_hop(way).start()

        for l in range(NX):

            @pl.when(has_in(way))
            def _():
                hop(way, l).wait_recv()

            @pl.when(has_out(way))
            def _():
                sbuf[way, l, 0:RC, :] = blk[l] * rbuf[way, l, 0:RC, :] + tot[way, l]
                if l != (0, NX - 1)[way]:
                    sbuf[way, l, RC:, :] = (
                        rbuf[way, l, RC:, :] + rfac[way, l : l + 1, :] * tot[1 - way, l]
                    )
                hop(way, l).start()

    @pl.when(left)
    def _():
        relay(0)

    @pl.when(jnp.logical_not(left))
    def _():
        relay(1)

    @pl.when(zq == 0)
    def _():
        relay_tails()

    @pl.when(zq == NB - 1)
    def _():
        relay_heads()

    mine_rows = pl.ds(pl.multiple_of(me_o * RC, RC), RC)
    for l in range(NX):
        pre = heads[l, :, 0:CH] + sum(w_ref[k : k + 1, :] * tails[l, k : k + 8, :] for k in range(3))
        act = jnp.where(iota((8, CH), 0) < 3, pre / (1.0 + jnp.exp(-pre)), 0.0).astype(BF16)
        hi, lo = split(act[:, :INNER].astype(F32) * heads[l, :, CH : CH + INNER])
        b_row = act[:, INNER : INNER + N]
        c_row = act[:, INNER + N :]
        cfull[...] = dot_tn(b_row, hi) + dot_tn(b_row, lo)
        corr[0, l] = cfull[mine_rows, :]
        hi, lo = split(heads[l, :, CH + INNER :])
        cfull[...] = dot_tn(c_row, hi) + dot_tn(c_row, lo)
        corr[1, l] = cfull[mine_rows, :]

    @pl.when(left)
    def _():
        relay(1)

    @pl.when(jnp.logical_not(left))
    def _():
        relay(0)

    def line_terms(l):
        f = rfac[0, l : l + 1, :]
        e = rfac[1, l : l + 1, :]
        return f, e, f * e * blk[l]

    def give_back(l, i, entering, way):
        rsend[NB * l + i, RC * way : RC * way + RC, :] = entering

    carry = jnp.zeros((RC, INNER), F32)
    for l in range(NX):
        f, e, whole = line_terms(l)
        weights = head_weights(l)
        at = rbuf[0, l, 0:RC, :] + f * carry
        for i in range(NB):
            here = at + weights[i] * corr[0, l]
            if i:
                here = here + pre_p[NB * l + i]
            give_back(l, i, here, 0)
            at = at * dbuf[NB * l + i]
        if l == NX - 1:
            break
        total = (
            e * (blk[l] * rbuf[0, l, 0:RC, :] + tot[0, l] + weights[4] * corr[0, l])
            + rbuf[1, l, RC:, :]
        )
        carry = whole * carry + total
    carry = jnp.zeros((RC, INNER), F32)
    for l in range(NX - 1, -1, -1):
        f, e, whole = line_terms(l)
        at = rbuf[1, l, 0:RC, :] + e * carry
        for i in range(NB - 1, -1, -1):
            here = at
            if i < NB - 1:
                here = here + pre_q[NB * l + i]
            give_back(l, i, here, 1)
            at = at * dbuf[NB * l + i]
        if l == 0:
            break
        total = (
            f * (blk[l] * rbuf[1, l, 0:RC, :] + tot[1, l]) + rbuf[0, l, RC:, :] + corr[1, l]
        )
        carry = whole * carry + total

    def back(k, _):
        o, target = mate(k)
        remote(rsend.at[o], ret.at[me_o], asend_sem.at[2], arecv_sem.at[2], target).start()
        return 0

    lax.fori_loop(1, NO, back, 0)
    ret[pl.ds(me_o, 1)] = rsend[pl.ds(me_o, 1)]

    @pl.when(z == 0)
    def _():
        xp[5:8, :] = tails[x, 0:3, :]
        activate(0, 16)

    local_terms()

    @pl.when(zq == 0)
    def _():
        pl.semaphore_signal(
            edge_sem, inc=1, device_id=device(x, y, lax.rem(ring + ZR - NB, ZR), core),
            device_id_type=MESH,
        )
        pl.semaphore_wait(edge_sem, 1)
        pl.semaphore_signal(known_sem, inc=1, device_id=along_line(1), device_id_type=MESH)

    @pl.when(zq == NB - 1)
    def _():
        pl.semaphore_signal(
            edge_sem, inc=1, device_id=device(x, y, lax.rem(ring + NB, ZR), core),
            device_id_type=MESH,
        )
        pl.semaphore_wait(edge_sem, 1)
        pl.semaphore_signal(known_sem, inc=1, device_id=along_line(-1), device_id_type=MESH)

    from_block(ret, 2).wait_recv()
    s_in = ret[:, 0:RC, :].reshape(N, INNER)
    g_after = ret[:, RC:, :].reshape(N, INNER)

    b_val = xb[:, INNER : INNER + N]
    c_val = xb[:, INNER + N :]
    s_hi, s_lo = split(s_in)
    g_hi, g_lo = split(g_after)
    state_back = dot(b_val, g_hi) + dot(b_val, g_lo)
    state_proj = dot(c_val, s_hi) + dot(c_val, s_lo)
    cot = cot_ref[...].astype(F32)
    vals = xb[:, :INNER].astype(F32)
    scaled = cot * up_e[...]
    hi, lo = split(scaled)
    grad_c = gcl[...] + dot_nt(hi, s_hi) + dot_nt(hi, s_lo) + dot_nt(lo, s_hi)
    hi, lo = split(vals * tw_e[...])
    grad_b = gbl[...] + dot_nt(hi, g_hi) + dot_nt(hi, g_lo) + dot_nt(lo, g_hi)
    local_step = head_sums(vals * ac[...])
    tail_grad = head_sums(vals * state_back)
    proj_term = head_sums(scaled * state_proj)
    skip_lanes = spread(jnp.broadcast_to(0.0, (8, 128)) + sum(
        jnp.where(iota((8, 128), 1) == h, skip_ref[h], 0.0) for h in range(H)
    ), 0)[0:1, :]
    grad_vals = st_e[...] * ac[...] + skip_lanes * cot + tw_e[...] * state_back

    step = rows_s[8:16, :]
    tw = rows_s[16:24, :]
    cum = rows_s[0:8, :]
    cum_last = cum[:, L - 1 : L]
    sel = head_rows(F32)
    skip_sum = jnp.sum(sel * jnp.sum(cot * vals, axis=0, keepdims=True), axis=1, keepdims=True)
    both = jnp.sum(
        sel * jnp.sum(s_in * g_after, axis=0, keepdims=True), axis=1, keepdims=True
    )
    tail_term = tail_grad * tw
    extra = jnp.sum(tail_term, axis=1, keepdims=True) + jnp.exp(cum_last) * both
    grad_cum = pair_s[...] - step * local_step + proj_term - tail_term
    since = (iota((L, L), 0) >= iota((L, L), 1)).astype(F32).astype(BF16)
    grad_log = sum(dot(part, since) for part in split3(grad_cum)) + extra
    rows_s[32 : 32 + H, :] = dt_ref[...]
    dt_pre = rows_s[32:40, :] + head_column(dt_bias_ref)
    rate = -jnp.exp(head_column(a_log_ref))
    grad_step = local_step + tail_grad * jnp.exp(cum_last - cum) + rate * grad_log
    grad_pre = grad_step / (1.0 + jnp.exp(-dt_pre))
    gpre_ref[...] = grad_pre[0:H, :]
    alog_sum = rate * jnp.sum(grad_log * step, axis=1, keepdims=True)
    bias_sum = jnp.sum(grad_pre, axis=1, keepdims=True)

    gc_pad[0:8, :] = jnp.zeros((8, CH), F32)
    gc_pad[8 + L : 16 + L, :] = jnp.zeros((8, CH), F32)
    for lanes, value in (
        (slice(0, INNER), grad_vals),
        (slice(INNER, INNER + N), grad_b),
        (slice(INNER + N, CH), grad_c),
    ):
        low_value = value.astype(BF16).astype(F32)
        sig = sig_s[:, lanes]
        gc_pad[8 : 8 + L, lanes] = low_value * sig * (1.0 + pre_s[:, lanes] * (1.0 - sig))

    spill_out[...] = sum(w_ref[k : k + 1, :] * gc_pad[3 - k : 11 - k, :] for k in range(K))

    def spill(target):
        return remote(spill_out, spill_in, ssend_sem.at[0], srecv_sem.at[0], (target, dp))

    @pl.when(place > 0)
    def _():
        spill(place - 1).start()

    sums_ref[...] = jnp.zeros_like(sums_ref)
    for k in range(K + 1):
        term = gc_pad[8 : 8 + L, :]
        if k < K:
            term = term * xp[5 + k : 5 + k + L, :]
        total = jnp.sum(term, axis=0, keepdims=True)
        for j in range(4):
            sums_ref[4 * k + j] = total[:, 128 * j : 128 * j + 128]
    lane = iota((8, 128), 1)
    row = iota((8, 128), 0)
    small = (
        jnp.where(lane == row, bias_sum, 0.0)
        + jnp.where(lane == row + 8, alog_sum, 0.0)
        + jnp.where(lane == row + 16, skip_sum, 0.0)
    )
    small = jnp.where(row < H, small, 0.0)
    sums_ref[20] = jnp.sum(small, axis=0, keepdims=True)

    me = (x * NY + y) * 2 + core

    def in_plane(k):
        r = lax.rem(me + k, NR)
        return r, device(r // 8, lax.rem(r // 2, NY), ring, lax.rem(r, 2))

    def all_of(buf, stage):
        part = buf.at[pl.ds(0, NR - 1)]
        return remote(part, part, rsend_sem.at[stage], rrecv_sem.at[stage], in_plane(1)[1])

    def scatter(k, _):
        r, target = in_plane(k)
        remote(sums_ref.at[r], plane.at[me], rsend_sem.at[0], rrecv_sem.at[0], target).start()
        return 0

    lax.fori_loop(1, NR, scatter, 0)
    plane[pl.ds(me, 1)] = sums_ref[pl.ds(me, 1)]
    for r in range(0, L, 64):
        rows = sum(
            w_ref[k : k + 1, :] * gc_pad[11 - k + r : 11 - k + r + 64, :] for k in range(K)
        )
        gx_ref[r : r + 64, :] = rows.astype(BF16)
        if r + 64 == L:
            tail = rows[48:64, :]

    @pl.when(jnp.logical_and(zq > 0, zq < NB - 1))
    def _():
        pl.semaphore_wait(known_sem, 1)

    all_of(plane, 0).wait_recv()
    mine = jnp.sum(plane[...], axis=0, keepdims=True)
    own[0:1] = mine

    def along(k, _):
        q = lax.rem(ring + k, ZR)
        remote(
            own.at[0], line.at[ring], rsend_sem.at[1], rrecv_sem.at[1], device(x, y, q, core)
        ).start()
        return 0

    lax.fori_loop(1, ZR, along, 0)
    line[pl.ds(ring, 1)] = mine

    @pl.when(place < NX * NZ - 1)
    def _():
        spill(place + 1).wait_recv()

    @pl.when(place == NX * NZ - 1)
    def _():
        spill_in[...] = jnp.zeros_like(spill_in)

    gx_ref[L - 16 : L, :] = jnp.concatenate(
        [tail[0:8, :], tail[8:16, :] + spill_in[...]], axis=0
    ).astype(BF16)

    all_of(line, 1).wait_recv()
    total = jnp.sum(line[...], axis=0, keepdims=True)
    own[1:2] = total
    totals[pl.ds(me, 1)] = total

    def spread_out(k, _):
        remote(
            own.at[1], totals.at[me], rsend_sem.at[2], rrecv_sem.at[2], in_plane(k)[1]
        ).start()
        return 0

    lax.fori_loop(1, NR, spread_out, 0)
    for way in range(2):

        @pl.when(has_out(way))
        def _():
            factor_hop(way).wait_send()
            for l in range(NX):
                hop(way, l).wait_send()

    @pl.when(zq < NB - 1)
    def _():
        for l in range(NX):
            head(l, hsend_sem.at[0, l], along_line(1)).wait_send()

    @pl.when(zq > 0)
    def _():
        for l in range(1, NX):
            last(l, hsend_sem.at[1, l], along_line(-1)).wait_send()

    @pl.when(z == 0)
    def _():
        for k in range(1, NO):
            head(0, hcast_sem.at[k], along_line(1)).wait_send()

    @pl.when(has_tail)
    def _():
        for k in range(1, NO):
            last(0, hcast_sem.at[k], along_line(-1)).wait_send()

    @pl.when(z < NZ - 1)
    def _():
        near(place + 1).wait_send()

    for i, buf in enumerate((dbuf, abuf, ret)):
        from_block(buf, i).wait_send()

    @pl.when(place > 0)
    def _():
        spill(place - 1).wait_send()

    for stage, buf in enumerate((plane, line)):
        all_of(buf, stage).wait_send()
    all_of(totals, 2).wait_recv()
    for k in range(K):
        for j in range(4):
            wg_ref[k : k + 1, 128 * j : 128 * j + 128] = totals[4 * k + j]
    for j in range(4):
        bg_ref[0:1, 128 * j : 128 * j + 128] = totals[16 + j]
    small_ref[...] = totals[20]
    all_of(totals, 2).wait_send()


def run_main(raw, weight, bias, dt_t, dt_bias, a_log, d_skip, cot):
    vmem = pl.BlockSpec(memory_space=pltpu.VMEM)
    hbm = pl.BlockSpec(memory_space=pltpu.HBM)
    return pl.pallas_call(
        main_kernel,
        out_shape=(
            jax.ShapeDtypeStruct((L, CH), BF16),
            jax.ShapeDtypeStruct((H, L), F32),
            jax.ShapeDtypeStruct((K, CH), F32),
            jax.ShapeDtypeStruct((1, CH), F32),
            jax.ShapeDtypeStruct((1, 128), F32),
        ),
        in_specs=[hbm] * 8,
        out_specs=(vmem,) * 5,
        scratch_shapes=[
            pltpu.SMEM((H,), F32),
            pltpu.SMEM((H,), F32),
            pltpu.SMEM((H,), F32),
            pltpu.VMEM((L, CH), BF16),
            pltpu.VMEM((K, CH), F32),
            pltpu.VMEM((1, CH), F32),
            pltpu.VMEM((H, L), F32),
            pltpu.VMEM((L, INNER), BF16),
            pltpu.SemaphoreType.DMA((8,)),
            pltpu.VMEM((8 + L, CH), F32),
            pltpu.VMEM((L, CH), F32),
            pltpu.VMEM((L, CH), F32),
            pltpu.VMEM((L, CH), BF16),
            pltpu.VMEM((128, L), F32),
            pltpu.VMEM((L, 128), F32),
            pltpu.VMEM((NO, 2 * RC, INNER), F32),
            pltpu.VMEM((1, 1, INNER), F32),
            pltpu.VMEM((L, INNER), F32),
            pltpu.VMEM((L, INNER), F32),
            pltpu.VMEM((L, INNER), F32),
            pltpu.VMEM((L, INNER), F32),
            pltpu.VMEM((L, N), F32),
            pltpu.VMEM((L, N), F32),
            pltpu.VMEM((8, L), F32),
            pltpu.VMEM((16 + L, CH), F32),
            pltpu.VMEM((NO, 2 * RC, INNER), F32),
            pltpu.VMEM((NO, 1, INNER), F32),
            pltpu.VMEM((NO, RC, INNER), F32),
            pltpu.VMEM((NO, RC, INNER), F32),
            pltpu.VMEM((2, NX, RC, INNER), F32),
            pltpu.VMEM((NX, 1, INNER), F32),
            pltpu.VMEM((2, NX, 2 * RC, INNER), F32),
            pltpu.VMEM((2, NX, 2 * RC, INNER), F32),
            pltpu.VMEM((2, 8, INNER), F32),
            pltpu.VMEM((2, 8, INNER), F32),
            pltpu.VMEM((NX, 8, CH + 2 * INNER), F32),
            pltpu.VMEM((NX, 16, CH), F32),
            pltpu.VMEM((N, INNER), F32),
            pltpu.VMEM((2, NX, RC, INNER), F32),
            pltpu.VMEM((NO, 2 * RC, INNER), F32),
            pltpu.VMEM((NO, 2 * RC, INNER), F32),
            pltpu.VMEM((8, CH), F32),
            pltpu.VMEM((8, CH), F32),
            pltpu.VMEM((8, CH), F32),
            pltpu.VMEM((8, CH), F32),
            pltpu.VMEM((NR, 1, 128), F32),
            pltpu.VMEM((NR, 1, 128), F32),
            pltpu.VMEM((ZR, 1, 128), F32),
            pltpu.VMEM((2, 1, 128), F32),
            pltpu.VMEM((NR, 1, 128), F32),
            pltpu.SemaphoreType.DMA((2, NX)),
            pltpu.SemaphoreType.DMA((2, NX)),
            pltpu.SemaphoreType.DMA((2,)),
            pltpu.SemaphoreType.DMA((2,)),
            pltpu.SemaphoreType.DMA((3,)),
            pltpu.SemaphoreType.DMA((3,)),
            pltpu.SemaphoreType.DMA((2, NX)),
            pltpu.SemaphoreType.DMA((2, NX)),
            pltpu.SemaphoreType.DMA((NO,)),
            pltpu.SemaphoreType.DMA((1,)),
            pltpu.SemaphoreType.DMA((1,)),
            pltpu.SemaphoreType.DMA((1,)),
            pltpu.SemaphoreType.DMA((1,)),
            pltpu.SemaphoreType.DMA((3,)),
            pltpu.SemaphoreType.DMA((3,)),
            pltpu.SemaphoreType.REGULAR,
            pltpu.SemaphoreType.REGULAR,
        ],
        compiler_params=pltpu.CompilerParams(
            collective_id=0, has_side_effects=True, vmem_limit_bytes=67043328
        ),
        name="slab",
    )(dt_bias, a_log, d_skip, raw, weight, bias, dt_t, cot)


def finish_kernel(gx, gpre, wg, bg, small, gx_o, gpre_o, wg_o, bg_o, db_o, da_o, ds_o):
    gx_o[...] = gx[...]
    gpre_o[...] = gpre[...]
    wg_o[...] = wg[...]
    bg_o[...] = bg[...]
    db_o[...] = small[0:1, 0:4]
    da_o[...] = small[0:1, 8:12]
    ds_o[...] = small[0:1, 16:20]


def finish(*parts):
    vmem = pl.BlockSpec(memory_space=pltpu.VMEM)
    head = jax.ShapeDtypeStruct((1, H), F32)
    return pl.pallas_call(
        finish_kernel,
        out_shape=tuple(jax.ShapeDtypeStruct(p.shape, p.dtype) for p in parts[:4]) + (head,) * 3,
        in_specs=[vmem] * 5,
        out_specs=(vmem,) * 7,
        compiler_params=pltpu.CompilerParams(vmem_limit_bytes=67043328),
        name="finish",
    )(*parts)


def on_device(xbc_raw, conv_weight, conv_bias, dt_raw, dt_bias, a_log, d_skip, grad_out):
    gx, gpre, weight_grad, bias_grad, bias, decay, skip = finish(*run_main(
        xbc_raw[0], conv_weight, conv_bias[None], dt_raw[0].T, dt_bias, a_log, d_skip, grad_out[0]
    ))
    return (
        gx[None], gpre.T[None], weight_grad, bias_grad[0], bias[0], decay[0], skip[0],
    )


def solution(mesh):
    rows = P("dp", "ctx", None)
    return jax.shard_map(
        on_device,
        mesh=mesh,
        in_specs=(rows, P(), P(), rows, P(), P(), P(), rows),
        out_specs=(rows, rows, P(), P(), P(), P(), P()),
        check_vma=False,
    )
```

```python
import functools

import jax
import jax.numpy as jnp
from jax import lax
from jax.experimental import pallas as pl
from jax.experimental.pallas import tpu as pltpu
from jax.sharding import PartitionSpec as P

H = 4
P_SIZE = 64
N = 128
K = 4
L = 256
CH = 512
INNER = H * P_SIZE
NZ = 16
NX = 4
NY = 4
NR = 32
ZR = 32
NB = 4
NO = 16
RC = N // NO
F32 = jnp.float32
BF16 = jnp.bfloat16
MESH = pl.DeviceIdType.MESH


def dot(a, b):
    return lax.dot_general(a, b, (((1,), (0,)), ((), ())), preferred_element_type=F32)


def dot_nt(a, b):
    return lax.dot_general(a, b, (((1,), (1,)), ((), ())), preferred_element_type=F32)


def dot_tn(a, b):
    return lax.dot_general(a, b, (((0,), (0,)), ((), ())), preferred_element_type=F32)


def split(a):
    hi = a.astype(BF16)
    return hi, (a - hi.astype(F32)).astype(BF16)


def split3(a):
    hi = a.astype(BF16)
    rest = a - hi.astype(F32)
    mid = rest.astype(BF16)
    return hi, mid, (rest - mid.astype(F32)).astype(BF16)


def iota(shape, dim):
    return lax.broadcasted_iota(jnp.int32, shape, dim)


def head_column(ref):
    rows = iota((8, 1), 0)
    col = jnp.zeros((8, 1), F32)
    for h in range(H):
        col = jnp.where(rows == h, ref[h], col)
    return col


def spread(cols, first):
    rows = cols.shape[0]
    low = iota((rows, 128), 1) < P_SIZE
    tiles = []
    for j in range(2):
        a = jnp.broadcast_to(cols[:, first + 2 * j : first + 2 * j + 1], (rows, 128))
        b = jnp.broadcast_to(cols[:, first + 2 * j + 1 : first + 2 * j + 2], (rows, 128))
        tiles.append(jnp.where(low, a, b))
    return jnp.concatenate(tiles, axis=1)


def head_rows(dtype):
    return (iota((8, INNER), 1) // P_SIZE == iota((8, INNER), 0)).astype(dtype)


def head_sums(x):
    sel = head_rows(F32).astype(BF16)
    hi, lo = split(x)
    return dot_nt(sel, hi) + dot_nt(sel, lo)


def main_kernel(
    dt_bias_hbm, a_log_hbm, skip_hbm, raw_hbm, w_hbm, bias_hbm, dt_hbm, cot_hbm,
    gx_ref, gpre_ref, wg_ref, bg_ref, small_ref,
    dt_bias_ref, a_log_ref, skip_ref, raw_ref, w_ref, bias_ref, dt_ref, cot_ref, in_sem,
    xp, pre_s, sig_s, xb, rows_s, cols_s, loc, dec, tw_e, up_e, st_e, ac, gbl, gcl, pair_s,
    gc_pad, abuf, dbuf, pre_p, pre_q, tot, blk, rbuf, sbuf, rfac, sfac, heads, tails, cfull, corr,
    rsend, ret, near_out, near_in, spill_out, spill_in, sums_ref, plane, line, own, totals,
    send_sem, recv_sem, fsend_sem, frecv_sem, asend_sem, arecv_sem, hsend_sem, hrecv_sem,
    hcast_sem, nsend_sem, nrecv_sem, ssend_sem, srecv_sem, rsend_sem, rrecv_sem, edge_sem,
    known_sem,
):
    place = lax.axis_index("ctx")
    dp = lax.axis_index("dp")
    z = lax.rem(place, NZ)
    x = place // NZ
    y = dp // 4
    z_hi = lax.rem(dp // 2, 2)
    core = lax.rem(dp, 2)

    def device(x_, y_, ring, core_):
        return (x_ * NZ + lax.rem(ring, NZ), y_ * 4 + (ring // NZ) * 2 + core_)

    ring = z_hi * NZ + z
    zq = z // NB
    zi = lax.rem(z, NB)
    me_o = x * NB + zi

    def remote(src, dst, send, recv, target):
        return pltpu.make_async_remote_copy(
            src_ref=src, dst_ref=dst, send_sem=send, recv_sem=recv, device_id=target,
            device_id_type=MESH,
        )

    def mate(k):
        o = lax.rem(me_o + k, NO)
        return o, ((o // NB) * NZ + zq * NB + lax.rem(o, NB), dp)

    heads[...] = jnp.zeros_like(heads)
    tails[...] = jnp.zeros_like(tails)
    barrier = pltpu.get_barrier_semaphore()
    inputs = [
        pltpu.make_async_copy(src, dst, in_sem.at[i])
        for i, (src, dst) in enumerate(
            ((raw_hbm, raw_ref), (w_hbm, w_ref), (bias_hbm, bias_ref), (dt_hbm, dt_ref),
             (cot_hbm, cot_ref), (dt_bias_hbm, dt_bias_ref), (a_log_hbm, a_log_ref),
             (skip_hbm, skip_ref))
        )
    ]
    for step in (1, ZR - 1, NB, ZR - NB):
        pl.semaphore_signal(
            barrier, inc=1, device_id=device(x, y, lax.rem(ring + step, ZR), core),
            device_id_type=MESH,
        )

    def greet(k, _):
        pl.semaphore_signal(barrier, inc=1, device_id=mate(k)[1], device_id_type=MESH)
        return 0

    lax.fori_loop(1, NO, greet, 0)
    for k in range(1, 2 * NY):
        q = lax.rem(y * 2 + core + k, 2 * NY)
        pl.semaphore_signal(
            barrier, inc=1, device_id=device(x, q // 2, ring, lax.rem(q, 2)), device_id_type=MESH
        )
    for copy in inputs:
        copy.start()
    for copy in inputs:
        copy.wait()

    xp[0:8, :] = jnp.zeros((8, CH), F32)
    xp[8 : 8 + L, :] = raw_ref[...].astype(F32)

    def activate(r, size):
        pre = bias_ref[...] + sum(
            w_ref[k : k + 1, :] * xp[5 + k + r : 5 + k + r + size, :] for k in range(K)
        )
        sig = 1.0 / (1.0 + jnp.exp(-pre))
        pre_s[r : r + size, :] = pre
        sig_s[r : r + size, :] = sig
        xb[r : r + size, :] = (pre * sig).astype(BF16)

    for r in range(0, L, 64):
        activate(r, 64)

    rate = -jnp.exp(head_column(a_log_ref))
    live = iota((8, 1), 0) < H
    rate = jnp.where(live, rate, 0.0)
    rows_s[...] = jnp.zeros_like(rows_s)
    rows_s[0:H, :] = dt_ref[...]
    dt_pre = rows_s[0:8, :] + head_column(dt_bias_ref)
    step = jnp.where(
        live, jnp.maximum(dt_pre, 0.0) + jnp.log1p(jnp.exp(-jnp.abs(dt_pre))), 0.0
    )
    upto = (iota((L, L), 0) <= iota((L, L), 1)).astype(F32).astype(BF16)
    cum = sum(dot(part, upto) for part in split3(step * rate))
    cum_last = cum[:, L - 1 : L]
    to_end = jnp.exp(cum_last - cum)
    tw = to_end * step
    up = jnp.exp(cum)
    rows_s[0:8, :] = cum
    rows_s[8:16, :] = step
    rows_s[16:24, :] = tw
    rows_s[24:32, :] = up
    cols = jnp.transpose(rows_s[...])
    cols_s[...] = cols
    tw_e[...] = spread(cols, 16)
    up_e[...] = spread(cols, 24)
    st_e[...] = spread(cols, 8)
    dec[0] = up_e[L - 1 : L, :]
    near_out[0:3, :] = xp[5 + L : 8 + L, :]

    pl.semaphore_wait(barrier, 4 + NO - 1 + 2 * NY - 1)

    def near(target):
        return remote(
            near_out.at[0:3], near_in.at[0:3], nsend_sem.at[0], nrecv_sem.at[0], (target, dp)
        )

    @pl.when(z < NZ - 1)
    def _():
        near(place + 1).start()

    def head(l, send, target):
        return remote(heads.at[l, 0:3], heads.at[l, 0:3], send, hrecv_sem.at[0, l], target)

    def last(l, send, target):
        return remote(tails.at[l, 0:3], tails.at[l, 0:3], send, hrecv_sem.at[1, l], target)

    @pl.when(z == 0)
    def _():
        heads[x, 0:3, 0:CH] = pre_s[0:3, :]
        heads[x, 0:3, CH : CH + INNER] = tw_e[0:3, :]
        heads[x, 0:3, CH + INNER :] = (cot_ref[...].astype(F32) * up_e[...])[0:3, :]

        def cast(k, _):
            o, target = mate(k)
            head(x, hcast_sem.at[k], target).start()
            return 0

        lax.fori_loop(1, NO, cast, 0)

    has_tail = jnp.logical_and(z == NZ - 1, x < NX - 1)

    @pl.when(has_tail)
    def _():
        tails[x + 1, 0:3, :] = near_out[0:3, :]

        def cast(k, _):
            o, target = mate(k)
            last(x + 1, hcast_sem.at[k], target).start()
            return 0

        lax.fori_loop(1, NO, cast, 0)

    @pl.when(z > 0)
    def _():
        near(place - 1).wait_recv()
        xp[5:8, :] = near_in[0:3, :]
        activate(0, 16)

    ready = jnp.logical_or(iota((L, INNER), 0) >= 3, z > 0)
    b_val = xb[:, INNER : INNER + N]
    c_val = xb[:, INNER + N :]
    hi, lo = split(jnp.where(ready, xb[:, :INNER].astype(F32) * tw_e[...], 0.0))
    loc[:, 0:RC, :] = (dot_tn(b_val, hi) + dot_tn(b_val, lo)).reshape(NO, RC, INNER)
    hi, lo = split(jnp.where(ready, cot_ref[...].astype(F32) * up_e[...], 0.0))
    loc[:, RC:, :] = (dot_tn(c_val, hi) + dot_tn(c_val, lo)).reshape(NO, RC, INNER)

    def to_owners(k, _):
        o, target = mate(k)
        remote(dec.at[0], dbuf.at[me_o], asend_sem.at[0], arecv_sem.at[0], target).start()
        remote(loc.at[o], abuf.at[me_o], asend_sem.at[1], arecv_sem.at[1], target).start()
        return 0

    lax.fori_loop(1, NO, to_owners, 0)
    abuf[pl.ds(me_o, 1)] = loc[pl.ds(me_o, 1)]
    dbuf[pl.ds(me_o, 1)] = dec[...]

    def from_block(buf, i):
        part = buf.at[pl.ds(0, NO - 1)]
        return remote(part, part, asend_sem.at[i], arecv_sem.at[i], mate(1)[1])

    def along_line(step):
        return (place + NB * step, dp)

    def relay_heads():
        for l in range(NX):

            @pl.when(jnp.logical_not(jnp.logical_and(z == 0, x == l)))
            def _():
                head(l, hsend_sem.at[0, l], along_line(1)).wait_recv()

            @pl.when(zq < NB - 1)
            def _():
                head(l, hsend_sem.at[0, l], along_line(1)).start()

    def relay_tails():
        for l in range(1, NX):

            @pl.when(jnp.logical_not(jnp.logical_and(z == NZ - 1, x == l - 1)))
            def _():
                last(l, hsend_sem.at[1, l], along_line(-1)).wait_recv()

            @pl.when(zq > 0)
            def _():
                last(l, hsend_sem.at[1, l], along_line(-1)).start()

    def local_terms():
        pair_s[...] = jnp.zeros_like(pair_s)
        low = iota((128, 128), 1) < P_SIZE
        for sb in range(2):
            t0 = 128 * sb
            wide = L - t0
            rs = slice(t0, t0 + 128)
            gram = dot_nt(xb[rs, INNER : INNER + N], xb[t0:, INNER + N :])
            mask = iota((128, wide), 1) >= iota((128, wide), 0)
            dgram = jnp.zeros((128, wide), F32)
            for j in range(2):
                cot_t = cot_ref[t0:, 128 * j : 128 * j + 128]
                v_t = xb[rs, 128 * j : 128 * j + 128]
                parts = []
                for i in range(2):
                    h = 2 * j + i
                    keep = low if i == 0 else jnp.logical_not(low)
                    v_h = jnp.where(keep, v_t.astype(F32), 0.0).astype(BF16)
                    gap = rows_s[h : h + 1, t0:] - cols_s[rs, h : h + 1]
                    within = jnp.exp(jnp.where(mask, gap, -1e30))
                    dmix = dot_nt(v_h, cot_t)
                    hi, lo = split(gram * within)
                    parts.append(dot(hi, cot_t) + dot(lo, cot_t))
                    dw = dmix * within * cols_s[rs, 8 + h : 9 + h]
                    dgram = dgram + dw
                    pair_s[h : h + 1, t0:] += jnp.sum(dw * gram, axis=0, keepdims=True)
                ac[rs, 128 * j : 128 * j + 128] = jnp.where(low, parts[0], parts[1])
            hi, lo = split(dgram)
            c_t = xb[t0:, INNER + N :]
            b_s = xb[rs, INNER : INNER + N]
            gbl[rs, :] = dot(hi, c_t) + dot(lo, c_t)
            from_here = dot_tn(hi, b_s) + dot_tn(lo, b_s)
            if sb == 0:
                gcl[...] = from_here
            else:
                gcl[t0:, :] += from_here

    left = zq < NB // 2

    @pl.when(left)
    def _():
        relay_heads()

    @pl.when(zq > 0)
    def _():
        relay_tails()

    @pl.when(zq == NB // 2)
    def _():
        relay_heads()

    from_block(dbuf, 0).wait_recv()
    from_block(abuf, 1).wait_recv()
    for l in range(NX):
        p = abuf[NB * l, 0:RC, :]
        q = abuf[NB * l + NB - 1, RC:, :]
        for i in range(1, NB):
            pre_p[NB * l + i] = p
            p = dbuf[NB * l + i] * p + abuf[NB * l + i, 0:RC, :]
            j = NB - 1 - i
            pre_q[NB * l + j] = q
            q = dbuf[NB * l + j] * q + abuf[NB * l + j, RC:, :]
        tot[0, l] = p
        tot[1, l] = q
        blk[l] = dbuf[NB * l] * dbuf[NB * l + 1] * dbuf[NB * l + 2] * dbuf[NB * l + 3]

    @pl.when(zq == 0)
    def _():
        rbuf[0] = jnp.zeros((NX, 2 * RC, INNER), F32)
        rfac[0] = jnp.ones((8, INNER), F32)

    @pl.when(zq == NB - 1)
    def _():
        rbuf[1] = jnp.zeros((NX, 2 * RC, INNER), F32)
        rfac[1] = jnp.ones((8, INNER), F32)

    first = jnp.where(left, 0, 1)

    def hop(way, l):
        rows = slice(0, RC if l == (0, NX - 1)[way] else 2 * RC)
        return remote(
            sbuf.at[way, l, rows], rbuf.at[way, l, rows], send_sem.at[way, l], recv_sem.at[way, l],
            along_line(1 - 2 * way),
        )

    def factor_hop(way):
        return remote(
            sfac.at[way], rfac.at[way], fsend_sem.at[way], frecv_sem.at[way],
            along_line(1 - 2 * way),
        )

    def has_in(way):
        return jnp.where(way == 0, zq, NB - 1 - zq) > 0

    def has_out(way):
        return jnp.where(way == 0, NB - 1 - zq, zq) > 0

    def head_weights(l):
        v0 = jnp.where(zq == 0, 0.0, rfac[0, 4 + l : 5 + l, :])
        v1 = jnp.where(zq == 0, 1.0, v0 * dbuf[NB * l])
        v2 = v1 * dbuf[NB * l + 1]
        v3 = v2 * dbuf[NB * l + 2]
        return v0, v1, v2, v3, v3 * dbuf[NB * l + 3]

    def relay(way):
        @pl.when(has_in(way))
        def _():
            factor_hop(way).wait_recv()

        @pl.when(has_out(way))
        def _():
            for l in range(NX):
                sfac[way, l : l + 1, :] = rfac[way, l : l + 1, :] * blk[l]
                sfac[way, 4 + l : 5 + l, :] = (
                    head_weights(l)[4] if way == 0 else jnp.zeros((1, INNER), F32)
                )
            factor_hop(way).start()

        for l in range(NX):

            @pl.when(has_in(way))
            def _():
                hop(way, l).wait_recv()

            @pl.when(has_out(way))
            def _():
                sbuf[way, l, 0:RC, :] = blk[l] * rbuf[way, l, 0:RC, :] + tot[way, l]
                if l != (0, NX - 1)[way]:
                    sbuf[way, l, RC:, :] = (
                        rbuf[way, l, RC:, :] + rfac[way, l : l + 1, :] * tot[1 - way, l]
                    )
                hop(way, l).start()

    @pl.when(left)
    def _():
        relay(0)

    @pl.when(jnp.logical_not(left))
    def _():
        relay(1)

    @pl.when(zq == 0)
    def _():
        relay_tails()

    @pl.when(zq == NB - 1)
    def _():
        relay_heads()

    mine_rows = pl.ds(pl.multiple_of(me_o * RC, RC), RC)
    for l in range(NX):
        pre = heads[l, :, 0:CH] + sum(w_ref[k : k + 1, :] * tails[l, k : k + 8, :] for k in range(3))
        act = jnp.where(iota((8, CH), 0) < 3, pre / (1.0 + jnp.exp(-pre)), 0.0).astype(BF16)
        hi, lo = split(act[:, :INNER].astype(F32) * heads[l, :, CH : CH + INNER])
        b_row = act[:, INNER : INNER + N]
        c_row = act[:, INNER + N :]
        cfull[...] = dot_tn(b_row, hi) + dot_tn(b_row, lo)
        corr[0, l] = cfull[mine_rows, :]
        hi, lo = split(heads[l, :, CH + INNER :])
        cfull[...] = dot_tn(c_row, hi) + dot_tn(c_row, lo)
        corr[1, l] = cfull[mine_rows, :]

    @pl.when(left)
    def _():
        relay(1)

    @pl.when(jnp.logical_not(left))
    def _():
        relay(0)

    def line_terms(l):
        f = rfac[0, l : l + 1, :]
        e = rfac[1, l : l + 1, :]
        return f, e, f * e * blk[l]

    def give_back(l, i, entering, way):
        rsend[NB * l + i, RC * way : RC * way + RC, :] = entering

    carry = jnp.zeros((RC, INNER), F32)
    for l in range(NX):
        f, e, whole = line_terms(l)
        weights = head_weights(l)
        at = rbuf[0, l, 0:RC, :] + f * carry
        for i in range(NB):
            here = at + weights[i] * corr[0, l]
            if i:
                here = here + pre_p[NB * l + i]
            give_back(l, i, here, 0)
            at = at * dbuf[NB * l + i]
        if l == NX - 1:
            break
        total = (
            e * (blk[l] * rbuf[0, l, 0:RC, :] + tot[0, l] + weights[4] * corr[0, l])
            + rbuf[1, l, RC:, :]
        )
        carry = whole * carry + total
    carry = jnp.zeros((RC, INNER), F32)
    for l in range(NX - 1, -1, -1):
        f, e, whole = line_terms(l)
        at = rbuf[1, l, 0:RC, :] + e * carry
        for i in range(NB - 1, -1, -1):
            here = at
            if i < NB - 1:
                here = here + pre_q[NB * l + i]
            give_back(l, i, here, 1)
            at = at * dbuf[NB * l + i]
        if l == 0:
            break
        total = (
            f * (blk[l] * rbuf[1, l, 0:RC, :] + tot[1, l]) + rbuf[0, l, RC:, :] + corr[1, l]
        )
        carry = whole * carry + total

    def back(k, _):
        o, target = mate(k)
        remote(rsend.at[o], ret.at[me_o], asend_sem.at[2], arecv_sem.at[2], target).start()
        return 0

    lax.fori_loop(1, NO, back, 0)
    ret[pl.ds(me_o, 1)] = rsend[pl.ds(me_o, 1)]

    @pl.when(z == 0)
    def _():
        xp[5:8, :] = tails[x, 0:3, :]
        activate(0, 16)

    local_terms()

    @pl.when(zq == 0)
    def _():
        pl.semaphore_signal(
            edge_sem, inc=1, device_id=device(x, y, lax.rem(ring + ZR - NB, ZR), core),
            device_id_type=MESH,
        )
        pl.semaphore_wait(edge_sem, 1)
        pl.semaphore_signal(known_sem, inc=1, device_id=along_line(1), device_id_type=MESH)

    @pl.when(zq == NB - 1)
    def _():
        pl.semaphore_signal(
            edge_sem, inc=1, device_id=device(x, y, lax.rem(ring + NB, ZR), core),
            device_id_type=MESH,
        )
        pl.semaphore_wait(edge_sem, 1)
        pl.semaphore_signal(known_sem, inc=1, device_id=along_line(-1), device_id_type=MESH)

    cot = cot_ref[...].astype(F32)
    vals = xb[:, :INNER].astype(F32)
    local_step = head_sums(vals * ac[...])
    sel = head_rows(F32)
    skip_sum = jnp.sum(sel * jnp.sum(cot * vals, axis=0, keepdims=True), axis=1, keepdims=True)
    skip_lanes = spread(jnp.broadcast_to(0.0, (8, 128)) + sum(
        jnp.where(iota((8, 128), 1) == h, skip_ref[h], 0.0) for h in range(H)
    ), 0)[0:1, :]
    ac[...] = st_e[...] * ac[...] + skip_lanes * cot

    from_block(ret, 2).wait_recv()
    s_in = ret[:, 0:RC, :].reshape(N, INNER)
    g_after = ret[:, RC:, :].reshape(N, INNER)

    b_val = xb[:, INNER : INNER + N]
    c_val = xb[:, INNER + N :]
    s_hi, s_lo = split(s_in)
    g_hi, g_lo = split(g_after)
    state_back = dot(b_val, g_hi) + dot(b_val, g_lo)
    state_proj = dot(c_val, s_hi) + dot(c_val, s_lo)
    scaled = cot * up_e[...]
    hi, lo = split(scaled)
    grad_c = gcl[...] + dot_nt(hi, s_hi) + dot_nt(hi, s_lo) + dot_nt(lo, s_hi)
    hi, lo = split(vals * tw_e[...])
    grad_b = gbl[...] + dot_nt(hi, g_hi) + dot_nt(hi, g_lo) + dot_nt(lo, g_hi)
    tail_grad = head_sums(vals * state_back)
    proj_term = head_sums(scaled * state_proj)
    grad_vals = ac[...] + tw_e[...] * state_back

    step = rows_s[8:16, :]
    tw = rows_s[16:24, :]
    cum = rows_s[0:8, :]
    cum_last = cum[:, L - 1 : L]
    both = jnp.sum(
        sel * jnp.sum(s_in * g_after, axis=0, keepdims=True), axis=1, keepdims=True
    )
    tail_term = tail_grad * tw
    extra = jnp.sum(tail_term, axis=1, keepdims=True) + jnp.exp(cum_last) * both
    grad_cum = pair_s[...] - step * local_step + proj_term - tail_term
    since = (iota((L, L), 0) >= iota((L, L), 1)).astype(F32).astype(BF16)
    grad_log = sum(dot(part, since) for part in split3(grad_cum)) + extra
    rows_s[32 : 32 + H, :] = dt_ref[...]
    dt_pre = rows_s[32:40, :] + head_column(dt_bias_ref)
    rate = -jnp.exp(head_column(a_log_ref))
    grad_step = local_step + tail_grad * jnp.exp(cum_last - cum) + rate * grad_log
    grad_pre = grad_step / (1.0 + jnp.exp(-dt_pre))
    gpre_ref[...] = grad_pre[0:H, :]
    alog_sum = rate * jnp.sum(grad_log * step, axis=1, keepdims=True)
    bias_sum = jnp.sum(grad_pre, axis=1, keepdims=True)

    gc_pad[0:8, :] = jnp.zeros((8, CH), F32)
    gc_pad[8 + L : 16 + L, :] = jnp.zeros((8, CH), F32)
    for lanes, value in (
        (slice(0, INNER), grad_vals),
        (slice(INNER, INNER + N), grad_b),
        (slice(INNER + N, CH), grad_c),
    ):
        low_value = value.astype(BF16).astype(F32)
        sig = sig_s[:, lanes]
        gc_pad[8 : 8 + L, lanes] = low_value * sig * (1.0 + pre_s[:, lanes] * (1.0 - sig))

    spill_out[...] = sum(w_ref[k : k + 1, :] * gc_pad[3 - k : 11 - k, :] for k in range(K))

    def spill(target):
        return remote(spill_out, spill_in, ssend_sem.at[0], srecv_sem.at[0], (target, dp))

    @pl.when(place > 0)
    def _():
        spill(place - 1).start()

    sums_ref[...] = jnp.zeros_like(sums_ref)
    for k in range(K + 1):
        term = gc_pad[8 : 8 + L, :]
        if k < K:
            term = term * xp[5 + k : 5 + k + L, :]
        total = jnp.sum(term, axis=0, keepdims=True)
        for j in range(4):
            sums_ref[4 * k + j] = total[:, 128 * j : 128 * j + 128]
    lane = iota((8, 128), 1)
    row = iota((8, 128), 0)
    small = (
        jnp.where(lane == row, bias_sum, 0.0)
        + jnp.where(lane == row + 8, alog_sum, 0.0)
        + jnp.where(lane == row + 16, skip_sum, 0.0)
    )
    small = jnp.where(row < H, small, 0.0)
    sums_ref[20] = jnp.sum(small, axis=0, keepdims=True)

    me = (x * NY + y) * 2 + core

    def in_plane(k):
        r = lax.rem(me + k, NR)
        return r, device(r // 8, lax.rem(r // 2, NY), ring, lax.rem(r, 2))

    def all_of(buf, stage):
        part = buf.at[pl.ds(0, NR - 1)]
        return remote(part, part, rsend_sem.at[stage], rrecv_sem.at[stage], in_plane(1)[1])

    def scatter(k, _):
        r, target = in_plane(k)
        remote(sums_ref.at[r], plane.at[me], rsend_sem.at[0], rrecv_sem.at[0], target).start()
        return 0

    lax.fori_loop(1, NR, scatter, 0)
    plane[pl.ds(me, 1)] = sums_ref[pl.ds(me, 1)]
    for r in range(0, L, 64):
        rows = sum(
            w_ref[k : k + 1, :] * gc_pad[11 - k + r : 11 - k + r + 64, :] for k in range(K)
        )
        gx_ref[r : r + 64, :] = rows.astype(BF16)
        if r + 64 == L:
            tail = rows[48:64, :]

    @pl.when(jnp.logical_and(zq > 0, zq < NB - 1))
    def _():
        pl.semaphore_wait(known_sem, 1)

    all_of(plane, 0).wait_recv()
    mine = jnp.sum(plane[...], axis=0, keepdims=True)
    own[0:1] = mine

    def along(k, _):
        q = lax.rem(ring + k, ZR)
        remote(
            own.at[0], line.at[ring], rsend_sem.at[1], rrecv_sem.at[1], device(x, y, q, core)
        ).start()
        return 0

    lax.fori_loop(1, ZR, along, 0)
    line[pl.ds(ring, 1)] = mine

    @pl.when(place < NX * NZ - 1)
    def _():
        spill(place + 1).wait_recv()

    @pl.when(place == NX * NZ - 1)
    def _():
        spill_in[...] = jnp.zeros_like(spill_in)

    gx_ref[L - 16 : L, :] = jnp.concatenate(
        [tail[0:8, :], tail[8:16, :] + spill_in[...]], axis=0
    ).astype(BF16)

    all_of(line, 1).wait_recv()
    total = jnp.sum(line[...], axis=0, keepdims=True)
    own[1:2] = total
    totals[pl.ds(me, 1)] = total

    def spread_out(k, _):
        remote(
            own.at[1], totals.at[me], rsend_sem.at[2], rrecv_sem.at[2], in_plane(k)[1]
        ).start()
        return 0

    lax.fori_loop(1, NR, spread_out, 0)
    for way in range(2):

        @pl.when(has_out(way))
        def _():
            factor_hop(way).wait_send()
            for l in range(NX):
                hop(way, l).wait_send()

    @pl.when(zq < NB - 1)
    def _():
        for l in range(NX):
            head(l, hsend_sem.at[0, l], along_line(1)).wait_send()

    @pl.when(zq > 0)
    def _():
        for l in range(1, NX):
            last(l, hsend_sem.at[1, l], along_line(-1)).wait_send()

    @pl.when(z == 0)
    def _():
        for k in range(1, NO):
            head(0, hcast_sem.at[k], along_line(1)).wait_send()

    @pl.when(has_tail)
    def _():
        for k in range(1, NO):
            last(0, hcast_sem.at[k], along_line(-1)).wait_send()

    @pl.when(z < NZ - 1)
    def _():
        near(place + 1).wait_send()

    for i, buf in enumerate((dbuf, abuf, ret)):
        from_block(buf, i).wait_send()

    @pl.when(place > 0)
    def _():
        spill(place - 1).wait_send()

    for stage, buf in enumerate((plane, line)):
        all_of(buf, stage).wait_send()
    all_of(totals, 2).wait_recv()
    for k in range(K):
        for j in range(4):
            wg_ref[k : k + 1, 128 * j : 128 * j + 128] = totals[4 * k + j]
    for j in range(4):
        bg_ref[0:1, 128 * j : 128 * j + 128] = totals[16 + j]
    small_ref[...] = totals[20]
    all_of(totals, 2).wait_send()


def run_main(raw, weight, bias, dt_t, dt_bias, a_log, d_skip, cot):
    vmem = pl.BlockSpec(memory_space=pltpu.VMEM)
    hbm = pl.BlockSpec(memory_space=pltpu.HBM)
    return pl.pallas_call(
        main_kernel,
        out_shape=(
            jax.ShapeDtypeStruct((L, CH), BF16),
            jax.ShapeDtypeStruct((H, L), F32),
            jax.ShapeDtypeStruct((K, CH), F32),
            jax.ShapeDtypeStruct((1, CH), F32),
            jax.ShapeDtypeStruct((1, 128), F32),
        ),
        in_specs=[hbm] * 8,
        out_specs=(vmem,) * 5,
        scratch_shapes=[
            pltpu.SMEM((H,), F32),
            pltpu.SMEM((H,), F32),
            pltpu.SMEM((H,), F32),
            pltpu.VMEM((L, CH), BF16),
            pltpu.VMEM((K, CH), F32),
            pltpu.VMEM((1, CH), F32),
            pltpu.VMEM((H, L), F32),
            pltpu.VMEM((L, INNER), BF16),
            pltpu.SemaphoreType.DMA((8,)),
            pltpu.VMEM((8 + L, CH), F32),
            pltpu.VMEM((L, CH), F32),
            pltpu.VMEM((L, CH), F32),
            pltpu.VMEM((L, CH), BF16),
            pltpu.VMEM((128, L), F32),
            pltpu.VMEM((L, 128), F32),
            pltpu.VMEM((NO, 2 * RC, INNER), F32),
            pltpu.VMEM((1, 1, INNER), F32),
            pltpu.VMEM((L, INNER), F32),
            pltpu.VMEM((L, INNER), F32),
            pltpu.VMEM((L, INNER), F32),
            pltpu.VMEM((L, INNER), F32),
            pltpu.VMEM((L, N), F32),
            pltpu.VMEM((L, N), F32),
            pltpu.VMEM((8, L), F32),
            pltpu.VMEM((16 + L, CH), F32),
            pltpu.VMEM((NO, 2 * RC, INNER), F32),
            pltpu.VMEM((NO, 1, INNER), F32),
            pltpu.VMEM((NO, RC, INNER), F32),
            pltpu.VMEM((NO, RC, INNER), F32),
            pltpu.VMEM((2, NX, RC, INNER), F32),
            pltpu.VMEM((NX, 1, INNER), F32),
            pltpu.VMEM((2, NX, 2 * RC, INNER), F32),
            pltpu.VMEM((2, NX, 2 * RC, INNER), F32),
            pltpu.VMEM((2, 8, INNER), F32),
            pltpu.VMEM((2, 8, INNER), F32),
            pltpu.VMEM((NX, 8, CH + 2 * INNER), F32),
            pltpu.VMEM((NX, 16, CH), F32),
            pltpu.VMEM((N, INNER), F32),
            pltpu.VMEM((2, NX, RC, INNER), F32),
            pltpu.VMEM((NO, 2 * RC, INNER), F32),
            pltpu.VMEM((NO, 2 * RC, INNER), F32),
            pltpu.VMEM((8, CH), F32),
            pltpu.VMEM((8, CH), F32),
            pltpu.VMEM((8, CH), F32),
            pltpu.VMEM((8, CH), F32),
            pltpu.VMEM((NR, 1, 128), F32),
            pltpu.VMEM((NR, 1, 128), F32),
            pltpu.VMEM((ZR, 1, 128), F32),
            pltpu.VMEM((2, 1, 128), F32),
            pltpu.VMEM((NR, 1, 128), F32),
            pltpu.SemaphoreType.DMA((2, NX)),
            pltpu.SemaphoreType.DMA((2, NX)),
            pltpu.SemaphoreType.DMA((2,)),
            pltpu.SemaphoreType.DMA((2,)),
            pltpu.SemaphoreType.DMA((3,)),
            pltpu.SemaphoreType.DMA((3,)),
            pltpu.SemaphoreType.DMA((2, NX)),
            pltpu.SemaphoreType.DMA((2, NX)),
            pltpu.SemaphoreType.DMA((NO,)),
            pltpu.SemaphoreType.DMA((1,)),
            pltpu.SemaphoreType.DMA((1,)),
            pltpu.SemaphoreType.DMA((1,)),
            pltpu.SemaphoreType.DMA((1,)),
            pltpu.SemaphoreType.DMA((3,)),
            pltpu.SemaphoreType.DMA((3,)),
            pltpu.SemaphoreType.REGULAR,
            pltpu.SemaphoreType.REGULAR,
        ],
        compiler_params=pltpu.CompilerParams(
            collective_id=0, has_side_effects=True, vmem_limit_bytes=67043328
        ),
        name="slab",
    )(dt_bias, a_log, d_skip, raw, weight, bias, dt_t, cot)


def finish_kernel(gx, gpre, wg, bg, small, gx_o, gpre_o, wg_o, bg_o, db_o, da_o, ds_o):
    gx_o[...] = gx[...]
    gpre_o[...] = gpre[...]
    wg_o[...] = wg[...]
    bg_o[...] = bg[...]
    db_o[...] = small[0:1, 0:4]
    da_o[...] = small[0:1, 8:12]
    ds_o[...] = small[0:1, 16:20]


def finish(*parts):
    vmem = pl.BlockSpec(memory_space=pltpu.VMEM)
    head = jax.ShapeDtypeStruct((1, H), F32)
    return pl.pallas_call(
        finish_kernel,
        out_shape=tuple(jax.ShapeDtypeStruct(p.shape, p.dtype) for p in parts[:4]) + (head,) * 3,
        in_specs=[vmem] * 5,
        out_specs=(vmem,) * 7,
        compiler_params=pltpu.CompilerParams(vmem_limit_bytes=67043328),
        name="finish",
    )(*parts)


def on_device(xbc_raw, conv_weight, conv_bias, dt_raw, dt_bias, a_log, d_skip, grad_out):
    gx, gpre, weight_grad, bias_grad, bias, decay, skip = finish(*run_main(
        xbc_raw[0], conv_weight, conv_bias[None], dt_raw[0].T, dt_bias, a_log, d_skip, grad_out[0]
    ))
    return (
        gx[None], gpre.T[None], weight_grad, bias_grad[0], bias[0], decay[0], skip[0],
    )


def solution(mesh):
    rows = P("dp", "ctx", None)
    return jax.shard_map(
        on_device,
        mesh=mesh,
        in_specs=(rows, P(), P(), rows, P(), P(), P(), rows),
        out_specs=(rows, rows, P(), P(), P(), P(), P()),
        check_vma=False,
    )
```
